32 devices in a mesh: win: 2 (over x), fib: 16 (over z, y, core).
Axes of the slice: x: 2, y: 2, z: 4, core: 2. Of those that a mesh axis runs over, the one named last changes fastest.
Arguments:
- strain: bfloat16 [8192, 4096], P(('win', 'fib')), parts along dimension 0, may hold values from -6 to 6
- steering: bfloat16 [9, 128, 256], replicated, may hold values from -0.375 to 0.375
- lag_range: bfloat16 [9, 512, 384], replicated, may hold values from -0.25 to 0.25
- pair_listed: int32 [32, 8], P(('win', 'fib')), parts along dimension 0, may hold values 0 or 1
- band_used: int32 [32, 8, 4], P(('win', 'fib')), parts along dimension 0, may hold values 0 or 1
Outputs:
- image: float32 [128, 4096], P(None, ('win', 'fib')), parts along dimension 1
The draws below stay inside these ranges and needn't reach their ends.
There are 2 independent parts, one for each index of `win`. The reference program is written for one: setup_inputs(seed, part) draws one part's arguments, and reference() takes and returns one part's arrays. A program takes and returns all parts, laid end to end along the dimension named above; an argument that names none is the same for every part. Nothing has to cross between parts.
All inputs are finite; a program needn't handle non-finite values. No bound on the sum of `pair_listed` or of `band_used` on one device may be relied on, other than what follows from the above.
Results may differ from the reference program's by a relative error of at most 0.012.
Values may be sent and summed in bfloat16 or wider, within the bound.
No kernel may reach another device: no remote copies, remote signals or barrier semaphores. Data moves between devices by JAX's collectives and lax.ppermute only.
A program may use at most 64 MiB of HBM per device.

```python
import math
import jax
import jax.numpy as jnp

C = 256
NT = 4096
F = 512
L = 512
LB = 128
A = 128
GR = 128
ROUNDS = 8
NBAND = 4
CHANNELS = 4096
N_FIB = 16


def set_ends(result, key, least, largest):
    place = [jax.random.randint(jax.random.fold_in(key, axis), (), 0, length) for axis, length in enumerate(result.shape)]
    widest = result.shape.index(max(result.shape))
    neighbour = place[:widest] + [(place[widest] + 1) % result.shape[widest]] + place[widest + 1:]
    return result.at[tuple(place)].set(least).at[tuple(neighbour)].set(largest)


def block_scale(key, dims, pieces, smallest, top_value):
    def one(axis_at, blocks):
        steps = jax.random.uniform(jax.random.fold_in(jax.random.fold_in(key, 6), axis_at), (blocks,), jnp.float32, smallest / len(pieces), top_value / len(pieces))
        return jnp.repeat(jnp.exp(steps), dims[axis_at] // blocks).reshape((-1,) + (1,) * (len(dims) - axis_at - 1))

    factor_of = one(*pieces[0])
    for cut in pieces[1:]:
        factor_of = factor_of * one(*cut)
    return factor_of


def normal_values(rng, extent, scale, bound, cuts=(), kind=jnp.bfloat16):
    factor_of = block_scale(rng, extent, cuts, -0.22, 0.18) if cuts else 1.0
    result = jax.random.normal(rng, extent, jnp.float32) * scale * factor_of
    return jnp.minimum(jnp.maximum(result, -bound), bound).astype(kind)


def setup_inputs(seed: int = 0, part: int = 0) -> dict:
    key_list = jax.random.split(jax.random.key(seed), 6)
    part_keys = jax.random.split(jax.random.fold_in(key_list[5], part), 6)
    return {
        "strain": normal_values(part_keys[0], (CHANNELS, NT), 1.0, 6.0, ((0, 16),)),
        "steering": normal_values(key_list[1], (ROUNDS + 1, A, C), C ** -0.5, 0.375),
        "lag_range": normal_values(key_list[2], (ROUNDS + 1, L, 3 * GR), L ** -0.5, 0.25),
        "pair_listed": set_ends((jax.random.randint(part_keys[3], (N_FIB, ROUNDS), 0, 4) < 3).astype(jnp.int32), jax.random.fold_in(part_keys[3], 1), 0, 1),
        "band_used": set_ends((jax.random.randint(part_keys[4], (N_FIB, ROUNDS, NBAND), 0, 2) < 1).astype(jnp.int32), jax.random.fold_in(part_keys[4], 1), 0, 1),
    }


def make_tables(samples):
    steps_t = jnp.arange(samples, dtype=jnp.int32)[:, None]
    freq = jnp.arange(1, F + 1, dtype=jnp.int32)[None, :]
    phase = ((steps_t * freq) % samples).astype(jnp.float32) * (2.0 * math.pi / samples)
    forward = (jnp.concatenate([jnp.cos(phase), -jnp.sin(phase)], axis=1) * (samples ** -0.5)).astype(jnp.bfloat16)
    lag_index = (jnp.arange(L, dtype=jnp.int32) - L // 2)[None, :]
    theta = ((freq.reshape(F, 1) * lag_index) % samples).astype(jnp.float32) * (2.0 * math.pi / samples)
    inverse = (jnp.concatenate([jnp.cos(theta), -jnp.sin(theta)], axis=0) * ((2 * F) ** -0.5)).astype(jnp.bfloat16)
    return forward, inverse


def reference(strain, steering, lag_range, pair_listed, band_used):
    blocks = N_FIB
    forward, inverse = make_tables(NT)
    spectrum = jnp.dot(strain, forward, preferred_element_type=jnp.float32).astype(jnp.bfloat16)
    spec_float = spectrum.astype(jnp.float32).reshape(blocks, C, 2 * F)
    real_own = spec_float[..., :F]
    imag_own = spec_float[..., F:]
    nbands = L // LB
    windows = jnp.zeros((blocks, A, 3 * GR), jnp.float32)
    for dist in range(0, ROUNDS + 1):
        if dist == 0:
            real_far = real_own
            imag_far = imag_own
            weight = jnp.ones((blocks, nbands), jnp.float32)
        else:
            filler = jnp.zeros((dist, C, F), jnp.float32)
            real_far = jnp.concatenate([filler, real_own[:-dist]], axis=0)
            imag_far = jnp.concatenate([filler, imag_own[:-dist]], axis=0)
            weight = (pair_listed[:, dist - 1][:, None] * band_used[:, dist - 1, :]).astype(jnp.float32)
        real_part = real_own * real_far + imag_own * imag_far
        imag_part = imag_own * real_far - real_own * imag_far
        cross = jnp.concatenate([real_part, imag_part], axis=2).astype(jnp.bfloat16)
        lags = jnp.dot(cross.reshape(blocks * C, 2 * F), inverse, preferred_element_type=jnp.float32)
        lags = lags.reshape(blocks, C, nbands, LB)
        lags = (lags * weight[:, None, :, None]).reshape(blocks, C, L).astype(jnp.bfloat16)
        beams = jnp.einsum("ac,bcl->bal", steering[dist].astype(jnp.float32), lags.astype(jnp.float32)).astype(jnp.bfloat16)
        windows = windows + jnp.einsum("bal,lg->bag", beams.astype(jnp.float32), lag_range[dist].astype(jnp.float32))
    parts = windows.reshape(blocks, A, 3, GR)
    middle = parts[:, :, 1, :]
    zero_row = jnp.zeros((1, A, GR), jnp.float32)
    from_below = jnp.concatenate([zero_row, parts[:-1, :, 2, :]], axis=0)
    from_above = jnp.concatenate([parts[1:, :, 0, :], zero_row], axis=0)
    total = middle + from_below + from_above
    return jnp.transpose(total, (1, 0, 2)).reshape(A, blocks * GR)
```

```python
import functools

import jax
import jax.numpy as jnp
import numpy as np
from jax import lax
from jax.experimental import pallas as pl
from jax.experimental.pallas import tpu as pltpu
from jax.sharding import PartitionSpec as P

AXIS = "fib"
F = 512
L = 512
Q = 4


def forward_table(samples):
    freqs = F // Q
    t = np.arange(samples // Q, dtype=np.int64)[None, :, None]
    k = Q * np.arange(freqs, dtype=np.int64)[None, None, :] + np.arange(Q)[:, None, None] + 1
    phase = (t * k % samples) * (2.0 * np.pi / samples)
    table = np.concatenate([np.cos(phase), -np.sin(phase)], axis=2) * samples ** (-0.5)
    return table.astype(jnp.bfloat16)


def inverse_table(samples):
    freqs = F // Q
    k = Q * np.arange(freqs, dtype=np.int64)[None, :, None] + np.arange(Q)[:, None, None] + 1
    lag = np.arange(L, dtype=np.int64)[None, None, :] - L // 2
    theta = (k * lag % samples) * (2.0 * np.pi / samples)
    table = np.concatenate([np.cos(theta), -np.sin(theta)], axis=1) * (2 * F) ** (-0.5)
    return table.astype(jnp.bfloat16)


def dot(a, b):
    return jnp.dot(a, b, preferred_element_type=jnp.float32)


def spectrum_kernel(listed, bands, x0, x1, x2, x3, table, *refs):
    outs, acc = refs[:Q], refs[Q]
    step, steps = pl.program_id(0), pl.num_programs(0)
    half = table.shape[2] // 2
    channels = x0.shape[0]
    me = lax.rem(lax.axis_index(AXIS), Q)

    q0, q1, q2, q3 = (x[...].astype(jnp.float32) for x in (x0, x1, x2, x3))
    even, odd = q0 + q2, q1 + q3
    fold0 = (even + odd).astype(jnp.bfloat16)
    fold2 = (even - odd).astype(jnp.bfloat16)
    a = (q0 - q2).astype(jnp.bfloat16)
    b = (q1 - q3).astype(jnp.bfloat16)
    parts = [
        dot(a, table[0]),
        dot(b, table[0]),
        dot(fold2, table[1]),
        dot(a, table[2]),
        dot(b, table[2]),
        dot(fold0, table[3]),
    ]

    @pl.when(step == 0)
    def _():
        for n, part in enumerate(parts):
            acc[n] = part

    @pl.when((step > 0) & (step < steps - 1))
    def _():
        for n, part in enumerate(parts):
            acc[n] += part

    @pl.when(step == steps - 1)
    def _():
        p1, b1, s2, p3, b3, s0 = (acc[n] + part for n, part in enumerate(parts))
        s1 = jnp.concatenate([p1[:, :half] + b1[:, half:], p1[:, half:] - b1[:, :half]], axis=1)
        s3 = jnp.concatenate([p3[:, :half] - b3[:, half:], p3[:, half:] + b3[:, :half]], axis=1)
        for s, value in enumerate((s1, s2, s3, s0)):
            value = value.astype(jnp.bfloat16)
            for p in range(Q):

                @pl.when(lax.bitwise_xor(me, s) == p)
                def _():
                    outs[p][:channels, :] = value

        rows, cols = outs[0].shape[0] - channels, outs[0].shape[1]
        rounds, nbands = bands.shape[1], bands.shape[2]
        place = (
            lax.broadcasted_iota(jnp.int32, (rows, cols), 0) * cols
            + lax.broadcasted_iota(jnp.int32, (rows, cols), 1)
        ) // (L // nbands)
        weight = jnp.zeros((rows, cols), jnp.float32)
        for d in range(rounds):
            for j in range(nbands):
                value = (listed[0, d] * bands[0, d, j]).astype(jnp.float32)
                weight = jnp.where(place == d * nbands + j, value, weight)
        weight = weight.astype(jnp.bfloat16)
        for p in range(Q):
            outs[p][channels:, :] = weight


def spectrum_call(strain, listed, bands, steps=2):
    channels, samples = strain.shape
    table = forward_table(samples)
    cols = table.shape[2]
    depth = samples // Q // steps
    rows = channels + bands.shape[1] * L // cols
    quarter = [
        pl.BlockSpec((channels, depth), lambda k, q=q: (0, q * steps + k)) for q in range(Q)
    ]
    return pl.pallas_call(
        spectrum_kernel,
        grid=(steps,),
        in_specs=[
            pl.BlockSpec(memory_space=pltpu.SMEM),
            pl.BlockSpec(memory_space=pltpu.SMEM),
            *quarter,
            pl.BlockSpec((Q, depth, cols), lambda k: (0, k, 0)),
        ],
        out_specs=[pl.BlockSpec((rows, cols), lambda k: (0, 0))] * Q,
        out_shape=[jax.ShapeDtypeStruct((rows, cols), jnp.bfloat16)] * Q,
        scratch_shapes=[pltpu.VMEM((6, channels, cols), jnp.float32)],
        compiler_params=pltpu.CompilerParams(dimension_semantics=("arbitrary",)),
        name="spectrum",
    )(listed, bands, strain, strain, strain, strain, jnp.asarray(table))


def pair_kernel(*refs):
    spec_in = refs[: 3 * Q]
    inv_in, steering, lag_range = refs[3 * Q : 3 * Q + 3]
    own, *outs = refs[3 * Q + 3 : 3 * Q + 3 + Q]
    spec, inv, grouped, window, segs, sems, inv_sem = refs[3 * Q + 3 + Q :]
    me = lax.rem(lax.axis_index(AXIS), Q)
    copies = []
    for plane in range(3):
        for p in range(Q):
            copies.append(
                pltpu.make_async_copy(
                    spec_in[plane * Q + p],
                    spec.at[plane * Q + lax.bitwise_xor(me, p)],
                    sems.at[plane * Q + p],
                )
            )
    inv_copy = pltpu.make_async_copy(inv_in.at[me], inv, inv_sem)
    for copy in copies:
        copy.start()
    inv_copy.start()
    for copy in copies:
        copy.wait()
    inv_copy.wait()

    rounds = steering.shape[0] - 1
    angles, channels = steering.shape[1], steering.shape[2]
    cols = spec.shape[2]
    half = cols // 2
    per = L // cols
    first = {}
    for d in range(rounds + 1):
        units = []
        for i in range(2 * Q):
            j = i - d
            if i < Q and -Q <= j:
                units.append((i, i, j if j >= 0 else 2 * Q + j))
            elif i >= Q and -Q <= j < 0:
                units.append((i, Q + i, 2 * Q + j))
        for n, (_, target, source) in enumerate(units):
            near_re = spec[target, :channels, :half].astype(jnp.float32)
            near_im = spec[target, :channels, half:].astype(jnp.float32)
            far_re = spec[source, :channels, :half].astype(jnp.float32)
            far_im = spec[source, :channels, half:].astype(jnp.float32)
            real = near_re * far_re + near_im * far_im
            imag = near_im * far_re - near_re * far_im
            cross = jnp.concatenate([real, imag], axis=1).astype(jnp.bfloat16)
            grouped[n * angles : (n + 1) * angles, :] = dot(steering[d], cross).astype(
                jnp.bfloat16
            )
        count = len(units)
        beams = dot(grouped[: count * angles, :], inv[...])
        if d > 0:
            masked = []
            for n, (_, target, _) in enumerate(units):
                row = channels + (d - 1) * per
                weight = jnp.concatenate(
                    [spec[target, row + h : row + h + 1, :] for h in range(per)], axis=1
                ).astype(jnp.float32)
                masked.append(beams[n * angles : (n + 1) * angles, :] * weight)
            beams = jnp.concatenate(masked, axis=0)
        part = dot(beams.astype(jnp.bfloat16), lag_range[d])
        for n, (slot, _, _) in enumerate(units):
            value = part[n * angles : (n + 1) * angles, :]
            if slot in first:
                window[slot] += value
            else:
                window[slot] = value
                first[slot] = True

    width = window.shape[2] // 3

    def third(slot, part):
        return window[slot, :, part * width : (part + 1) * width]

    def segment(s):
        total = None
        for slot, part in ((s, 1), (s - 1, 2), (s + 1, 0)):
            if 0 <= slot < 2 * Q:
                value = third(slot, part)
                total = value if total is None else total + value
        return total

    for p in range(Q):
        segs[p, 0] = segment(p)
        segs[p, 1] = segment(Q + p)
        if p == 0:
            segs[p, 2] = segment(2 * Q)
        elif p == Q - 1:
            segs[p, 2] = segment(-1)
        else:
            segs[p, 2] = jnp.zeros((angles, width), jnp.float32)
    own[...] = segs[me]
    for p in range(1, Q):
        outs[p - 1][...] = segs[lax.bitwise_xor(me, p)].astype(jnp.bfloat16)


def pair_call(spectra, samples, steering, lag_range):
    rows, cols = spectra[0].shape
    angles = steering.shape[1]
    width = lag_range.shape[2] // 3
    inv = inverse_table(samples)
    hbm = pl.BlockSpec(memory_space=pl.ANY)
    vmem = pl.BlockSpec(memory_space=pltpu.VMEM)
    return pl.pallas_call(
        pair_kernel,
        in_specs=[hbm] * (3 * Q + 1) + [vmem, vmem],
        out_specs=[vmem] * Q,
        out_shape=[jax.ShapeDtypeStruct((3, angles, width), jnp.float32)]
        + [jax.ShapeDtypeStruct((3, angles, width), jnp.bfloat16)] * (Q - 1),
        scratch_shapes=[
            pltpu.VMEM((3 * Q, rows, cols), jnp.bfloat16),
            pltpu.VMEM((cols, L), jnp.bfloat16),
            pltpu.VMEM((Q * angles, cols), jnp.bfloat16),
            pltpu.VMEM((2 * Q, angles, 3 * width), jnp.float32),
            pltpu.VMEM((Q, 3, angles, width), jnp.float32),
            pltpu.SemaphoreType.DMA((3 * Q,)),
            pltpu.SemaphoreType.DMA(()),
        ],
        name="pairs",
    )(*spectra, jnp.asarray(inv), steering, lag_range)


def exchange(value, devices, target):
    pairs = [(i, target(i)) for i in range(devices) if target(i) is not None]
    pairs = [(i, j) for i, j in pairs if 0 <= j < devices]
    return lax.ppermute(value, AXIS, pairs)


def per_device(devices, strain, steering, lag_range, pair_listed, band_used):
    slices = spectrum_call(strain, pair_listed, band_used)
    own = [slices[0]] + [
        exchange(slices[p], devices, lambda i: i ^ p) for p in range(1, Q)
    ]
    below = [exchange(slices[p], devices, lambda i: (i ^ p) + Q) for p in range(Q)]
    above = [exchange(slices[p], devices, lambda i: (i ^ p) - Q) for p in range(Q)]
    mine, *sends = pair_call(own + below + above, strain.shape[1], steering, lag_range)
    for p in range(1, Q):
        mine = mine + exchange(sends[p - 1], devices, lambda i: i ^ p).astype(jnp.float32)
    up = exchange(mine[1].astype(jnp.bfloat16), devices, lambda i: i + Q)

    def ends(i):
        if i % Q == 0:
            return i + 2 * Q
        if i % Q == Q - 1:
            return i - Q
        return None

    extra = exchange(mine[2].astype(jnp.bfloat16), devices, ends)
    return mine[0] + up.astype(jnp.float32) + extra.astype(jnp.float32)


def solution(mesh):
    return jax.shard_map(
        functools.partial(per_device, mesh.shape[AXIS]),
        mesh=mesh,
        in_specs=(
            P(("win", AXIS), None),
            P(),
            P(),
            P(("win", AXIS), None),
            P(("win", AXIS), None, None),
        ),
        out_specs=P(None, ("win", AXIS)),
        check_vma=False,
    )
```

```python
import functools

import jax
import jax.numpy as jnp
import numpy as np
from jax import lax
from jax.experimental import pallas as pl
from jax.experimental.pallas import tpu as pltpu
from jax.sharding import PartitionSpec as P

AXIS = "fib"
F = 512
L = 512
Q = 4


def forward_table(samples):
    freqs = F // Q
    t = np.arange(samples // Q, dtype=np.int64)[None, :, None]
    k = Q * np.arange(freqs, dtype=np.int64)[None, None, :] + np.arange(Q)[:, None, None] + 1
    phase = (t * k % samples) * (2.0 * np.pi / samples)
    table = np.concatenate([np.cos(phase), -np.sin(phase)], axis=2) * samples ** (-0.5)
    return table.astype(jnp.bfloat16)


def inverse_table(samples):
    freqs = F // Q
    k = Q * np.arange(freqs, dtype=np.int64)[None, :, None] + np.arange(Q)[:, None, None] + 1
    lag = np.arange(L, dtype=np.int64)[None, None, :] - L // 2
    theta = (k * lag % samples) * (2.0 * np.pi / samples)
    table = np.concatenate([np.cos(theta), -np.sin(theta)], axis=1) * (2 * F) ** (-0.5)
    return table.astype(jnp.bfloat16)


def dot(a, b):
    return jnp.dot(a, b, preferred_element_type=jnp.float32)


def spectrum_kernel(listed, bands, x0, x1, x2, x3, table, keep, mate, swap, acc, weight):
    step, steps = pl.program_id(0), pl.num_programs(0)
    half = table.shape[2] // 2
    channels = x0.shape[0]
    me = lax.rem(lax.axis_index(AXIS), Q)

    q0, q1, q2, q3 = (x[...].astype(jnp.float32) for x in (x0, x1, x2, x3))
    even, odd = q0 + q2, q1 + q3
    fold0 = (even + odd).astype(jnp.bfloat16)
    fold2 = (even - odd).astype(jnp.bfloat16)
    a = (q0 - q2).astype(jnp.bfloat16)
    b = (q1 - q3).astype(jnp.bfloat16)
    parts = [
        dot(a, table[0]),
        dot(b, table[0]),
        dot(fold2, table[1]),
        dot(a, table[2]),
        dot(b, table[2]),
        dot(fold0, table[3]),
    ]

    @pl.when(step == 0)
    def _():
        for n, part in enumerate(parts):
            acc[n] = part

    @pl.when((step > 0) & (step < steps - 1))
    def _():
        for n, part in enumerate(parts):
            acc[n] += part

    @pl.when(step == steps - 1)
    def _():
        p1, b1, s2, p3, b3, s0 = (acc[n] + part for n, part in enumerate(parts))
        s1 = jnp.concatenate([p1[:, :half] + b1[:, half:], p1[:, half:] - b1[:, :half]], axis=1)
        s3 = jnp.concatenate([p3[:, :half] - b3[:, half:], p3[:, half:] + b3[:, :half]], axis=1)
        outs = (keep, swap.at[0], mate, swap.at[1])
        for s, value in enumerate((s1, s2, s3, s0)):
            value = value.astype(jnp.bfloat16)
            for p, out in enumerate(outs):

                @pl.when(lax.bitwise_xor(me, s) == p)
                def _():
                    out[:channels, :] = value

        cols = keep.shape[1]
        rounds, nbands = bands.shape[1], bands.shape[2]
        width = L // nbands
        square = (rounds, rounds)
        diagonal = lax.broadcasted_iota(jnp.int32, square, 0) == lax.broadcasted_iota(
            jnp.int32, square, 1
        )
        column = jnp.sum(
            jnp.where(diagonal, jnp.broadcast_to(listed[...], square), 0).astype(jnp.float32),
            axis=1,
            keepdims=True,
        )
        used = column * bands[0].astype(jnp.float32)
        for d in range(rounds):
            for j in range(nbands):
                row, lane = divmod((d * nbands + j) * width, cols)
                weight[row : row + 1, lane : lane + width] = jnp.broadcast_to(
                    used[d : d + 1, j : j + 1], (1, width)
                )
        for out in outs:
            out[channels:, :] = weight[...].astype(jnp.bfloat16)


def spectrum_call(strain, listed, bands, steps=2):
    channels, samples = strain.shape
    table = forward_table(samples)
    cols = table.shape[2]
    depth = samples // Q // steps
    rows = channels + bands.shape[1] * L // cols
    quarter = [
        pl.BlockSpec((channels, depth), lambda k, q=q: (0, q * steps + k)) for q in range(Q)
    ]
    return pl.pallas_call(
        spectrum_kernel,
        grid=(steps,),
        in_specs=[
            pl.BlockSpec(listed.shape, lambda k: (0, 0)),
            pl.BlockSpec(bands.shape, lambda k: (0, 0, 0)),
            *quarter,
            pl.BlockSpec((Q, depth, cols), lambda k: (0, k, 0)),
        ],
        out_specs=[
            pl.BlockSpec((rows, cols), lambda k: (0, 0)),
            pl.BlockSpec((rows, cols), lambda k: (0, 0)),
            pl.BlockSpec((2, rows, cols), lambda k: (0, 0, 0)),
        ],
        out_shape=[
            jax.ShapeDtypeStruct((rows, cols), jnp.bfloat16),
            jax.ShapeDtypeStruct((rows, cols), jnp.bfloat16),
            jax.ShapeDtypeStruct((2, rows, cols), jnp.bfloat16),
        ],
        scratch_shapes=[
            pltpu.VMEM((6, channels, cols), jnp.float32),
            pltpu.VMEM((rows - channels, cols), jnp.float32),
        ],
        compiler_params=pltpu.CompilerParams(dimension_semantics=("arbitrary",)),
        name="spectrum",
    )(listed, bands, strain, strain, strain, strain, jnp.asarray(table))


def pair_kernel(keep, swap, mate, near_b, far_b, near_a, far_a, inv_in, steering, lag_range, *refs):
    own, send, spec, inv, grouped, window, segs, sems, inv_sem = refs
    me = lax.rem(lax.axis_index(AXIS), Q)
    sources = [
        keep, swap.at[0], mate.at[0], mate.at[1],
        near_b.at[0], near_b.at[1], far_b.at[0], far_b.at[1],
        near_a.at[0], near_a.at[1], far_a.at[0], far_a.at[1],
    ]
    copies = []
    for n, source in enumerate(sources):
        slot = n // Q * Q + lax.bitwise_xor(me, n % Q)
        copies.append(pltpu.make_async_copy(source, spec.at[slot], sems.at[n]))
    inv_copy = pltpu.make_async_copy(inv_in.at[me], inv, inv_sem)
    for copy in copies:
        copy.start()
    inv_copy.start()
    for copy in copies:
        copy.wait()
    inv_copy.wait()

    rounds = steering.shape[0] - 1
    angles, channels = steering.shape[1], steering.shape[2]
    cols = spec.shape[2]
    half = cols // 2
    per = L // cols
    first = {}
    for d in range(rounds + 1):
        units = []
        for i in range(2 * Q):
            j = i - d
            if i < Q and -Q <= j:
                units.append((i, i, j if j >= 0 else 2 * Q + j))
            elif i >= Q and -Q <= j < 0:
                units.append((i, Q + i, 2 * Q + j))
        for n, (_, target, source) in enumerate(units):
            near_re = spec[target, :channels, :half].astype(jnp.float32)
            near_im = spec[target, :channels, half:].astype(jnp.float32)
            far_re = spec[source, :channels, :half].astype(jnp.float32)
            far_im = spec[source, :channels, half:].astype(jnp.float32)
            real = near_re * far_re + near_im * far_im
            imag = near_im * far_re - near_re * far_im
            cross = jnp.concatenate([real, imag], axis=1).astype(jnp.bfloat16)
            grouped[n * angles : (n + 1) * angles, :] = dot(steering[d], cross).astype(
                jnp.bfloat16
            )
        count = len(units)
        beams = dot(grouped[: count * angles, :], inv[...])
        if d > 0:
            masked = []
            for n, (_, target, _) in enumerate(units):
                row = channels + (d - 1) * per
                weight = jnp.concatenate(
                    [spec[target, row + h : row + h + 1, :] for h in range(per)], axis=1
                ).astype(jnp.float32)
                masked.append(beams[n * angles : (n + 1) * angles, :] * weight)
            beams = jnp.concatenate(masked, axis=0)
        part = dot(beams.astype(jnp.bfloat16), lag_range[d])
        for n, (slot, _, _) in enumerate(units):
            value = part[n * angles : (n + 1) * angles, :]
            if slot in first:
                window[slot] += value
            else:
                window[slot] = value
                first[slot] = True

    width = window.shape[2] // 3

    def third(slot, part):
        return window[slot, :, part * width : (part + 1) * width]

    def segment(s):
        total = None
        for slot, part in ((s, 1), (s - 1, 2), (s + 1, 0)):
            if 0 <= slot < 2 * Q:
                value = third(slot, part)
                total = value if total is None else total + value
        return total

    for p in range(Q):
        segs[p, 0] = segment(p)
        segs[p, 1] = segment(Q + p)
        if p == 0:
            segs[p, 2] = segment(2 * Q)
        elif p == Q - 1:
            segs[p, 2] = segment(-1)
        else:
            segs[p, 2] = jnp.zeros((angles, width), jnp.float32)
    own[0] = segs[me]
    own[1] = segs[lax.bitwise_xor(me, 2)]
    send[0] = segs[lax.bitwise_xor(me, 1)].astype(jnp.bfloat16)
    send[1] = segs[lax.bitwise_xor(me, 3)].astype(jnp.bfloat16)


def pair_call(spectra, samples, steering, lag_range):
    rows, cols = spectra[0].shape
    angles = steering.shape[1]
    width = lag_range.shape[2] // 3
    inv = inverse_table(samples)
    hbm = pl.BlockSpec(memory_space=pl.ANY)
    vmem = pl.BlockSpec(memory_space=pltpu.VMEM)
    return pl.pallas_call(
        pair_kernel,
        in_specs=[vmem] * len(spectra) + [hbm, vmem, vmem],
        out_specs=[vmem, vmem],
        out_shape=[
            jax.ShapeDtypeStruct((2, 3, angles, width), jnp.float32),
            jax.ShapeDtypeStruct((2, 3, angles, width), jnp.bfloat16),
        ],
        scratch_shapes=[
            pltpu.VMEM((3 * Q, rows, cols), jnp.bfloat16),
            pltpu.VMEM((cols, L), jnp.bfloat16),
            pltpu.VMEM((Q * angles, cols), jnp.bfloat16),
            pltpu.VMEM((2 * Q, angles, 3 * width), jnp.float32),
            pltpu.VMEM((Q, 3, angles, width), jnp.float32),
            pltpu.SemaphoreType.DMA((3 * Q,)),
            pltpu.SemaphoreType.DMA(()),
        ],
        name="pairs",
    )(*spectra, jnp.asarray(inv), steering, lag_range)


def exchange(value, devices, target):
    pairs = [(i, target(i)) for i in range(devices) if target(i) is not None]
    pairs = [(i, j) for i, j in pairs if 0 <= j < devices]
    return lax.ppermute(value, AXIS, pairs)


def per_device(devices, strain, steering, lag_range, pair_listed, band_used):
    def shift(value, by):
        return exchange(value, devices, lambda i: i + by)

    def flip(value, by):
        return exchange(value, devices, lambda i: i ^ by)

    keep, mate, swap = spectrum_call(strain, pair_listed, band_used)
    swap = flip(swap, 1)
    mates = flip(jnp.stack([mate, swap[1]]), 2)
    near = jnp.stack([keep, swap[0]])
    spectra = [keep, swap, mates]
    for by in (Q, -Q):
        spectra += [shift(near, by), shift(mates, by)]
    mine, send = pair_call(spectra, strain.shape[1], steering, lag_range)
    mine = mine + flip(send, 1).astype(jnp.float32)
    mine = mine[0] + flip(mine[1].astype(jnp.bfloat16), 2).astype(jnp.float32)
    up = shift(mine[1].astype(jnp.bfloat16), Q)

    def ends(i):
        if i % Q == 0:
            return i + 2 * Q
        if i % Q == Q - 1:
            return i - Q
        return None

    extra = exchange(mine[2].astype(jnp.bfloat16), devices, ends)
    return mine[0] + up.astype(jnp.float32) + extra.astype(jnp.float32)


def solution(mesh):
    return jax.shard_map(
        functools.partial(per_device, mesh.shape[AXIS]),
        mesh=mesh,
        in_specs=(
            P(("win", AXIS), None),
            P(),
            P(),
            P(("win", AXIS), None),
            P(("win", AXIS), None, None),
        ),
        out_specs=P(None, ("win", AXIS)),
        check_vma=False,
    )
```

```python
import functools

import jax
import jax.numpy as jnp
import numpy as np
from jax import lax
from jax.experimental import pallas as pl
from jax.experimental.pallas import tpu as pltpu
from jax.sharding import PartitionSpec as P

AXIS = "fib"
F = 512
L = 512
Q = 4


def forward_table(samples):
    freqs = F // Q
    t = np.arange(samples // Q, dtype=np.int64)[None, :, None]
    k = Q * np.arange(freqs, dtype=np.int64)[None, None, :] + np.arange(Q)[:, None, None] + 1
    phase = (t * k % samples) * (2.0 * np.pi / samples)
    table = np.concatenate([np.cos(phase), -np.sin(phase)], axis=2) * samples ** (-0.5)
    return table.astype(jnp.bfloat16)


def inverse_table(samples):
    freqs = F // Q
    k = Q * np.arange(freqs, dtype=np.int64)[None, :, None] + np.arange(Q)[:, None, None] + 1
    lag = np.arange(L, dtype=np.int64)[None, None, :] - L // 2
    theta = (k * lag % samples) * (2.0 * np.pi / samples)
    table = np.concatenate([np.cos(theta), -np.sin(theta)], axis=1) * (2 * F) ** (-0.5)
    return table.astype(jnp.bfloat16)


def in_hbm(value):
    return pltpu.with_memory_space_constraint(value, pltpu.HBM)


def dot(a, b):
    return jnp.dot(a, b, preferred_element_type=jnp.float32)


def spectrum_kernel(listed, bands, x0, x1, x2, x3, table, keep, mate, swap, acc, weight):
    step, steps = pl.program_id(0), pl.num_programs(0)
    half = table.shape[2] // 2
    channels = x0.shape[0]
    me = lax.rem(lax.axis_index(AXIS), Q)

    q0, q1, q2, q3 = (x[...].astype(jnp.float32) for x in (x0, x1, x2, x3))
    even, odd = q0 + q2, q1 + q3
    fold0 = (even + odd).astype(jnp.bfloat16)
    fold2 = (even - odd).astype(jnp.bfloat16)
    a = (q0 - q2).astype(jnp.bfloat16)
    b = (q1 - q3).astype(jnp.bfloat16)
    parts = [
        dot(a, table[0]),
        dot(b, table[0]),
        dot(fold2, table[1]),
        dot(a, table[2]),
        dot(b, table[2]),
        dot(fold0, table[3]),
    ]

    @pl.when(step == 0)
    def _():
        for n, part in enumerate(parts):
            acc[n] = part

    @pl.when((step > 0) & (step < steps - 1))
    def _():
        for n, part in enumerate(parts):
            acc[n] += part

    @pl.when(step == steps - 1)
    def _():
        p1, b1, s2, p3, b3, s0 = (acc[n] + part for n, part in enumerate(parts))
        s1 = jnp.concatenate([p1[:, :half] + b1[:, half:], p1[:, half:] - b1[:, :half]], axis=1)
        s3 = jnp.concatenate([p3[:, :half] - b3[:, half:], p3[:, half:] + b3[:, :half]], axis=1)
        outs = (keep, swap.at[0], mate, swap.at[1])
        for s, value in enumerate((s1, s2, s3, s0)):
            value = value.astype(jnp.bfloat16)
            for p, out in enumerate(outs):

                @pl.when(lax.bitwise_xor(me, s) == p)
                def _():
                    out[:channels, :] = value

        cols = keep.shape[1]
        nbands, rounds = bands.shape[1], bands.shape[2]
        width = L // nbands
        used = (listed[...] * bands[0]).astype(jnp.float32)
        for j in range(nbands):
            part, lane = divmod(j * width, cols)
            for d in range(rounds):
                row = part * rounds + d
                weight[row : row + 1, lane : lane + width] = jnp.broadcast_to(
                    used[j : j + 1, d : d + 1], (1, width)
                )
        for out in outs:
            out[channels:, :] = weight[...].astype(jnp.bfloat16)


def spectrum_call(strain, listed, bands, steps=2):
    channels, samples = strain.shape
    table = forward_table(samples)
    cols = table.shape[2]
    depth = samples // Q // steps
    rows = channels + bands.shape[2] * L // cols
    quarter = [
        pl.BlockSpec((channels, depth), lambda k, q=q: (0, q * steps + k)) for q in range(Q)
    ]
    return pl.pallas_call(
        spectrum_kernel,
        grid=(steps,),
        in_specs=[
            pl.BlockSpec(listed.shape, lambda k: (0, 0)),
            pl.BlockSpec(bands.shape, lambda k: (0, 0, 0)),
            *quarter,
            pl.BlockSpec((Q, depth, cols), lambda k: (0, k, 0)),
        ],
        out_specs=[pl.BlockSpec(memory_space=pltpu.VMEM)] * 3,
        out_shape=[
            pltpu.VMEM((rows, cols), jnp.bfloat16),
            pltpu.VMEM((rows, cols), jnp.bfloat16),
            pltpu.VMEM((2, rows, cols), jnp.bfloat16),
        ],
        scratch_shapes=[
            pltpu.VMEM((6, channels, cols), jnp.float32),
            pltpu.VMEM((rows - channels, cols), jnp.float32),
        ],
        compiler_params=pltpu.CompilerParams(
            dimension_semantics=("arbitrary",), vmem_limit_bytes=LIMIT
        ),
        name="spectrum",
    )(listed, bands, *[in_hbm(strain)] * Q, in_hbm(jnp.asarray(table)))


UNROLL = 3
LIMIT = 16 << 20


def unit_table(rounds):
    early, late = [], []
    for me in range(Q):
        units = ([], [])
        for i in range(2 * Q):
            for j in range(-Q, Q):
                d = i - j
                if not 0 <= d <= rounds or (i >= Q and j >= 0):
                    continue
                p, q = i % Q ^ me, j % Q ^ me
                target = p if i < Q else 2 * Q + p
                source = q if j >= 0 else Q + q
                far = (i >= Q and p >= Q // 2) or (j < 0 and q >= Q // 2)
                mask = p if i < Q else Q + p
                row = d - 1 if d else rounds
                units[far].append((target, source, d, i, mask, row))
        early.append(units[0])
        late.append(units[1])
    return np.asarray(early, np.int32), np.asarray(late, np.int32)


def run_units(table, me, spec, mask, steering, inv, lag_range, window):
    channels, angles = steering.shape[2], steering.shape[1]
    cols = spec.shape[2]
    half = cols // 2

    def body(n, carry):
        units = [
            [table[me, (n * UNROLL + u) * 6 + e] for e in range(6)] for u in range(UNROLL)
        ]
        beams = []
        for target, source, d, _, _, _ in units:
            near_re = spec[target, :channels, :half].astype(jnp.float32)
            near_im = spec[target, :channels, half:].astype(jnp.float32)
            far_re = spec[source, :channels, :half].astype(jnp.float32)
            far_im = spec[source, :channels, half:].astype(jnp.float32)
            real = near_re * far_re + near_im * far_im
            imag = near_im * far_re - near_re * far_im
            cross = jnp.concatenate([real, imag], axis=1).astype(jnp.bfloat16)
            beams.append(dot(steering[d], cross).astype(jnp.bfloat16))
        beams = dot(jnp.concatenate(beams, axis=0), inv[...])
        for u, (_, _, d, slot, target, row) in enumerate(units):
            weight = jnp.concatenate(
                [mask[target, h, pl.ds(row, 1), :] for h in range(L // cols)], axis=1
            )
            masked = (beams[u * angles : (u + 1) * angles, :] * weight).astype(jnp.bfloat16)
            window[slot] += dot(masked, lag_range[d])
        return carry

    lax.fori_loop(0, table.shape[1] // (6 * UNROLL), body, 0)


def fill_mask(mask, entry, spec, slot, channels):
    rounds = mask.shape[2] // 2
    rows = spec[slot, channels:, :].astype(jnp.float32)
    for h in range(mask.shape[1]):
        mask[entry, h, :rounds, :] = rows[h * rounds : (h + 1) * rounds, :]
        mask[entry, h, rounds:, :] = jnp.ones((rounds, mask.shape[3]), jnp.float32)


def early_kernel(
    table, keep, swap, mates, below, above, inv_all, steering, lag_range,
    spec, inv, window, mask, sems,
):
    me = lax.rem(lax.axis_index(AXIS), Q)
    copies = [
        pltpu.make_async_copy(keep, spec.at[0], sems.at[0]),
        pltpu.make_async_copy(swap.at[0], spec.at[1], sems.at[1]),
        pltpu.make_async_copy(mates, spec.at[2:4], sems.at[2]),
        pltpu.make_async_copy(below, spec.at[Q : Q + 2], sems.at[3]),
        pltpu.make_async_copy(above, spec.at[2 * Q : 2 * Q + 2], sems.at[4]),
        pltpu.make_async_copy(inv_all.at[me], inv, sems.at[5]),
    ]
    for copy in copies:
        copy.start()
    window[...] = jnp.zeros_like(window)
    for copy in copies:
        copy.wait()
    channels = steering.shape[2]
    for p in range(Q):
        fill_mask(mask, p, spec, p, channels)
    for p in range(Q // 2):
        fill_mask(mask, Q + p, spec, 2 * Q + p, channels)
    run_units(table, me, spec, mask, steering, inv, lag_range, window)


def late_kernel(
    table, spec_in, inv, window_in, below, above, steering, lag_range,
    own, send, spec, window, mask, segs, sems,
):
    me = lax.rem(lax.axis_index(AXIS), Q)
    copies = [
        pltpu.make_async_copy(below, spec.at[Q + 2 : Q + 4], sems.at[0]),
        pltpu.make_async_copy(above, spec.at[2 * Q + 2 : 2 * Q + 4], sems.at[1]),
    ]
    for copy in copies:
        copy.start()
    for copy in copies:
        copy.wait()
    channels, angles = steering.shape[2], steering.shape[1]
    for p in range(Q):
        fill_mask(mask, p, spec, p, channels)
        fill_mask(mask, Q + p, spec, 2 * Q + p, channels)
    run_units(table, me, spec, mask, steering, inv, lag_range, window)

    width = window.shape[2] // 3

    def segment(s):
        total = None
        for slot, part in ((s, 1), (s - 1, 2), (s + 1, 0)):
            if 0 <= slot < 2 * Q:
                value = window[slot, :, part * width : (part + 1) * width]
                total = value if total is None else total + value
        return total

    for p in range(Q):
        segs[p, 0] = segment(p)
        segs[p, 1] = segment(Q + p)
        if p == 0:
            segs[p, 2] = segment(2 * Q)
        elif p == Q - 1:
            segs[p, 2] = segment(-1)
        else:
            segs[p, 2] = jnp.zeros((angles, width), jnp.float32)
    own[0] = segs[me]
    own[1] = segs[lax.bitwise_xor(me, 2)]
    send[0] = segs[lax.bitwise_xor(me, 1)].astype(jnp.bfloat16)
    send[1] = segs[lax.bitwise_xor(me, 3)].astype(jnp.bfloat16)


def join_kernel(keep, mate, swap, near, mates, sems):
    copies = [
        pltpu.make_async_copy(mate, mates.at[0], sems.at[0]),
        pltpu.make_async_copy(swap.at[1], mates.at[1], sems.at[1]),
        pltpu.make_async_copy(keep, near.at[0], sems.at[2]),
        pltpu.make_async_copy(swap.at[0], near.at[1], sems.at[3]),
    ]
    for copy in copies:
        copy.start()
    for copy in copies:
        copy.wait()


def core_sum_kernel(own, received, mine, send):
    mine[...] = own[0] + received[0].astype(jnp.float32)
    send[...] = (own[1] + received[1].astype(jnp.float32)).astype(jnp.bfloat16)


def plane_sum_kernel(own, received, middle, up, extra):
    middle[...] = own[0] + received[0].astype(jnp.float32)
    up[...] = (own[1] + received[1].astype(jnp.float32)).astype(jnp.bfloat16)
    extra[...] = (own[2] + received[2].astype(jnp.float32)).astype(jnp.bfloat16)


def image_kernel(middle, up, extra, image):
    image[...] = middle[...] + up[...].astype(jnp.float32) + extra[...].astype(jnp.float32)


VMEM_SPEC = pl.BlockSpec(memory_space=pltpu.VMEM)
SMEM_SPEC = pl.BlockSpec(memory_space=pltpu.SMEM)
HBM_SPEC = pl.BlockSpec(memory_space=pl.ANY)


def near_vmem(*values):
    return [pltpu.with_memory_space_constraint(value, pltpu.VMEM) for value in values]


def local_call(kernel, name, outs, *values, scratch=()):
    return pl.pallas_call(
        kernel,
        in_specs=[VMEM_SPEC] * len(values),
        out_specs=[VMEM_SPEC] * len(outs),
        out_shape=outs,
        scratch_shapes=list(scratch),
        compiler_params=pltpu.CompilerParams(vmem_limit_bytes=LIMIT),
        name=name,
    )(*near_vmem(*values))


def early_call(table, keep, swap, mates, below, above, inv_all, steering, lag_range):
    rows, cols = keep.shape
    angles, group = steering.shape[1], lag_range.shape[2]
    rounds = steering.shape[0] - 1
    return pl.pallas_call(
        early_kernel,
        in_specs=[SMEM_SPEC] + [VMEM_SPEC] * 5 + [HBM_SPEC] + [VMEM_SPEC] * 2,
        out_specs=[VMEM_SPEC] * 3,
        out_shape=[
            pltpu.VMEM((3 * Q, rows, cols), jnp.bfloat16),
            pltpu.VMEM((cols, L), jnp.bfloat16),
            pltpu.VMEM((2 * Q, angles, group), jnp.float32),
        ],
        scratch_shapes=[
            pltpu.VMEM((2 * Q, L // cols, 2 * rounds, cols), jnp.float32),
            pltpu.SemaphoreType.DMA((6,)),
        ],
        compiler_params=pltpu.CompilerParams(vmem_limit_bytes=LIMIT),
        name="early_pairs",
    )(table, *near_vmem(keep, swap, mates, below, above), inv_all, *near_vmem(steering, lag_range))


def late_call(table, spec, inv, window, below, above, steering, lag_range):
    cols = spec.shape[2]
    angles, group = steering.shape[1], lag_range.shape[2]
    rounds = steering.shape[0] - 1
    piece = (2, 3, angles, group // 3)
    return pl.pallas_call(
        late_kernel,
        in_specs=[SMEM_SPEC] + [VMEM_SPEC] * 7,
        out_specs=[VMEM_SPEC] * 4,
        out_shape=[
            pltpu.VMEM(piece, jnp.float32),
            pltpu.VMEM(piece, jnp.bfloat16),
            pltpu.VMEM(spec.shape, spec.dtype),
            pltpu.VMEM(window.shape, window.dtype),
        ],
        input_output_aliases={1: 2, 3: 3},
        scratch_shapes=[
            pltpu.VMEM((2 * Q, L // cols, 2 * rounds, cols), jnp.float32),
            pltpu.VMEM((Q,) + piece[1:], jnp.float32),
            pltpu.SemaphoreType.DMA((2,)),
        ],
        compiler_params=pltpu.CompilerParams(vmem_limit_bytes=LIMIT),
        name="late_pairs",
    )(table, *near_vmem(spec, inv, window, below, above, steering, lag_range))[:2]


def exchange(value, devices, target):
    pairs = [(i, target(i)) for i in range(devices) if target(i) is not None]
    pairs = [(i, j) for i, j in pairs if 0 <= j < devices]
    return lax.ppermute(value, AXIS, pairs)


def per_device(devices, strain, steering, lag_range, pair_listed, band_used):
    def shift(value, by):
        return exchange(value, devices, lambda i: i + by)

    def flip(value, by):
        return exchange(value, devices, lambda i: i ^ by)

    keep, mate, swap = spectrum_call(strain, pair_listed, jnp.transpose(band_used, (0, 2, 1)))
    swap = flip(swap, 1)
    pair = pltpu.VMEM((2,) + keep.shape, keep.dtype)
    near, mates = local_call(
        join_kernel, "join", [pair, pair], keep, mate, swap, scratch=[pltpu.SemaphoreType.DMA((4,))]
    )
    mates = flip(mates, 2)
    near_below, near_above = shift(near, Q), shift(near, -Q)
    far_below, far_above = shift(mates, Q), shift(mates, -Q)
    early, late = (jnp.asarray(t.reshape(Q, -1)) for t in unit_table(steering.shape[0] - 1))
    inv_all = jnp.asarray(inverse_table(strain.shape[1]))
    spec, inv, window = early_call(
        early, keep, swap, mates, near_below, near_above, inv_all, steering, lag_range
    )
    mine, send = late_call(
        late, spec, inv, window, far_below, far_above, steering, lag_range
    )
    piece = mine.shape[1:]
    mine, send = local_call(
        core_sum_kernel,
        "core_sum",
        [pltpu.VMEM(piece, jnp.float32), pltpu.VMEM(piece, jnp.bfloat16)],
        mine,
        flip(send, 1),
    )
    middle, up, extra = local_call(
        plane_sum_kernel,
        "plane_sum",
        [pltpu.VMEM(piece[1:], dtype) for dtype in (jnp.float32, jnp.bfloat16, jnp.bfloat16)],
        mine,
        flip(send, 2),
    )

    def ends(i):
        if i % Q == 0:
            return i + 2 * Q
        if i % Q == Q - 1:
            return i - Q
        return None

    up, extra = shift(up, Q), exchange(extra, devices, ends)
    return local_call(
        image_kernel,
        "image",
        [jax.ShapeDtypeStruct(middle.shape, jnp.float32)],
        middle,
        up,
        extra,
    )[0]


def solution(mesh):
    return jax.shard_map(
        functools.partial(per_device, mesh.shape[AXIS]),
        mesh=mesh,
        in_specs=(
            P(("win", AXIS), None),
            P(),
            P(),
            P(("win", AXIS), None),
            P(("win", AXIS), None, None),
        ),
        out_specs=P(None, ("win", AXIS)),
        check_vma=False,
    )
```

```python
import functools

import jax
import jax.numpy as jnp
import numpy as np
from jax import lax
from jax.experimental import pallas as pl
from jax.experimental.pallas import tpu as pltpu
from jax.sharding import PartitionSpec as P

AXIS = "fib"
F = 512
L = 512
Q = 4


def forward_table(samples):
    freqs = F // Q
    t = np.arange(samples // Q, dtype=np.int64)[None, :, None]
    k = Q * np.arange(freqs, dtype=np.int64)[None, None, :] + np.arange(Q)[:, None, None] + 1
    phase = (t * k % samples) * (2.0 * np.pi / samples)
    table = np.concatenate([np.cos(phase), -np.sin(phase)], axis=2) * samples ** (-0.5)
    return table.astype(jnp.bfloat16)


def inverse_table(samples):
    freqs = F // Q
    k = Q * np.arange(freqs, dtype=np.int64)[None, :, None] + np.arange(Q)[:, None, None] + 1
    lag = np.arange(L, dtype=np.int64)[None, None, :] - L // 2
    theta = (k * lag % samples) * (2.0 * np.pi / samples)
    table = np.concatenate([np.cos(theta), -np.sin(theta)], axis=1) * (2 * F) ** (-0.5)
    return table.astype(jnp.bfloat16)


def in_hbm(value):
    return pltpu.with_memory_space_constraint(value, pltpu.HBM)


def dot(a, b):
    return jnp.dot(a, b, preferred_element_type=jnp.float32)


def spectrum_kernel(listed, bands, x0, x1, x2, x3, table, near, mates, swap, acc, weight):
    step, steps = pl.program_id(0), pl.num_programs(0)
    half = table.shape[2] // 2
    channels = x0.shape[0]
    me = lax.rem(lax.axis_index(AXIS), Q)

    q0, q1, q2, q3 = (x[...].astype(jnp.float32) for x in (x0, x1, x2, x3))
    even, odd = q0 + q2, q1 + q3
    fold0 = (even + odd).astype(jnp.bfloat16)
    fold2 = (even - odd).astype(jnp.bfloat16)
    a = (q0 - q2).astype(jnp.bfloat16)
    b = (q1 - q3).astype(jnp.bfloat16)
    parts = [
        dot(a, table[0]),
        dot(b, table[0]),
        dot(fold2, table[1]),
        dot(a, table[2]),
        dot(b, table[2]),
        dot(fold0, table[3]),
    ]

    @pl.when(step == 0)
    def _():
        for n, part in enumerate(parts):
            acc[n] = part

    @pl.when((step > 0) & (step < steps - 1))
    def _():
        for n, part in enumerate(parts):
            acc[n] += part

    @pl.when(step == steps - 1)
    def _():
        p1, b1, s2, p3, b3, s0 = (acc[n] + part for n, part in enumerate(parts))
        s1 = jnp.concatenate([p1[:, :half] + b1[:, half:], p1[:, half:] - b1[:, :half]], axis=1)
        s3 = jnp.concatenate([p3[:, :half] - b3[:, half:], p3[:, half:] + b3[:, :half]], axis=1)
        outs = (near.at[0], swap.at[0], mates.at[0], swap.at[1])
        for s, value in enumerate((s1, s2, s3, s0)):
            value = value.astype(jnp.bfloat16)
            for p, out in enumerate(outs):

                @pl.when(lax.bitwise_xor(me, s) == p)
                def _():
                    out[:channels, :] = value

        cols = near.shape[2]
        nbands, rounds = bands.shape[1], bands.shape[2]
        width = L // nbands
        used = (listed[...] * bands[0]).astype(jnp.float32)
        for j in range(nbands):
            part, lane = divmod(j * width, cols)
            for d in range(rounds):
                row = part * rounds + d
                weight[row : row + 1, lane : lane + width] = jnp.broadcast_to(
                    used[j : j + 1, d : d + 1], (1, width)
                )
        for out in outs:
            out[channels:, :] = weight[...].astype(jnp.bfloat16)


def spectrum_call(strain, listed, bands, steps=2):
    channels, samples = strain.shape
    table = forward_table(samples)
    cols = table.shape[2]
    depth = samples // Q // steps
    rows = channels + bands.shape[2] * L // cols
    quarter = [
        pl.BlockSpec((channels, depth), lambda k, q=q: (0, q * steps + k)) for q in range(Q)
    ]
    return pl.pallas_call(
        spectrum_kernel,
        grid=(steps,),
        in_specs=[
            pl.BlockSpec(listed.shape, lambda k: (0, 0)),
            pl.BlockSpec(bands.shape, lambda k: (0, 0, 0)),
            *quarter,
            pl.BlockSpec((Q, depth, cols), lambda k: (0, k, 0)),
        ],
        out_specs=[pl.BlockSpec(memory_space=pltpu.VMEM)] * 3,
        out_shape=[
            pltpu.VMEM((2, rows, cols), jnp.bfloat16),
            pltpu.VMEM((2, rows, cols), jnp.bfloat16),
            pltpu.VMEM((2, rows, cols), jnp.bfloat16),
        ],
        scratch_shapes=[
            pltpu.VMEM((6, channels, cols), jnp.float32),
            pltpu.VMEM((rows - channels, cols), jnp.float32),
        ],
        compiler_params=pltpu.CompilerParams(
            dimension_semantics=("arbitrary",), vmem_limit_bytes=LIMIT
        ),
        name="spectrum",
    )(in_hbm(listed), in_hbm(bands), *[in_hbm(strain)] * Q, in_hbm(jnp.asarray(table)))


UNROLL = 3
LIMIT = 16 << 20


def unit_table(rounds):
    early, late = [], []
    for me in range(Q):
        units = ([], [])
        for i in range(2 * Q):
            for j in range(-Q, Q):
                d = i - j
                if not 0 <= d <= rounds or (i >= Q and j >= 0):
                    continue
                p, q = i % Q ^ me, j % Q ^ me
                target = p if i < Q else 2 * Q + p
                source = q if j >= 0 else Q + q
                far = (i >= Q and p >= Q // 2) or (j < 0 and q >= Q // 2)
                mask = p if i < Q else Q + p
                row = d - 1 if d else rounds
                units[far].append((target, source, d, i, mask, row))
        early.append(units[0])
        late.append(units[1])
    return np.asarray(early, np.int32), np.asarray(late, np.int32)


def run_units(table, me, spec, mask, steering, inv, lag_range, window):
    channels, angles = steering.shape[2], steering.shape[1]
    cols = spec.shape[2]
    half = cols // 2

    def body(n, carry):
        units = [
            [table[me, (n * UNROLL + u) * 6 + e] for e in range(6)] for u in range(UNROLL)
        ]
        beams = []
        for target, source, d, _, _, _ in units:
            near_re = spec[target, :channels, :half].astype(jnp.float32)
            near_im = spec[target, :channels, half:].astype(jnp.float32)
            far_re = spec[source, :channels, :half].astype(jnp.float32)
            far_im = spec[source, :channels, half:].astype(jnp.float32)
            real = near_re * far_re + near_im * far_im
            imag = near_im * far_re - near_re * far_im
            cross = jnp.concatenate([real, imag], axis=1).astype(jnp.bfloat16)
            beams.append(dot(steering[d], cross).astype(jnp.bfloat16))
        beams = dot(jnp.concatenate(beams, axis=0), inv[...])
        for u, (_, _, d, slot, target, row) in enumerate(units):
            weight = jnp.concatenate(
                [mask[target, h, pl.ds(row, 1), :] for h in range(L // cols)], axis=1
            )
            masked = (beams[u * angles : (u + 1) * angles, :] * weight).astype(jnp.bfloat16)
            window[slot] += dot(masked, lag_range[d])
        return carry

    lax.fori_loop(0, table.shape[1] // (6 * UNROLL), body, 0)


def fill_mask(mask, entry, spec, slot, channels):
    rounds = mask.shape[2] // 2
    rows = spec[slot, channels:, :].astype(jnp.float32)
    for h in range(mask.shape[1]):
        mask[entry, h, :rounds, :] = rows[h * rounds : (h + 1) * rounds, :]
        mask[entry, h, rounds:, :] = jnp.ones((rounds, mask.shape[3]), jnp.float32)


def early_kernel(
    table, near, mates, below, above, inv, steering, lag_range, spec, window, mask
):
    me = lax.rem(lax.axis_index(AXIS), Q)
    spec[0:2] = near[...]
    spec[2:4] = mates[...]
    spec[Q : Q + 2] = below[...]
    spec[2 * Q : 2 * Q + 2] = above[...]
    window[...] = jnp.zeros_like(window)
    channels = steering.shape[2]
    for p in range(Q):
        fill_mask(mask, p, spec, p, channels)
    for p in range(Q // 2):
        fill_mask(mask, Q + p, spec, 2 * Q + p, channels)
    run_units(table, me, spec, mask, steering, inv.at[me], lag_range, window)


def late_kernel(
    table, spec_in, window_in, below, above, inv, steering, lag_range,
    keep, send, spec, window, mask,
):
    me = lax.rem(lax.axis_index(AXIS), Q)
    spec[Q + 2 : Q + 4] = below[...]
    spec[2 * Q + 2 : 2 * Q + 4] = above[...]
    channels = steering.shape[2]
    for p in range(Q):
        fill_mask(mask, p, spec, p, channels)
        fill_mask(mask, Q + p, spec, 2 * Q + p, channels)
    run_units(table, me, spec, mask, steering, inv.at[me], lag_range, window)

    width = window.shape[2] // 3

    def segment(s):
        total = None
        for slot, part in ((s, 1), (s - 1, 2), (s + 1, 0)):
            if 0 <= slot < 2 * Q:
                value = window[slot, :, part * width : (part + 1) * width]
                total = value if total is None else total + value
        return total

    core = lax.rem(me, 2)
    here = [segment(s) for s in list(range(Q)) + [2 * Q, -1]]
    there = [segment(Q + p) for p in range(Q)]

    @pl.when(core == 0)
    def _():
        for n, value in enumerate(there):
            keep[n] = value
        for n in range(Q, Q + 2):
            keep[n] = jnp.zeros_like(there[0])
        for n, value in enumerate(here):
            send[n] = value.astype(jnp.bfloat16)

    @pl.when(core == 1)
    def _():
        for n, value in enumerate(here):
            keep[n] = value
        for n, value in enumerate(there):
            send[n] = value.astype(jnp.bfloat16)
        for n in range(Q, Q + 2):
            send[n] = jnp.zeros_like(there[0]).astype(jnp.bfloat16)


def join_kernel(swap, near_in, mates_in, near, mates):
    near[1] = swap[0]
    mates[1] = swap[1]


def core_sum_kernel(kept, received, mine, send):
    side = lax.rem(lax.axis_index(AXIS), Q) // 2

    def total(n):
        return kept[n] + received[n].astype(jnp.float32)

    for n in range(2):
        mine[n] = total(2 * side + n)
        send[n] = total(2 * (1 - side) + n).astype(jnp.bfloat16)
    mine[2] = total(Q + side)
    send[2] = total(Q + 1 - side).astype(jnp.bfloat16)


def plane_sum_kernel(kept, received, mine, send):
    core = lax.rem(lax.axis_index(AXIS), 2)
    totals = [kept[n] + received[n].astype(jnp.float32) for n in range(3)]
    mine[0] = totals[0]
    mine[1] = totals[1]

    @pl.when(core == 0)
    def _():
        send[0] = totals[0].astype(jnp.bfloat16)
        send[1] = totals[1].astype(jnp.bfloat16)

    @pl.when(core == 1)
    def _():
        send[0] = totals[2].astype(jnp.bfloat16)
        send[1] = jnp.zeros_like(totals[2]).astype(jnp.bfloat16)


def end_sum_kernel(kept, received, mine, send):
    me = lax.rem(lax.axis_index(AXIS), Q)
    first = received[0].astype(jnp.float32)
    second = received[1].astype(jnp.float32)
    core, side = lax.rem(me, 2), me // 2

    @pl.when(core == 0)
    def _():
        mine[...] = first
        send[...] = second

    @pl.when((core == 1) & (side == 0))
    def _():
        mine[...] = kept[1]
        send[...] = kept[0] + first

    @pl.when((core == 1) & (side == 1))
    def _():
        mine[...] = kept[1] + first
        send[...] = kept[0]


def image_kernel(kept, received, image):
    image[...] = kept[...] + received[...]


VMEM_SPEC = pl.BlockSpec(memory_space=pltpu.VMEM)
SMEM_SPEC = pl.BlockSpec(memory_space=pltpu.SMEM)
HBM_SPEC = pl.BlockSpec(memory_space=pl.ANY)


def near_vmem(*values):
    return [pltpu.with_memory_space_constraint(value, pltpu.VMEM) for value in values]


def local_call(kernel, name, outs, *values, aliases={}):
    return pl.pallas_call(
        kernel,
        in_specs=[VMEM_SPEC] * len(values),
        out_specs=[VMEM_SPEC] * len(outs),
        out_shape=outs,
        input_output_aliases=aliases,
        compiler_params=pltpu.CompilerParams(vmem_limit_bytes=LIMIT),
        name=name,
    )(*near_vmem(*values))


def early_call(table, near, mates, below, above, inv, steering, lag_range):
    _, rows, cols = near.shape
    angles, group = steering.shape[1], lag_range.shape[2]
    rounds = steering.shape[0] - 1
    return pl.pallas_call(
        early_kernel,
        in_specs=[SMEM_SPEC] + [VMEM_SPEC] * 7,
        out_specs=[VMEM_SPEC] * 2,
        out_shape=[
            pltpu.VMEM((3 * Q, rows, cols), jnp.bfloat16),
            pltpu.VMEM((2 * Q, angles, group), jnp.float32),
        ],
        scratch_shapes=[pltpu.VMEM((2 * Q, L // cols, 2 * rounds, cols), jnp.float32)],
        compiler_params=pltpu.CompilerParams(vmem_limit_bytes=LIMIT),
        name="early_pairs",
    )(table, *near_vmem(near, mates, below, above, inv, steering, lag_range))


def late_call(table, spec, window, below, above, inv, steering, lag_range):
    cols = spec.shape[2]
    angles, group = steering.shape[1], lag_range.shape[2]
    rounds = steering.shape[0] - 1
    pieces = (Q + 2, angles, group // 3)
    return pl.pallas_call(
        late_kernel,
        in_specs=[SMEM_SPEC] + [VMEM_SPEC] * 7,
        out_specs=[VMEM_SPEC] * 4,
        out_shape=[
            pltpu.VMEM(pieces, jnp.float32),
            pltpu.VMEM(pieces, jnp.bfloat16),
            pltpu.VMEM(spec.shape, spec.dtype),
            pltpu.VMEM(window.shape, window.dtype),
        ],
        input_output_aliases={1: 2, 2: 3},
        scratch_shapes=[pltpu.VMEM((2 * Q, L // cols, 2 * rounds, cols), jnp.float32)],
        compiler_params=pltpu.CompilerParams(vmem_limit_bytes=LIMIT),
        name="late_pairs",
    )(table, *near_vmem(spec, window, below, above, inv, steering, lag_range))[:2]


def exchange(value, devices, target):
    pairs = [(i, target(i)) for i in range(devices) if target(i) is not None]
    pairs = [(i, j) for i, j in pairs if 0 <= j < devices]
    return lax.ppermute(value, AXIS, pairs)


def per_device(devices, strain, steering, lag_range, pair_listed, band_used):
    def shift(value, by):
        return exchange(value, devices, lambda i: i + by)

    def flip(value, by):
        return exchange(value, devices, lambda i: i ^ by)

    near, mates, swap = spectrum_call(strain, pair_listed, jnp.transpose(band_used, (0, 2, 1)))
    joined = pltpu.VMEM(near.shape, near.dtype)
    near, mates = local_call(
        join_kernel, "join", [joined, joined], flip(swap, 1), near, mates, aliases={1: 0, 2: 1}
    )
    mates = flip(mates, 2)
    near_below, near_above = shift(near, Q), shift(near, -Q)
    far_below, far_above = shift(mates, Q), shift(mates, -Q)
    early, late = (jnp.asarray(t.reshape(Q, -1)) for t in unit_table(steering.shape[0] - 1))
    inv = jnp.asarray(inverse_table(strain.shape[1]))
    shared = (inv, steering, lag_range)
    spec, window = early_call(early, near, mates, near_below, near_above, *shared)
    kept, send = late_call(late, spec, window, far_below, far_above, *shared)

    def pieces(count, dtype):
        return pltpu.VMEM(((count,) if count else ()) + kept.shape[1:], dtype)

    def ends(i):
        if i % 2 == 0:
            return i + Q
        return i + 2 * Q if i % Q < 2 else i - Q

    kept, send = local_call(
        core_sum_kernel,
        "core_sum",
        [pieces(3, jnp.float32), pieces(3, jnp.bfloat16)],
        kept,
        flip(send, 1),
    )
    kept, send = local_call(
        plane_sum_kernel,
        "plane_sum",
        [pieces(2, jnp.float32), pieces(2, jnp.bfloat16)],
        kept,
        flip(send, 2),
    )
    kept, send = local_call(
        end_sum_kernel,
        "end_sum",
        [pieces(0, jnp.float32), pieces(0, jnp.float32)],
        kept,
        exchange(send, devices, ends),
    )
    return local_call(
        image_kernel,
        "image",
        [jax.ShapeDtypeStruct(kept.shape, jnp.float32)],
        kept,
        flip(send, 1),
    )[0]


def solution(mesh):
    return jax.shard_map(
        functools.partial(per_device, mesh.shape[AXIS]),
        mesh=mesh,
        in_specs=(
            P(("win", AXIS), None),
            P(),
            P(),
            P(("win", AXIS), None),
            P(("win", AXIS), None, None),
        ),
        out_specs=P(None, ("win", AXIS)),
        check_vma=False,
    )
```

```python
import functools

import jax
import jax.numpy as jnp
import numpy as np
from jax import lax
from jax.experimental import pallas as pl
from jax.experimental.pallas import tpu as pltpu
from jax.sharding import PartitionSpec as P

AXIS = "fib"
F = 512
L = 512
Q = 4


def forward_table(samples):
    freqs = F // Q
    t = np.arange(samples // Q, dtype=np.int64)[None, :, None]
    k = Q * np.arange(freqs, dtype=np.int64)[None, None, :] + np.arange(Q)[:, None, None] + 1
    phase = (t * k % samples) * (2.0 * np.pi / samples)
    table = np.concatenate([np.cos(phase), -np.sin(phase)], axis=2) * samples ** (-0.5)
    return table.astype(jnp.bfloat16)


def inverse_table(samples):
    freqs = F // Q
    k = Q * np.arange(freqs, dtype=np.int64)[None, :, None] + np.arange(Q)[:, None, None] + 1
    lag = np.arange(L, dtype=np.int64)[None, None, :] - L // 2
    theta = (k * lag % samples) * (2.0 * np.pi / samples)
    table = np.concatenate([np.cos(theta), -np.sin(theta)], axis=1) * (2 * F) ** (-0.5)
    return table.astype(jnp.bfloat16)


def in_hbm(value):
    return pltpu.with_memory_space_constraint(value, pltpu.HBM)


def dot(a, b):
    return jnp.dot(a, b, preferred_element_type=jnp.float32)


def spectrum_kernel(listed, bands, x0, x1, x2, x3, table, near, mates, swap, acc, weight):
    step, steps = pl.program_id(0), pl.num_programs(0)
    half = table.shape[2] // 2
    channels = x0.shape[0]
    me = lax.rem(lax.axis_index(AXIS), Q)

    q0, q1, q2, q3 = (x[...].astype(jnp.float32) for x in (x0, x1, x2, x3))
    even, odd = q0 + q2, q1 + q3
    fold0 = (even + odd).astype(jnp.bfloat16)
    fold2 = (even - odd).astype(jnp.bfloat16)
    a = (q0 - q2).astype(jnp.bfloat16)
    b = (q1 - q3).astype(jnp.bfloat16)
    parts = [
        dot(a, table[0]),
        dot(b, table[0]),
        dot(fold2, table[1]),
        dot(a, table[2]),
        dot(b, table[2]),
        dot(fold0, table[3]),
    ]

    @pl.when(step == 0)
    def _():
        for n, part in enumerate(parts):
            acc[n] = part

    @pl.when((step > 0) & (step < steps - 1))
    def _():
        for n, part in enumerate(parts):
            acc[n] += part

    @pl.when(step == steps - 1)
    def _():
        p1, b1, s2, p3, b3, s0 = (acc[n] + part for n, part in enumerate(parts))
        s1 = jnp.concatenate([p1[:, :half] + b1[:, half:], p1[:, half:] - b1[:, :half]], axis=1)
        s3 = jnp.concatenate([p3[:, :half] - b3[:, half:], p3[:, half:] + b3[:, :half]], axis=1)
        outs = (near.at[0], swap.at[0], mates.at[0], swap.at[1])
        for s, value in enumerate((s1, s2, s3, s0)):
            value = value.astype(jnp.bfloat16)
            for p, out in enumerate(outs):

                @pl.when(lax.bitwise_xor(me, s) == p)
                def _():
                    out[:channels, :] = value

        cols = near.shape[2]
        nbands, rounds = bands.shape[1], bands.shape[2]
        width = L // nbands
        used = (listed[...] * bands[0]).astype(jnp.float32)
        for j in range(nbands):
            part, lane = divmod(j * width, cols)
            for d in range(rounds):
                row = part * rounds + d
                weight[row : row + 1, lane : lane + width] = jnp.broadcast_to(
                    used[j : j + 1, d : d + 1], (1, width)
                )
        for out in outs:
            out[channels:, :] = weight[...].astype(jnp.bfloat16)


def spectrum_call(strain, listed, bands, steps=2):
    channels, samples = strain.shape
    table = forward_table(samples)
    cols = table.shape[2]
    depth = samples // Q // steps
    rows = channels + bands.shape[2] * L // cols
    quarter = [
        pl.BlockSpec((channels, depth), lambda k, q=q: (0, q * steps + k)) for q in range(Q)
    ]
    return pl.pallas_call(
        spectrum_kernel,
        grid=(steps,),
        in_specs=[
            pl.BlockSpec(listed.shape, lambda k: (0, 0)),
            pl.BlockSpec(bands.shape, lambda k: (0, 0, 0)),
            *quarter,
            pl.BlockSpec((Q, depth, cols), lambda k: (0, k, 0)),
        ],
        out_specs=[pl.BlockSpec(memory_space=pltpu.VMEM)] * 3,
        out_shape=[
            pltpu.VMEM((2, rows, cols), jnp.bfloat16),
            pltpu.VMEM((2, rows, cols), jnp.bfloat16),
            pltpu.VMEM((2, rows, cols), jnp.bfloat16),
        ],
        scratch_shapes=[
            pltpu.VMEM((6, channels, cols), jnp.float32),
            pltpu.VMEM((rows - channels, cols), jnp.float32),
        ],
        compiler_params=pltpu.CompilerParams(
            dimension_semantics=("arbitrary",), vmem_limit_bytes=LIMIT
        ),
        name="spectrum",
    )(in_hbm(listed), in_hbm(bands), *[in_hbm(strain)] * Q, in_hbm(jnp.asarray(table)))


UNROLL = 3
LIMIT = 16 << 20


def unit_table(rounds):
    early, late = [], []
    for me in range(Q):
        units = ([], [])
        for i in range(2 * Q):
            for j in range(-Q, Q):
                d = i - j
                if not 0 <= d <= rounds or (i >= Q and j >= 0):
                    continue
                p, q = i % Q ^ me, j % Q ^ me
                target = p if i < Q else 2 * Q + p
                source = q if j >= 0 else Q + q
                far = (i >= Q and p >= Q // 2) or (j < 0 and q >= Q // 2)
                mask = p if i < Q else Q + p
                row = d - 1 if d else rounds
                units[far].append((target, source, d, i, mask, row))
        early.append(units[0])
        late.append(units[1])
    return np.asarray(early, np.int32), np.asarray(late, np.int32)


def run_units(table, me, spec, mask, steering, inv, lag_range, window):
    channels, angles = steering.shape[2], steering.shape[1]
    cols = spec.shape[2]
    half = cols // 2

    def body(n, carry):
        units = [
            [table[me, (n * UNROLL + u) * 6 + e] for e in range(6)] for u in range(UNROLL)
        ]
        beams = []
        for target, source, d, _, _, _ in units:
            near_re = spec[target, :channels, :half].astype(jnp.float32)
            near_im = spec[target, :channels, half:].astype(jnp.float32)
            far_re = spec[source, :channels, :half].astype(jnp.float32)
            far_im = spec[source, :channels, half:].astype(jnp.float32)
            real = near_re * far_re + near_im * far_im
            imag = near_im * far_re - near_re * far_im
            cross = jnp.concatenate([real, imag], axis=1).astype(jnp.bfloat16)
            beams.append(dot(steering[d], cross).astype(jnp.bfloat16))
        beams = dot(jnp.concatenate(beams, axis=0), inv[...])
        for u, (_, _, d, slot, target, row) in enumerate(units):
            weight = jnp.concatenate(
                [mask[target, h, pl.ds(row, 1), :] for h in range(L // cols)], axis=1
            )
            masked = (beams[u * angles : (u + 1) * angles, :] * weight).astype(jnp.bfloat16)
            window[slot] += dot(masked, lag_range[d])
        return carry

    lax.fori_loop(0, table.shape[1] // (6 * UNROLL), body, 0)


def fill_mask(mask, entry, spec, slot, channels):
    rounds = mask.shape[2] // 2
    rows = spec[slot, channels:, :].astype(jnp.float32)
    for h in range(mask.shape[1]):
        mask[entry, h, :rounds, :] = rows[h * rounds : (h + 1) * rounds, :]
        mask[entry, h, rounds:, :] = jnp.ones((rounds, mask.shape[3]), jnp.float32)


def neighbour_slots():
    parity = lax.rem(lax.axis_index(AXIS) // Q, 2)
    return Q * (2 - parity), Q * (1 + parity)


def early_kernel(
    table, near, mates, even, odd, inv, steering, lag_range, spec, window, mask
):
    me = lax.rem(lax.axis_index(AXIS), Q)
    even_slot, odd_slot = neighbour_slots()
    spec[0:2] = near[...]
    spec[2:4] = mates[...]
    spec[pl.ds(even_slot, 2)] = even[...]
    spec[pl.ds(odd_slot, 2)] = odd[...]
    window[...] = jnp.zeros_like(window)
    channels = steering.shape[2]
    for p in range(Q):
        fill_mask(mask, p, spec, p, channels)
    for p in range(Q // 2):
        fill_mask(mask, Q + p, spec, 2 * Q + p, channels)
    run_units(table, me, spec, mask, steering, inv.at[me], lag_range, window)


def late_kernel(
    table, spec_in, window_in, even, odd, inv, steering, lag_range,
    keep, send, spec, window, mask,
):
    me = lax.rem(lax.axis_index(AXIS), Q)
    even_slot, odd_slot = neighbour_slots()
    spec[pl.ds(even_slot + 2, 2)] = even[...]
    spec[pl.ds(odd_slot + 2, 2)] = odd[...]
    channels = steering.shape[2]
    for p in range(Q):
        fill_mask(mask, p, spec, p, channels)
        fill_mask(mask, Q + p, spec, 2 * Q + p, channels)
    run_units(table, me, spec, mask, steering, inv.at[me], lag_range, window)

    width = window.shape[2] // 3

    def segment(s):
        total = None
        for slot, part in ((s, 1), (s - 1, 2), (s + 1, 0)):
            if 0 <= slot < 2 * Q:
                value = window[slot, :, part * width : (part + 1) * width]
                total = value if total is None else total + value
        return total

    core = lax.rem(me, 2)
    here = [segment(s) for s in list(range(Q)) + [2 * Q, -1]]
    there = [segment(Q + p) for p in range(Q)]

    @pl.when(core == 0)
    def _():
        for n, value in enumerate(there):
            keep[n] = value
        for n in range(Q, Q + 2):
            keep[n] = jnp.zeros_like(there[0])
        for n, value in enumerate(here):
            send[n] = value.astype(jnp.bfloat16)

    @pl.when(core == 1)
    def _():
        for n, value in enumerate(here):
            keep[n] = value
        for n, value in enumerate(there):
            send[n] = value.astype(jnp.bfloat16)
        for n in range(Q, Q + 2):
            send[n] = jnp.zeros_like(there[0]).astype(jnp.bfloat16)


def join_kernel(swap, near_in, mates_in, near, mates):
    near[1] = swap[0]
    mates[1] = swap[1]


def core_sum_kernel(kept, received, mine, send):
    side = lax.rem(lax.axis_index(AXIS), Q) // 2

    def total(n):
        return kept[n] + received[n].astype(jnp.float32)

    for n in range(2):
        mine[n] = total(2 * side + n)
        send[n] = total(2 * (1 - side) + n).astype(jnp.bfloat16)
    mine[2] = total(Q + side)
    send[2] = total(Q + 1 - side).astype(jnp.bfloat16)


def plane_sum_kernel(kept, received, mine, send):
    core = lax.rem(lax.axis_index(AXIS), 2)
    totals = [kept[n] + received[n].astype(jnp.float32) for n in range(3)]
    mine[0] = totals[0]
    mine[1] = totals[1]

    @pl.when(core == 0)
    def _():
        send[0] = totals[0].astype(jnp.bfloat16)
        send[1] = totals[1].astype(jnp.bfloat16)

    @pl.when(core == 1)
    def _():
        send[0] = totals[2].astype(jnp.bfloat16)
        send[1] = jnp.zeros_like(totals[2]).astype(jnp.bfloat16)


def end_sum_kernel(kept, received, mine, send):
    me = lax.rem(lax.axis_index(AXIS), Q)
    first = received[0].astype(jnp.float32)
    second = received[1].astype(jnp.float32)
    core, side = lax.rem(me, 2), me // 2

    @pl.when(core == 0)
    def _():
        mine[...] = first
        send[...] = second

    @pl.when((core == 1) & (side == 0))
    def _():
        mine[...] = kept[1]
        send[...] = kept[0] + first

    @pl.when((core == 1) & (side == 1))
    def _():
        mine[...] = kept[1] + first
        send[...] = kept[0]


def image_kernel(kept, received, image):
    image[...] = kept[...] + received[...]


VMEM_SPEC = pl.BlockSpec(memory_space=pltpu.VMEM)
SMEM_SPEC = pl.BlockSpec(memory_space=pltpu.SMEM)
HBM_SPEC = pl.BlockSpec(memory_space=pl.ANY)


def near_vmem(*values):
    return [pltpu.with_memory_space_constraint(value, pltpu.VMEM) for value in values]


def local_call(kernel, name, outs, *values, aliases={}):
    return pl.pallas_call(
        kernel,
        in_specs=[VMEM_SPEC] * len(values),
        out_specs=[VMEM_SPEC] * len(outs),
        out_shape=outs,
        input_output_aliases=aliases,
        compiler_params=pltpu.CompilerParams(vmem_limit_bytes=LIMIT),
        name=name,
    )(*near_vmem(*values))


def early_call(table, near, mates, even, odd, inv, steering, lag_range):
    _, rows, cols = near.shape
    angles, group = steering.shape[1], lag_range.shape[2]
    rounds = steering.shape[0] - 1
    return pl.pallas_call(
        early_kernel,
        in_specs=[SMEM_SPEC] + [VMEM_SPEC] * 7,
        out_specs=[VMEM_SPEC] * 2,
        out_shape=[
            pltpu.VMEM((3 * Q, rows, cols), jnp.bfloat16),
            pltpu.VMEM((2 * Q, angles, group), jnp.float32),
        ],
        scratch_shapes=[pltpu.VMEM((2 * Q, L // cols, 2 * rounds, cols), jnp.float32)],
        compiler_params=pltpu.CompilerParams(vmem_limit_bytes=LIMIT),
        name="early_pairs",
    )(table, *near_vmem(near, mates, even, odd, inv, steering, lag_range))


def late_call(table, spec, window, even, odd, inv, steering, lag_range):
    cols = spec.shape[2]
    angles, group = steering.shape[1], lag_range.shape[2]
    rounds = steering.shape[0] - 1
    pieces = (Q + 2, angles, group // 3)
    return pl.pallas_call(
        late_kernel,
        in_specs=[SMEM_SPEC] + [VMEM_SPEC] * 7,
        out_specs=[VMEM_SPEC] * 4,
        out_shape=[
            pltpu.VMEM(pieces, jnp.float32),
            pltpu.VMEM(pieces, jnp.bfloat16),
            pltpu.VMEM(spec.shape, spec.dtype),
            pltpu.VMEM(window.shape, window.dtype),
        ],
        input_output_aliases={1: 2, 2: 3},
        scratch_shapes=[pltpu.VMEM((2 * Q, L // cols, 2 * rounds, cols), jnp.float32)],
        compiler_params=pltpu.CompilerParams(vmem_limit_bytes=LIMIT),
        name="late_pairs",
    )(table, *near_vmem(spec, window, even, odd, inv, steering, lag_range))[:2]


def exchange(value, devices, target):
    pairs = [(i, target(i)) for i in range(devices) if target(i) is not None]
    pairs = [(i, j) for i, j in pairs if 0 <= j < devices]
    return lax.ppermute(value, AXIS, pairs)


def per_device(devices, strain, steering, lag_range, pair_listed, band_used):
    def planes(value, parity):
        return exchange(value, devices, lambda i: i + (Q if i // Q % 2 == parity else -Q))

    def flip(value, by):
        return exchange(value, devices, lambda i: i ^ by)

    near, mates, swap = spectrum_call(strain, pair_listed, jnp.transpose(band_used, (0, 2, 1)))
    joined = pltpu.VMEM(near.shape, near.dtype)
    near, mates = local_call(
        join_kernel, "join", [joined, joined], flip(swap, 1), near, mates, aliases={1: 0, 2: 1}
    )
    mates = flip(mates, 2)
    near_odd, near_even = planes(near, 1), planes(near, 0)
    far_odd, far_even = planes(mates, 1), planes(mates, 0)
    early, late = (jnp.asarray(t.reshape(Q, -1)) for t in unit_table(steering.shape[0] - 1))
    inv = jnp.asarray(inverse_table(strain.shape[1]))
    near, steering, lag_range, inv = lax.optimization_barrier((near, steering, lag_range, inv))
    shared = (inv, steering, lag_range)
    spec, window = early_call(early, near, mates, near_even, near_odd, *shared)
    kept, send = late_call(late, spec, window, far_even, far_odd, *shared)

    def pieces(count, dtype):
        return pltpu.VMEM(((count,) if count else ()) + kept.shape[1:], dtype)

    def ends(i):
        if i % 2 == 0:
            return i + Q
        return i + 2 * Q if i % Q < 2 else i - Q

    kept, send = local_call(
        core_sum_kernel,
        "core_sum",
        [pieces(3, jnp.float32), pieces(3, jnp.bfloat16)],
        kept,
        flip(send, 1),
    )
    kept, send = local_call(
        plane_sum_kernel,
        "plane_sum",
        [pieces(2, jnp.float32), pieces(2, jnp.bfloat16)],
        kept,
        flip(send, 2),
    )
    kept, send = local_call(
        end_sum_kernel,
        "end_sum",
        [pieces(0, jnp.float32), pieces(0, jnp.float32)],
        kept,
        exchange(send, devices, ends),
    )
    return local_call(
        image_kernel,
        "image",
        [jax.ShapeDtypeStruct(kept.shape, jnp.float32)],
        kept,
        flip(send, 1),
    )[0]


def solution(mesh):
    return jax.shard_map(
        functools.partial(per_device, mesh.shape[AXIS]),
        mesh=mesh,
        in_specs=(
            P(("win", AXIS), None),
            P(),
            P(),
            P(("win", AXIS), None),
            P(("win", AXIS), None, None),
        ),
        out_specs=P(None, ("win", AXIS)),
        check_vma=False,
    )
```

```python
import functools

import jax
import jax.numpy as jnp
import numpy as np
from jax import lax
from jax.experimental import pallas as pl
from jax.experimental.pallas import tpu as pltpu
from jax.sharding import PartitionSpec as P

AXIS = "fib"
F = 512
L = 512
Q = 4
LIMIT = 16 << 20
VMEM_SPEC = pl.BlockSpec(memory_space=pltpu.VMEM)
SMEM_SPEC = pl.BlockSpec(memory_space=pltpu.SMEM)
HBM_SPEC = pl.BlockSpec(memory_space=pl.ANY)


def forward_table(samples):
    freqs = F // Q
    t = np.arange(samples // Q, dtype=np.int64)[None, :, None]
    k = Q * np.arange(freqs, dtype=np.int64)[None, None, :] + np.arange(Q)[:, None, None] + 1
    phase = (t * k % samples) * (2.0 * np.pi / samples)
    table = np.concatenate([np.cos(phase), -np.sin(phase)], axis=2) * samples ** (-0.5)
    return np.stack([table[0::2], table[1::2]]).astype(jnp.bfloat16)


def inverse_table(samples):
    freqs = F // Q
    k = Q * np.arange(freqs, dtype=np.int64)[None, :, None] + np.arange(Q)[:, None, None] + 1
    lag = np.arange(L, dtype=np.int64)[None, None, :] - L // 2
    theta = (k * lag % samples) * (2.0 * np.pi / samples)
    table = np.concatenate([np.cos(theta), -np.sin(theta)], axis=1) * (2 * F) ** (-0.5)
    return table.astype(jnp.bfloat16)


def in_hbm(value):
    return pltpu.with_memory_space_constraint(value, pltpu.HBM)


def dot(a, b):
    return jnp.dot(a, b, preferred_element_type=jnp.float32)


def complex_classes(folds, table):
    channels = folds.shape[1]
    half = table.shape[2] // 2
    both = folds[...].reshape(2 * channels, folds.shape[2])
    values = []
    for n, sign in ((0, 1.0), (1, -1.0)):
        product = dot(both, table[n])
        a, b = product[:channels], product[channels:] * sign
        values.append(
            jnp.concatenate([a[:, :half] + b[:, half:], a[:, half:] - b[:, :half]], axis=1)
        )
    return values


def real_classes(folds, table):
    return [dot(folds[n], table[n]) for n in range(2)]


def send_kernel(strain, table, listed, bands, swap, folds, kept_table, time, sent_table, sems):
    me = lax.rem(lax.axis_index(AXIS), Q)
    core, side = lax.rem(me, 2), me // 2
    channels, samples = strain.shape
    quarter = samples // Q
    depth = quarter // 2
    copies = []
    for h in range(2):
        for q in range(Q):
            part = (slice(None), pl.ds(q * quarter + h * depth, depth))
            copies.append(
                pltpu.make_async_copy(strain.at[part], time.at[part], sems.at[h * Q + q])
            )
    tables = [
        pltpu.make_async_copy(table.at[1 - core], sent_table, sems.at[2 * Q]),
        pltpu.make_async_copy(table.at[core], kept_table, sems.at[2 * Q + 1]),
    ]
    for copy in copies + tables:
        copy.start()

    nbands = bands.shape[1]
    width = swap.shape[2] // nbands
    rounds = bands.shape[2]
    used = (listed[...] * bands[0]).astype(jnp.float32)
    pick = lax.broadcasted_iota(jnp.int32, (rounds, rounds), 0) == lax.broadcasted_iota(
        jnp.int32, (rounds, rounds), 1
    )
    weight = jnp.concatenate(
        [
            jnp.broadcast_to(
                jnp.sum(
                    jnp.where(pick, jnp.broadcast_to(used[j : j + 1], (rounds, rounds)), 0.0),
                    axis=1,
                    keepdims=True,
                ),
                (rounds, width),
            )
            for j in range(nbands)
        ],
        axis=1,
    ).astype(jnp.bfloat16)
    for n in range(2):
        swap[n, channels:, :] = weight

    for h in range(2):
        for copy in copies[h * Q : (h + 1) * Q]:
            copy.wait()
        here = pl.ds(h * depth, depth)
        q0, q1, q2, q3 = (time[:, pl.ds(q * quarter + h * depth, depth)] for q in range(Q))
        folds[0, 0, :, here] = q0 - q2
        folds[0, 1, :, here] = q1 - q3
        even = q0.astype(jnp.float32) + q2.astype(jnp.float32)
        odd = q1.astype(jnp.float32) + q3.astype(jnp.float32)
        folds[1, 0, :, here] = (even - odd).astype(jnp.bfloat16)
        folds[1, 1, :, here] = (even + odd).astype(jnp.bfloat16)
    tables[0].wait()

    def store(values):
        for n, value in enumerate(values):
            swap[lax.bitwise_xor(side, n), :channels, :] = value.astype(jnp.bfloat16)

    @pl.when(core == 0)
    def _():
        store(real_classes(folds.at[1], sent_table))

    @pl.when(core == 1)
    def _():
        store(complex_classes(folds.at[0], sent_table))

    tables[1].wait()


def keep_kernel(swap, folds, table, near, mates):
    me = lax.rem(lax.axis_index(AXIS), Q)
    core, side = lax.rem(me, 2), me // 2
    channels = folds.shape[2]
    near[0, channels:, :] = swap[0, channels:, :]
    mates[0, channels:, :] = swap[0, channels:, :]

    def store(values):
        for n, value in enumerate(values):
            value = value.astype(jnp.bfloat16)

            @pl.when(side == n)
            def _():
                near[0, :channels, :] = value

            @pl.when(side != n)
            def _():
                mates[0, :channels, :] = value

    @pl.when(core == 0)
    def _():
        store(complex_classes(folds.at[0], table))

    @pl.when(core == 1)
    def _():
        store(real_classes(folds.at[1], table))


def send_call(strain, listed, bands):
    channels, samples = strain.shape
    table = forward_table(samples)
    rows, cols = channels + bands.shape[2], table.shape[3]
    quarter = samples // Q
    return pl.pallas_call(
        send_kernel,
        in_specs=[HBM_SPEC, HBM_SPEC, VMEM_SPEC, VMEM_SPEC],
        out_specs=[VMEM_SPEC] * 3,
        out_shape=[
            pltpu.VMEM((2, rows, cols), jnp.bfloat16),
            pltpu.VMEM((2, 2, channels, quarter), jnp.bfloat16),
            pltpu.VMEM((2, quarter, cols), jnp.bfloat16),
        ],
        scratch_shapes=[
            pltpu.VMEM((channels, samples), jnp.bfloat16),
            pltpu.VMEM((2, quarter, cols), jnp.bfloat16),
            pltpu.SemaphoreType.DMA((2 * Q + 2,)),
        ],
        compiler_params=pltpu.CompilerParams(vmem_limit_bytes=LIMIT),
        name="spectrum_sent",
    )(in_hbm(strain), in_hbm(jnp.asarray(table)), in_hbm(listed), in_hbm(bands))


def unit_table(rounds):
    early, late = [], []
    for me in range(Q):
        units = ([], [])
        for i in range(2 * Q):
            for j in range(-Q, Q):
                d = i - j
                if not 0 <= d <= rounds or (i >= Q and j >= 0):
                    continue
                p, q = i % Q ^ me, j % Q ^ me
                target = p if i < Q else 2 * Q + p
                source = q if j >= 0 else Q + q
                far = (i >= Q and p >= Q // 2) or (j < 0 and q >= Q // 2)
                mask = p if i < Q else Q + p
                row = d - 1 if d else rounds
                units[far].append((target, source, d, i, mask, row))
        early.append(units[0])
        late.append(units[1])
    return twins_first(early), twins_first(late)


def twins_first(tables):
    ordered = []
    for units in tables:
        twins, single = [], {}
        for unit in units:
            if unit[2] in single:
                twins.append((single.pop(unit[2]), unit))
            else:
                single[unit[2]] = unit
        ordered.append((twins, list(single.values())))
    count = min(len(twins) for twins, _ in ordered)
    table = []
    for twins, rest in ordered:
        flat = [unit for pair in twins for unit in pair] + rest
        table.append(flat)
    return np.asarray(table, np.int32).reshape(len(tables), -1), count


def run_units(table, me, spec, mask, steering, inv, lag_range, window, unroll, twins):
    channels, angles = steering.shape[2], steering.shape[1]
    cols = spec.shape[2]
    half = cols // 2

    def body(n, carry):
        units = [
            [table[me, (n * unroll + u) * 6 + e] for e in range(6)] for u in range(unroll)
        ]
        beams = []
        for target, source, d, _, _, _ in units:
            near_re, near_im = spec[target, :channels, :half], spec[target, :channels, half:]
            far_re, far_im = spec[source, :channels, :half], spec[source, :channels, half:]
            real = near_re * far_re + near_im * far_im
            imag = near_im * far_re - near_re * far_im
            cross = jnp.concatenate([real, imag], axis=1)
            beams.append(dot(steering[d], cross).astype(jnp.bfloat16))
        beams = dot(jnp.concatenate(beams, axis=0), inv[...])
        masked = []
        for u, (_, _, _, _, target, row) in enumerate(units):
            weight = jnp.concatenate(
                [mask[target, h, pl.ds(row, 1), :] for h in range(L // cols)], axis=1
            )
            masked.append((beams[u * angles : (u + 1) * angles, :] * weight).astype(jnp.bfloat16))
        for u in range(0, 2 * twins, 2):
            part = dot(jnp.concatenate(masked[u : u + 2], axis=0), lag_range[units[u][2]])
            window[units[u][3]] += part[:angles]
            window[units[u + 1][3]] += part[angles:]
        for u in range(2 * twins, unroll):
            window[units[u][3]] += dot(masked[u], lag_range[units[u][2]])
        return carry

    lax.fori_loop(0, table.shape[1] // (6 * unroll), body, 0)


def fill_mask(mask, entry, spec, slot, channels, nbands):
    rounds = mask.shape[2] // 2
    rows = spec[slot, channels:, :].astype(jnp.float32)
    cols = mask.shape[3]
    for j in range(nbands):
        h, lane = divmod(j * (mask.shape[1] * cols // nbands), cols)
        width = mask.shape[1] * cols // nbands
        mask[entry, h, :rounds, lane : lane + width] = jnp.broadcast_to(
            rows[:, j * (cols // nbands) : j * (cols // nbands) + 1], (rounds, width)
        )
    mask[entry, :, rounds:, :] = jnp.ones((mask.shape[1], rounds, cols), jnp.float32)


def neighbour_slots():
    parity = lax.rem(lax.axis_index(AXIS) // Q, 2)
    return Q * (2 - parity), Q * (1 + parity)


def early_kernel(
    nbands, unroll, twins, table, near, mates, even, odd, inv, steering, lag_range, spec, window, mask
):
    me = lax.rem(lax.axis_index(AXIS), Q)
    even_slot, odd_slot = neighbour_slots()
    spec[0:2] = near[...]
    spec[2:4] = mates[...]
    spec[pl.ds(even_slot, 2)] = even[...]
    spec[pl.ds(odd_slot, 2)] = odd[...]
    window[...] = jnp.zeros_like(window)
    channels = steering.shape[2]
    for p in range(Q):
        fill_mask(mask, p, spec, p, channels, nbands)
    for p in range(Q // 2):
        fill_mask(mask, Q + p, spec, 2 * Q + p, channels, nbands)
    run_units(table, me, spec, mask, steering, inv.at[me], lag_range, window, unroll, twins)


def late_kernel(
    nbands, unroll, twins, table, spec_in, window_in, even, odd, inv, steering, lag_range,
    keep, send, spec, window, mask,
):
    me = lax.rem(lax.axis_index(AXIS), Q)
    even_slot, odd_slot = neighbour_slots()
    spec[pl.ds(even_slot + 2, 2)] = even[...]
    spec[pl.ds(odd_slot + 2, 2)] = odd[...]
    channels = steering.shape[2]
    for p in range(Q):
        fill_mask(mask, p, spec, p, channels, nbands)
        fill_mask(mask, Q + p, spec, 2 * Q + p, channels, nbands)
    run_units(table, me, spec, mask, steering, inv.at[me], lag_range, window, unroll, twins)

    width = window.shape[2] // 3

    def segment(s):
        total = None
        for slot, part in ((s, 1), (s - 1, 2), (s + 1, 0)):
            if 0 <= slot < 2 * Q:
                value = window[slot, :, part * width : (part + 1) * width]
                total = value if total is None else total + value
        return total

    core = lax.rem(me, 2)
    here = [segment(s) for s in list(range(Q)) + [2 * Q, -1]]
    there = [segment(Q + p) for p in range(Q)]

    @pl.when(core == 0)
    def _():
        for n, value in enumerate(there):
            keep[n] = value
        for n in range(Q, Q + 2):
            keep[n] = jnp.zeros_like(there[0])
        for n, value in enumerate(here):
            send[n] = value.astype(jnp.bfloat16)

    @pl.when(core == 1)
    def _():
        for n, value in enumerate(here):
            keep[n] = value
        for n, value in enumerate(there):
            send[n] = value.astype(jnp.bfloat16)
        for n in range(Q, Q + 2):
            send[n] = jnp.zeros_like(there[0]).astype(jnp.bfloat16)


def join_kernel(swap, near_in, mates_in, near, mates):
    near[1] = swap[0]
    mates[1] = swap[1]


def core_sum_kernel(kept, received, mine, send):
    side = lax.rem(lax.axis_index(AXIS), Q) // 2

    def total(n):
        return kept[n] + received[n].astype(jnp.float32)

    for n in range(2):
        mine[n] = total(2 * side + n)
        send[n] = total(2 * (1 - side) + n).astype(jnp.bfloat16)
    mine[2] = total(Q + side)
    send[2] = total(Q + 1 - side).astype(jnp.bfloat16)


def plane_sum_kernel(kept, received, mine, send):
    core = lax.rem(lax.axis_index(AXIS), 2)
    totals = [kept[n] + received[n].astype(jnp.float32) for n in range(3)]
    mine[0] = totals[0]
    mine[1] = totals[1]

    @pl.when(core == 0)
    def _():
        send[0] = totals[0].astype(jnp.bfloat16)
        send[1] = totals[1].astype(jnp.bfloat16)

    @pl.when(core == 1)
    def _():
        send[0] = totals[2].astype(jnp.bfloat16)
        send[1] = jnp.zeros_like(totals[2]).astype(jnp.bfloat16)


def end_sum_kernel(kept, received, mine, send):
    me = lax.rem(lax.axis_index(AXIS), Q)
    first = received[0].astype(jnp.float32)
    second = received[1].astype(jnp.float32)
    core, side = lax.rem(me, 2), me // 2

    @pl.when(core == 0)
    def _():
        mine[...] = first
        send[...] = second

    @pl.when((core == 1) & (side == 0))
    def _():
        mine[...] = kept[1]
        send[...] = kept[0] + first

    @pl.when((core == 1) & (side == 1))
    def _():
        mine[...] = kept[1] + first
        send[...] = kept[0]


def image_kernel(kept, received, image):
    image[...] = kept[...] + received[...]


def near_vmem(*values):
    return [pltpu.with_memory_space_constraint(value, pltpu.VMEM) for value in values]


def local_call(kernel, name, outs, *values, aliases={}):
    return pl.pallas_call(
        kernel,
        in_specs=[VMEM_SPEC] * len(values),
        out_specs=[VMEM_SPEC] * len(outs),
        out_shape=outs,
        input_output_aliases=aliases,
        compiler_params=pltpu.CompilerParams(vmem_limit_bytes=LIMIT),
        name=name,
    )(*near_vmem(*values))


def divide(count, most=8):
    return max(n for n in range(1, most + 1) if count % n == 0)


def early_call(plan, nbands, near, mates, even, odd, inv, steering, lag_range):
    _, rows, cols = near.shape
    angles, group = steering.shape[1], lag_range.shape[2]
    rounds = steering.shape[0] - 1
    table, _ = plan
    return pl.pallas_call(
        functools.partial(early_kernel, nbands, divide(table.shape[1] // 6), 0),
        in_specs=[SMEM_SPEC] + [VMEM_SPEC] * 7,
        out_specs=[VMEM_SPEC] * 2,
        out_shape=[
            pltpu.VMEM((3 * Q, rows, cols), jnp.bfloat16),
            pltpu.VMEM((2 * Q, angles, group), jnp.float32),
        ],
        scratch_shapes=[pltpu.VMEM((2 * Q, L // cols, 2 * rounds, cols), jnp.float32)],
        compiler_params=pltpu.CompilerParams(vmem_limit_bytes=LIMIT),
        name="early_pairs",
    )(jnp.asarray(table), *near_vmem(near, mates, even, odd, inv, steering, lag_range))


def late_call(plan, nbands, spec, window, even, odd, inv, steering, lag_range):
    cols = spec.shape[2]
    angles, group = steering.shape[1], lag_range.shape[2]
    rounds = steering.shape[0] - 1
    pieces = (Q + 2, angles, group // 3)
    table, twins = plan
    return pl.pallas_call(
        functools.partial(late_kernel, nbands, table.shape[1] // 6, twins),
        in_specs=[SMEM_SPEC] + [VMEM_SPEC] * 7,
        out_specs=[VMEM_SPEC] * 4,
        out_shape=[
            pltpu.VMEM(pieces, jnp.float32),
            pltpu.VMEM(pieces, jnp.bfloat16),
            pltpu.VMEM(spec.shape, spec.dtype),
            pltpu.VMEM(window.shape, window.dtype),
        ],
        input_output_aliases={1: 2, 2: 3},
        scratch_shapes=[pltpu.VMEM((2 * Q, L // cols, 2 * rounds, cols), jnp.float32)],
        compiler_params=pltpu.CompilerParams(vmem_limit_bytes=LIMIT),
        name="late_pairs",
    )(jnp.asarray(table), *near_vmem(spec, window, even, odd, inv, steering, lag_range))[:2]


def exchange(value, devices, target):
    pairs = [(i, target(i)) for i in range(devices) if target(i) is not None]
    pairs = [(i, j) for i, j in pairs if 0 <= j < devices]
    return lax.ppermute(value, AXIS, pairs)


def per_device(devices, strain, steering, lag_range, pair_listed, band_used):
    def planes(value, parity):
        return exchange(value, devices, lambda i: i + (Q if i // Q % 2 == parity else -Q))

    def flip(value, by):
        return exchange(value, devices, lambda i: i ^ by)

    swap, folds, table = send_call(strain, pair_listed, jnp.transpose(band_used, (0, 2, 1)))
    joined = pltpu.VMEM(swap.shape, swap.dtype)
    near, mates = local_call(keep_kernel, "spectrum_kept", [joined, joined], swap, folds, table)
    near, mates = local_call(
        join_kernel, "join", [joined, joined], flip(swap, 1), near, mates, aliases={1: 0, 2: 1}
    )
    mates = flip(mates, 2)
    near_odd, near_even = planes(near, 1), planes(near, 0)
    far_odd, far_even = planes(mates, 1), planes(mates, 0)
    early, late = unit_table(steering.shape[0] - 1)
    nbands = band_used.shape[2]
    inv = jnp.asarray(inverse_table(strain.shape[1]))
    shared = (inv, steering, lag_range)
    spec, window = early_call(early, nbands, near, mates, near_even, near_odd, *shared)
    kept, send = late_call(late, nbands, spec, window, far_even, far_odd, *shared)

    def pieces(count, dtype):
        return pltpu.VMEM(((count,) if count else ()) + kept.shape[1:], dtype)

    def ends(i):
        if i % 2 == 0:
            return i + Q
        return i + 2 * Q if i % Q < 2 else i - Q

    kept, send = local_call(
        core_sum_kernel,
        "core_sum",
        [pieces(3, jnp.float32), pieces(3, jnp.bfloat16)],
        kept,
        flip(send, 1),
    )
    kept, send = local_call(
        plane_sum_kernel,
        "plane_sum",
        [pieces(2, jnp.float32), pieces(2, jnp.bfloat16)],
        kept,
        flip(send, 2),
    )
    kept, send = local_call(
        end_sum_kernel,
        "end_sum",
        [pieces(0, jnp.float32), pieces(0, jnp.float32)],
        kept,
        exchange(send, devices, ends),
    )
    return local_call(
        image_kernel,
        "image",
        [jax.ShapeDtypeStruct(kept.shape, jnp.float32)],
        kept,
        flip(send, 1),
    )[0]


def solution(mesh):
    return jax.shard_map(
        functools.partial(per_device, mesh.shape[AXIS]),
        mesh=mesh,
        in_specs=(
            P(("win", AXIS), None),
            P(),
            P(),
            P(("win", AXIS), None),
            P(("win", AXIS), None, None),
        ),
        out_specs=P(None, ("win", AXIS)),
        check_vma=False,
    )
```

```python
import functools

import jax
import jax.numpy as jnp
import numpy as np
from jax import lax
from jax.experimental import pallas as pl
from jax.experimental.pallas import tpu as pltpu
from jax.sharding import PartitionSpec as P

AXIS = "fib"
F = 512
L = 512
Q = 4
LIMIT = 16 << 20
VMEM_SPEC = pl.BlockSpec(memory_space=pltpu.VMEM)
SMEM_SPEC = pl.BlockSpec(memory_space=pltpu.SMEM)
HBM_SPEC = pl.BlockSpec(memory_space=pl.ANY)


STEP = 32


def forward_factors(samples):
    m = np.arange(F // Q, dtype=np.int64)
    k = (Q * m[None, :] + np.arange(Q)[:, None] + 1)[:, None, :]
    scale = samples ** (-0.5)
    parts = []
    for step, factor in ((STEP, scale), (1, 1.0)):
        count = samples // Q // STEP if step == STEP else STEP
        t = step * np.arange(count, dtype=np.int64)[None, :, None]
        phase = (t * k % samples) * (2.0 * np.pi / samples)
        parts += [np.cos(phase) * factor, np.sin(phase) * factor]
    table = np.stack(parts)
    return np.stack([table[:, 0::2], table[:, 1::2]]).astype(np.float32)


def inverse_table(samples):
    freqs = F // Q
    k = Q * np.arange(freqs, dtype=np.int64)[None, :, None] + np.arange(Q)[:, None, None] + 1
    lag = np.arange(L, dtype=np.int64)[None, None, :] - L // 2
    theta = (k * lag % samples) * (2.0 * np.pi / samples)
    table = np.concatenate([np.cos(theta), -np.sin(theta)], axis=1) * (2 * F) ** (-0.5)
    return table.astype(jnp.bfloat16)


def in_hbm(value):
    return pltpu.with_memory_space_constraint(value, pltpu.HBM)


def dot(a, b):
    return jnp.dot(a, b, preferred_element_type=jnp.float32)


def combine(a, b):
    half = a.shape[1] // 2
    return jnp.concatenate([a[:, :half] + b[:, half:], a[:, half:] - b[:, :half]], axis=1)


def complex_classes(folds, table):
    channels = folds.shape[1]
    both = folds[...].reshape(2 * channels, folds.shape[2])
    values = []
    for n, sign in ((0, 1.0), (1, -1.0)):
        product = dot(both, table[n])
        values.append(combine(product[:channels], product[channels:] * sign))
    return values


def real_classes(folds, table):
    return [dot(folds[n], table[n]) for n in range(2)]


def fill_table(factors, table):
    half = table.shape[2] // 2
    for n in range(2):
        cos_v, sin_v = factors[2, n], factors[3, n]
        for u in range(factors.shape[2]):
            cos_u, sin_u = factors[0, n, u : u + 1, :], factors[1, n, u : u + 1, :]
            rows = slice(u * STEP, (u + 1) * STEP)
            table[n, rows, :half] = (cos_u * cos_v - sin_u * sin_v).astype(jnp.bfloat16)
            table[n, rows, half:] = (-sin_u * cos_v - cos_u * sin_v).astype(jnp.bfloat16)


def send_kernel(
    strain, factors, listed, bands,
    swap, folds, kept_table,
    time, sent_table, factors_in, listed_in, bands_in, sems,
):
    me = lax.rem(lax.axis_index(AXIS), Q)
    core, side = lax.rem(me, 2), me // 2
    channels, samples = strain.shape
    quarter = samples // Q
    depth = quarter // 2
    small = [
        pltpu.make_async_copy(factors, factors_in, sems.at[2 * Q]),
        pltpu.make_async_copy(listed, listed_in, sems.at[2 * Q + 1]),
        pltpu.make_async_copy(bands, bands_in, sems.at[2 * Q + 2]),
    ]
    copies = []
    for h in range(2):
        for q in range(Q):
            part = (slice(None), pl.ds(q * quarter + h * depth, depth))
            copies.append(
                pltpu.make_async_copy(strain.at[part], time.at[part], sems.at[h * Q + q])
            )
    for copy in small + copies:
        copy.start()
    for copy in small:
        copy.wait()

    fill_table(factors_in.at[1 - core], sent_table)
    nbands = bands.shape[1]
    width = swap.shape[2] // nbands
    rounds = bands.shape[2]
    used = (listed_in[...] * bands_in[0]).astype(jnp.float32)
    pick = lax.broadcasted_iota(jnp.int32, (rounds, rounds), 0) == lax.broadcasted_iota(
        jnp.int32, (rounds, rounds), 1
    )
    weight = jnp.concatenate(
        [
            jnp.broadcast_to(
                jnp.sum(
                    jnp.where(pick, jnp.broadcast_to(used[j : j + 1], (rounds, rounds)), 0.0),
                    axis=1,
                    keepdims=True,
                ),
                (rounds, width),
            )
            for j in range(nbands)
        ],
        axis=1,
    ).astype(jnp.bfloat16)
    for n in range(2):
        swap[n, channels:, :] = weight
    fill_table(factors_in.at[core], kept_table)

    for h in range(2):
        for copy in copies[h * Q : (h + 1) * Q]:
            copy.wait()
        here = pl.ds(h * depth, depth)
        q0, q1, q2, q3 = (time[:, pl.ds(q * quarter + h * depth, depth)] for q in range(Q))
        folds[0, 0, :, here] = q0 - q2
        folds[0, 1, :, here] = q1 - q3
        even = q0.astype(jnp.float32) + q2.astype(jnp.float32)
        odd = q1.astype(jnp.float32) + q3.astype(jnp.float32)
        folds[1, 0, :, here] = (even - odd).astype(jnp.bfloat16)
        folds[1, 1, :, here] = (even + odd).astype(jnp.bfloat16)

    def store(values):
        for n, value in enumerate(values):
            swap[lax.bitwise_xor(side, n), :channels, :] = value.astype(jnp.bfloat16)

    @pl.when(core == 0)
    def _():
        store(real_classes(folds.at[1], sent_table))

    @pl.when(core == 1)
    def _():
        store(complex_classes(folds.at[0], sent_table))


def keep_kernel(swap, folds, table, near, mates):
    me = lax.rem(lax.axis_index(AXIS), Q)
    core, side = lax.rem(me, 2), me // 2
    channels = folds.shape[2]
    near[0, channels:, :] = swap[0, channels:, :]
    mates[0, channels:, :] = swap[0, channels:, :]

    def store(values):
        for n, value in enumerate(values):
            value = value.astype(jnp.bfloat16)

            @pl.when(side == n)
            def _():
                near[0, :channels, :] = value

            @pl.when(side != n)
            def _():
                mates[0, :channels, :] = value

    @pl.when(core == 0)
    def _():
        store(complex_classes(folds.at[0], table))

    @pl.when(core == 1)
    def _():
        store(real_classes(folds.at[1], table))


def send_call(strain, listed, bands):
    channels, samples = strain.shape
    factors = forward_factors(samples)
    rows, cols = channels + bands.shape[2], 2 * factors.shape[4]
    quarter = samples // Q
    return pl.pallas_call(
        send_kernel,
        in_specs=[HBM_SPEC] * 4,
        out_specs=[VMEM_SPEC] * 3,
        out_shape=[
            pltpu.VMEM((2, rows, cols), jnp.bfloat16),
            pltpu.VMEM((2, 2, channels, quarter), jnp.bfloat16),
            pltpu.VMEM((2, quarter, cols), jnp.bfloat16),
        ],
        scratch_shapes=[
            pltpu.VMEM((channels, samples), jnp.bfloat16),
            pltpu.VMEM((2, quarter, cols), jnp.bfloat16),
            pltpu.VMEM(factors.shape, jnp.float32),
            pltpu.VMEM(listed.shape, listed.dtype),
            pltpu.VMEM(bands.shape, bands.dtype),
            pltpu.SemaphoreType.DMA((2 * Q + 3,)),
        ],
        compiler_params=pltpu.CompilerParams(vmem_limit_bytes=LIMIT),
        name="spectrum_sent",
    )(in_hbm(strain), in_hbm(jnp.asarray(factors)), in_hbm(listed), in_hbm(bands))


def unit_table(rounds):
    early, late = [], []
    for me in range(Q):
        units = ([], [])
        for i in range(2 * Q):
            for j in range(-Q, Q):
                d = i - j
                if not 0 <= d <= rounds or (i >= Q and j >= 0):
                    continue
                p, q = i % Q ^ me, j % Q ^ me
                target = p if i < Q else 2 * Q + p
                source = q if j >= 0 else Q + q
                far = (i >= Q and p >= Q // 2) or (j < 0 and q >= Q // 2)
                mask = p if i < Q else Q + p
                row = d - 1 if d else rounds
                units[far].append((target, source, d, i, mask, row))
        early.append(units[0])
        late.append(units[1])
    return twins_first(early), twins_first(late)


def twins_first(tables):
    ordered = []
    for units in tables:
        twins, single = [], {}
        for unit in units:
            if unit[2] in single:
                twins.append((single.pop(unit[2]), unit))
            else:
                single[unit[2]] = unit
        ordered.append((twins, list(single.values())))
    count = min(len(twins) for twins, _ in ordered)
    table = []
    for twins, rest in ordered:
        flat = [unit for pair in twins for unit in pair] + rest
        table.append(flat)
    return np.asarray(table, np.int32).reshape(len(tables), -1), count


def run_units(table, me, spec, mask, steering, inv, lag_range, window, unroll, twins):
    channels, angles = steering.shape[2], steering.shape[1]
    cols = spec.shape[2]
    half = cols // 2

    def body(n, carry):
        units = [
            [table[me, (n * unroll + u) * 6 + e] for e in range(6)] for u in range(unroll)
        ]
        beams = []
        for target, source, d, _, _, _ in units:
            near_re, near_im = spec[target, :channels, :half], spec[target, :channels, half:]
            far_re, far_im = spec[source, :channels, :half], spec[source, :channels, half:]
            real = near_re * far_re + near_im * far_im
            imag = near_im * far_re - near_re * far_im
            cross = jnp.concatenate([real, imag], axis=1)
            beams.append(dot(steering[d], cross).astype(jnp.bfloat16))
        beams = dot(jnp.concatenate(beams, axis=0), inv[...])
        masked = []
        for u, (_, _, _, _, target, row) in enumerate(units):
            weight = jnp.concatenate(
                [mask[target, h, pl.ds(row, 1), :] for h in range(L // cols)], axis=1
            )
            masked.append((beams[u * angles : (u + 1) * angles, :] * weight).astype(jnp.bfloat16))
        for u in range(0, 2 * twins, 2):
            part = dot(jnp.concatenate(masked[u : u + 2], axis=0), lag_range[units[u][2]])
            window[units[u][3]] += part[:angles]
            window[units[u + 1][3]] += part[angles:]
        for u in range(2 * twins, unroll):
            window[units[u][3]] += dot(masked[u], lag_range[units[u][2]])
        return carry

    lax.fori_loop(0, table.shape[1] // (6 * unroll), body, 0)


def fill_mask(mask, entry, spec, slot, channels, nbands):
    rounds = mask.shape[2] // 2
    rows = spec[slot, channels:, :].astype(jnp.float32)
    cols = mask.shape[3]
    for j in range(nbands):
        h, lane = divmod(j * (mask.shape[1] * cols // nbands), cols)
        width = mask.shape[1] * cols // nbands
        mask[entry, h, :rounds, lane : lane + width] = jnp.broadcast_to(
            rows[:, j * (cols // nbands) : j * (cols // nbands) + 1], (rounds, width)
        )
    mask[entry, :, rounds:, :] = jnp.ones((mask.shape[1], rounds, cols), jnp.float32)


def neighbour_slots():
    parity = lax.rem(lax.axis_index(AXIS) // Q, 2)
    return Q * (2 - parity), Q * (1 + parity)


def early_kernel(
    nbands, unroll, twins, table, near, mates, even, odd, inv_all, steering, lag_range,
    spec, window, inv, mask, sem,
):
    me = lax.rem(lax.axis_index(AXIS), Q)
    copy = pltpu.make_async_copy(inv_all.at[me], inv, sem)
    copy.start()
    even_slot, odd_slot = neighbour_slots()
    spec[0:2] = near[...]
    spec[2:4] = mates[...]
    spec[pl.ds(even_slot, 2)] = even[...]
    spec[pl.ds(odd_slot, 2)] = odd[...]
    window[...] = jnp.zeros_like(window)
    channels = steering.shape[2]
    for p in range(Q):
        fill_mask(mask, p, spec, p, channels, nbands)
    for p in range(Q // 2):
        fill_mask(mask, Q + p, spec, 2 * Q + p, channels, nbands)
    copy.wait()
    run_units(table, me, spec, mask, steering, inv, lag_range, window, unroll, twins)


def late_kernel(
    nbands, unroll, twins, table, spec_in, window_in, even, odd, inv, steering, lag_range,
    keep, send, spec, window, mask,
):
    me = lax.rem(lax.axis_index(AXIS), Q)
    even_slot, odd_slot = neighbour_slots()
    spec[pl.ds(even_slot + 2, 2)] = even[...]
    spec[pl.ds(odd_slot + 2, 2)] = odd[...]
    channels = steering.shape[2]
    for p in range(Q):
        fill_mask(mask, p, spec, p, channels, nbands)
        fill_mask(mask, Q + p, spec, 2 * Q + p, channels, nbands)
    run_units(table, me, spec, mask, steering, inv, lag_range, window, unroll, twins)

    width = window.shape[2] // 3

    def segment(s):
        total = None
        for slot, part in ((s, 1), (s - 1, 2), (s + 1, 0)):
            if 0 <= slot < 2 * Q:
                value = window[slot, :, part * width : (part + 1) * width]
                total = value if total is None else total + value
        return total

    core = lax.rem(me, 2)
    here = [segment(s) for s in list(range(Q)) + [2 * Q, -1]]
    there = [segment(Q + p) for p in range(Q)]

    @pl.when(core == 0)
    def _():
        for n, value in enumerate(there):
            keep[n] = value
        for n in range(Q, Q + 2):
            keep[n] = jnp.zeros_like(there[0])
        for n, value in enumerate(here):
            send[n] = value.astype(jnp.bfloat16)

    @pl.when(core == 1)
    def _():
        for n, value in enumerate(here):
            keep[n] = value
        for n, value in enumerate(there):
            send[n] = value.astype(jnp.bfloat16)
        for n in range(Q, Q + 2):
            send[n] = jnp.zeros_like(there[0]).astype(jnp.bfloat16)


def join_kernel(swap, near_in, mates_in, near, mates):
    near[1] = swap[0]
    mates[1] = swap[1]


def core_sum_kernel(kept, received, mine, send):
    side = lax.rem(lax.axis_index(AXIS), Q) // 2

    def total(n):
        return kept[n] + received[n].astype(jnp.float32)

    for n in range(2):
        mine[n] = total(2 * side + n)
        send[n] = total(2 * (1 - side) + n).astype(jnp.bfloat16)
    mine[2] = total(Q + side)
    send[2] = total(Q + 1 - side).astype(jnp.bfloat16)


def plane_sum_kernel(kept, received, mine, send):
    core = lax.rem(lax.axis_index(AXIS), 2)
    totals = [kept[n] + received[n].astype(jnp.float32) for n in range(3)]
    mine[0] = totals[0]
    mine[1] = totals[1]

    @pl.when(core == 0)
    def _():
        send[0] = totals[0].astype(jnp.bfloat16)
        send[1] = totals[1].astype(jnp.bfloat16)

    @pl.when(core == 1)
    def _():
        send[0] = totals[2].astype(jnp.bfloat16)
        send[1] = jnp.zeros_like(totals[2]).astype(jnp.bfloat16)


def end_sum_kernel(kept, received, mine, send):
    me = lax.rem(lax.axis_index(AXIS), Q)
    first = received[0].astype(jnp.float32)
    second = received[1].astype(jnp.float32)
    core, side = lax.rem(me, 2), me // 2

    @pl.when(core == 0)
    def _():
        mine[...] = first
        send[...] = second

    @pl.when((core == 1) & (side == 0))
    def _():
        mine[...] = kept[1]
        send[...] = kept[0] + first

    @pl.when((core == 1) & (side == 1))
    def _():
        mine[...] = kept[1] + first
        send[...] = kept[0]


def image_kernel(kept, received, image):
    image[...] = kept[...] + received[...]


def near_vmem(*values):
    return [pltpu.with_memory_space_constraint(value, pltpu.VMEM) for value in values]


def local_call(kernel, name, outs, *values, aliases={}):
    return pl.pallas_call(
        kernel,
        in_specs=[VMEM_SPEC] * len(values),
        out_specs=[VMEM_SPEC] * len(outs),
        out_shape=outs,
        input_output_aliases=aliases,
        compiler_params=pltpu.CompilerParams(vmem_limit_bytes=LIMIT),
        name=name,
    )(*near_vmem(*values))


def divide(count, most=8):
    return max(n for n in range(1, most + 1) if count % n == 0)


def early_call(plan, nbands, near, mates, even, odd, inv, steering, lag_range):
    _, rows, cols = near.shape
    angles, group = steering.shape[1], lag_range.shape[2]
    rounds = steering.shape[0] - 1
    table, _ = plan
    return pl.pallas_call(
        functools.partial(early_kernel, nbands, divide(table.shape[1] // 6), 0),
        in_specs=[SMEM_SPEC] + [VMEM_SPEC] * 4 + [HBM_SPEC] + [VMEM_SPEC] * 2,
        out_specs=[VMEM_SPEC] * 3,
        out_shape=[
            pltpu.VMEM((3 * Q, rows, cols), jnp.bfloat16),
            pltpu.VMEM((2 * Q, angles, group), jnp.float32),
            pltpu.VMEM(inv.shape[1:], inv.dtype),
        ],
        scratch_shapes=[
            pltpu.VMEM((2 * Q, L // cols, 2 * rounds, cols), jnp.float32),
            pltpu.SemaphoreType.DMA(()),
        ],
        compiler_params=pltpu.CompilerParams(vmem_limit_bytes=LIMIT),
        name="early_pairs",
    )(jnp.asarray(table), *near_vmem(near, mates, even, odd), in_hbm(inv), *near_vmem(steering, lag_range))


def late_call(plan, nbands, spec, window, even, odd, inv, steering, lag_range):
    cols = spec.shape[2]
    angles, group = steering.shape[1], lag_range.shape[2]
    rounds = steering.shape[0] - 1
    pieces = (Q + 2, angles, group // 3)
    table, twins = plan
    return pl.pallas_call(
        functools.partial(late_kernel, nbands, table.shape[1] // 6, twins),
        in_specs=[SMEM_SPEC] + [VMEM_SPEC] * 7,
        out_specs=[VMEM_SPEC] * 4,
        out_shape=[
            pltpu.VMEM(pieces, jnp.float32),
            pltpu.VMEM(pieces, jnp.bfloat16),
            pltpu.VMEM(spec.shape, spec.dtype),
            pltpu.VMEM(window.shape, window.dtype),
        ],
        input_output_aliases={1: 2, 2: 3},
        scratch_shapes=[pltpu.VMEM((2 * Q, L // cols, 2 * rounds, cols), jnp.float32)],
        compiler_params=pltpu.CompilerParams(vmem_limit_bytes=LIMIT),
        name="late_pairs",
    )(jnp.asarray(table), *near_vmem(spec, window, even, odd, inv, steering, lag_range))[:2]


def exchange(value, devices, target):
    pairs = [(i, target(i)) for i in range(devices) if target(i) is not None]
    pairs = [(i, j) for i, j in pairs if 0 <= j < devices]
    return lax.ppermute(value, AXIS, pairs)


def per_device(devices, strain, steering, lag_range, pair_listed, band_used):
    def planes(value, parity):
        return exchange(value, devices, lambda i: i + (Q if i // Q % 2 == parity else -Q))

    def flip(value, by):
        return exchange(value, devices, lambda i: i ^ by)

    swap, folds, table = send_call(strain, pair_listed, jnp.transpose(band_used, (0, 2, 1)))
    joined = pltpu.VMEM(swap.shape, swap.dtype)
    near, mates = local_call(keep_kernel, "spectrum_kept", [joined, joined], swap, folds, table)
    near, mates = local_call(
        join_kernel, "join", [joined, joined], flip(swap, 1), near, mates, aliases={1: 0, 2: 1}
    )
    mates = flip(mates, 2)
    near_odd, near_even = planes(near, 1), planes(near, 0)
    far_odd, far_even = planes(mates, 1), planes(mates, 0)
    early, late = unit_table(steering.shape[0] - 1)
    nbands = band_used.shape[2]
    inv = jnp.asarray(inverse_table(strain.shape[1]))
    spec, window, inv = early_call(
        early, nbands, near, mates, near_even, near_odd, inv, steering, lag_range
    )
    kept, send = late_call(
        late, nbands, spec, window, far_even, far_odd, inv, steering, lag_range
    )

    def pieces(count, dtype):
        return pltpu.VMEM(((count,) if count else ()) + kept.shape[1:], dtype)

    def ends(i):
        if i % 2 == 0:
            return i + Q
        return i + 2 * Q if i % Q < 2 else i - Q

    kept, send = local_call(
        core_sum_kernel,
        "core_sum",
        [pieces(3, jnp.float32), pieces(3, jnp.bfloat16)],
        kept,
        flip(send, 1),
    )
    kept, send = local_call(
        plane_sum_kernel,
        "plane_sum",
        [pieces(2, jnp.float32), pieces(2, jnp.bfloat16)],
        kept,
        flip(send, 2),
    )
    kept, send = local_call(
        end_sum_kernel,
        "end_sum",
        [pieces(0, jnp.float32), pieces(0, jnp.float32)],
        kept,
        exchange(send, devices, ends),
    )
    return local_call(
        image_kernel,
        "image",
        [jax.ShapeDtypeStruct(kept.shape, jnp.float32)],
        kept,
        flip(send, 1),
    )[0]


def solution(mesh):
    return jax.shard_map(
        functools.partial(per_device, mesh.shape[AXIS]),
        mesh=mesh,
        in_specs=(
            P(("win", AXIS), None),
            P(),
            P(),
            P(("win", AXIS), None),
            P(("win", AXIS), None, None),
        ),
        out_specs=P(None, ("win", AXIS)),
        check_vma=False,
    )
```

```python
import functools

import jax
import jax.numpy as jnp
import numpy as np
from jax import lax
from jax.experimental import pallas as pl
from jax.experimental.pallas import tpu as pltpu
from jax.sharding import PartitionSpec as P

AXIS = "fib"
F = 512
L = 512
Q = 4
LIMIT = 16 << 20
VMEM_SPEC = pl.BlockSpec(memory_space=pltpu.VMEM)
HBM_SPEC = pl.BlockSpec(memory_space=pl.ANY)


STEP = 32


def forward_factors(samples):
    m = np.arange(F // Q, dtype=np.int64)
    k = (Q * m[None, :] + np.arange(Q)[:, None] + 1)[:, None, :]
    scale = samples ** (-0.5)
    parts = []
    for step, factor in ((STEP, scale), (1, 1.0)):
        count = samples // Q // STEP if step == STEP else STEP
        t = step * np.arange(count, dtype=np.int64)[None, :, None]
        phase = (t * k % samples) * (2.0 * np.pi / samples)
        parts += [np.cos(phase) * factor, np.sin(phase) * factor]
    table = np.stack(parts)
    return np.stack([table[:, 0::2], table[:, 1::2]]).astype(np.float32)


def inverse_table(samples):
    freqs = F // Q
    k = Q * np.arange(freqs, dtype=np.int64)[None, :, None] + np.arange(Q)[:, None, None] + 1
    lag = np.arange(L, dtype=np.int64)[None, None, :] - L // 2
    theta = (k * lag % samples) * (2.0 * np.pi / samples)
    table = np.concatenate([np.cos(theta), -np.sin(theta)], axis=1) * (2 * F) ** (-0.5)
    return table.astype(jnp.bfloat16)


def in_hbm(value):
    return pltpu.with_memory_space_constraint(value, pltpu.HBM)


def dot(a, b):
    return jnp.dot(a, b, preferred_element_type=jnp.float32)


def combine(a, b):
    half = a.shape[1] // 2
    return jnp.concatenate([a[:, :half] + b[:, half:], a[:, half:] - b[:, :half]], axis=1)


def complex_classes(folds, table):
    channels = folds.shape[1]
    both = folds[...].reshape(2 * channels, folds.shape[2])
    values = []
    for n, sign in ((0, 1.0), (1, -1.0)):
        product = dot(both, table[n])
        values.append(combine(product[:channels], product[channels:] * sign))
    return values


def real_classes(folds, table):
    return [dot(folds[n], table[n]) for n in range(2)]


def fill_table(factors, table):
    half = table.shape[2] // 2
    for n in range(2):
        cos_v, sin_v = factors[2, n], factors[3, n]
        for u in range(factors.shape[2]):
            cos_u, sin_u = factors[0, n, u : u + 1, :], factors[1, n, u : u + 1, :]
            rows = slice(u * STEP, (u + 1) * STEP)
            table[n, rows, :half] = (cos_u * cos_v - sin_u * sin_v).astype(jnp.bfloat16)
            table[n, rows, half:] = (-sin_u * cos_v - cos_u * sin_v).astype(jnp.bfloat16)


def send_kernel(
    strain, factors, listed, bands,
    swap, folds, kept_table,
    time, sent_table, factors_in, listed_in, bands_in, sems,
):
    me = lax.rem(lax.axis_index(AXIS), Q)
    core, side = lax.rem(me, 2), me // 2
    channels, samples = strain.shape
    quarter = samples // Q
    depth = quarter // 2
    small = [
        pltpu.make_async_copy(factors, factors_in, sems.at[2 * Q]),
        pltpu.make_async_copy(listed, listed_in, sems.at[2 * Q + 1]),
        pltpu.make_async_copy(bands, bands_in, sems.at[2 * Q + 2]),
    ]
    copies = []
    for h in range(2):
        for q in range(Q):
            part = (slice(None), pl.ds(q * quarter + h * depth, depth))
            copies.append(
                pltpu.make_async_copy(strain.at[part], time.at[part], sems.at[h * Q + q])
            )
    for copy in small + copies:
        copy.start()
    for copy in small:
        copy.wait()

    fill_table(factors_in.at[1 - core], sent_table)
    nbands = bands.shape[1]
    width = swap.shape[2] // nbands
    rounds = bands.shape[2]
    used = (listed_in[...] * bands_in[0]).astype(jnp.float32)
    pick = lax.broadcasted_iota(jnp.int32, (rounds, rounds), 0) == lax.broadcasted_iota(
        jnp.int32, (rounds, rounds), 1
    )
    weight = jnp.concatenate(
        [
            jnp.broadcast_to(
                jnp.sum(
                    jnp.where(pick, jnp.broadcast_to(used[j : j + 1], (rounds, rounds)), 0.0),
                    axis=1,
                    keepdims=True,
                ),
                (rounds, width),
            )
            for j in range(nbands)
        ],
        axis=1,
    ).astype(jnp.bfloat16)
    for n in range(2):
        swap[n, channels:, :] = weight
    fill_table(factors_in.at[core], kept_table)

    for h in range(2):
        for copy in copies[h * Q : (h + 1) * Q]:
            copy.wait()
        here = pl.ds(h * depth, depth)
        q0, q1, q2, q3 = (time[:, pl.ds(q * quarter + h * depth, depth)] for q in range(Q))
        folds[0, 0, :, here] = q0 - q2
        folds[0, 1, :, here] = q1 - q3
        even = q0.astype(jnp.float32) + q2.astype(jnp.float32)
        odd = q1.astype(jnp.float32) + q3.astype(jnp.float32)
        folds[1, 0, :, here] = (even - odd).astype(jnp.bfloat16)
        folds[1, 1, :, here] = (even + odd).astype(jnp.bfloat16)

    def store(values):
        for n, value in enumerate(values):
            swap[lax.bitwise_xor(side, n), :channels, :] = value.astype(jnp.bfloat16)

    @pl.when(core == 0)
    def _():
        store(real_classes(folds.at[1], sent_table))

    @pl.when(core == 1)
    def _():
        store(complex_classes(folds.at[0], sent_table))


def keep_kernel(swap, folds, table, near, mates):
    me = lax.rem(lax.axis_index(AXIS), Q)
    core, side = lax.rem(me, 2), me // 2
    channels = folds.shape[2]
    near[0, channels:, :] = swap[0, channels:, :]
    mates[0, channels:, :] = swap[0, channels:, :]

    def store(values):
        for n, value in enumerate(values):
            value = value.astype(jnp.bfloat16)

            @pl.when(side == n)
            def _():
                near[0, :channels, :] = value

            @pl.when(side != n)
            def _():
                mates[0, :channels, :] = value

    @pl.when(core == 0)
    def _():
        store(complex_classes(folds.at[0], table))

    @pl.when(core == 1)
    def _():
        store(real_classes(folds.at[1], table))


def send_call(strain, listed, bands):
    channels, samples = strain.shape
    factors = forward_factors(samples)
    rows, cols = channels + bands.shape[2], 2 * factors.shape[4]
    quarter = samples // Q
    return pl.pallas_call(
        send_kernel,
        in_specs=[HBM_SPEC] * 4,
        out_specs=[VMEM_SPEC] * 3,
        out_shape=[
            pltpu.VMEM((2, rows, cols), jnp.bfloat16),
            pltpu.VMEM((2, 2, channels, quarter), jnp.bfloat16),
            pltpu.VMEM((2, quarter, cols), jnp.bfloat16),
        ],
        scratch_shapes=[
            pltpu.VMEM((channels, samples), jnp.bfloat16),
            pltpu.VMEM((2, quarter, cols), jnp.bfloat16),
            pltpu.VMEM(factors.shape, jnp.float32),
            pltpu.VMEM(listed.shape, listed.dtype),
            pltpu.VMEM(bands.shape, bands.dtype),
            pltpu.SemaphoreType.DMA((2 * Q + 3,)),
        ],
        compiler_params=pltpu.CompilerParams(vmem_limit_bytes=LIMIT),
        name="spectrum_sent",
    )(in_hbm(strain), in_hbm(jnp.asarray(factors)), in_hbm(listed), in_hbm(bands))


def make_unit(me, rounds, i, j):
    target_plane, i = i
    source_plane, j = j
    p, q = lax.bitwise_xor(me, i), lax.bitwise_xor(me, j)
    d = (target_plane + source_plane) * Q + i - j
    target = 2 * Q * target_plane + p
    source = Q * source_plane + q
    row = d - 1 if target_plane + source_plane or i != j else rounds
    return target, source, d, target_plane * Q + i, target_plane * Q + p, row


def early_units(me, rounds):
    base = 2 * (me // 2)

    def unit(i, j):
        return make_unit(me, rounds, i, j)

    def own(i, j):
        return unit((0, i), (0, j))

    def low(i, e):
        return unit((0, i), (1, base + e))

    def mid(e, f):
        return unit((1, base + e), (1, base + f))

    twins, rest = [], []
    for d in range(Q):
        group = [own(i, i - d) for i in range(d, Q)]
        twins += [group[n : n + 2] for n in range(0, len(group) // 2 * 2, 2)]
        rest += group[len(group) // 2 * 2 :]
    twins += [[low(i, 0), low(i + 1, 1)] for i in range(Q - 1)]
    twins.append([mid(0, 0), mid(1, 1)])
    rest += [low(Q - 1, 0), low(0, 1), mid(0, 1)]
    return twins, rest


def late_units(me, rounds):
    base = 2 * (1 - me // 2)

    def low(i, e):
        return make_unit(me, rounds, (0, i), (1, base + e))

    def mid(i, j):
        return make_unit(me, rounds, (1, i), (1, j))

    twins = [[low(i, 0), low(i + 1, 1)] for i in range(Q - 1)]
    twins.append([mid(base, base), mid(base + 1, base + 1)])
    twins.append([mid(0, 2), mid(1, 3)])
    twins.append([mid(1, 2), mid(base, base + 1)])
    return twins, [low(Q - 1, 0), low(0, 1), mid(0, 3)]


def run_units(plan, spec, mask, steering, inv, lag_range, window):
    channels, angles = steering.shape[2], steering.shape[1]
    cols = spec.shape[2]
    half = cols // 2
    twins, rest = plan
    units = [unit for pair in twins for unit in pair] + rest
    beams = []
    for target, source, d, _, _, _ in units:
        near_re, near_im = spec[target, :channels, :half], spec[target, :channels, half:]
        far_re, far_im = spec[source, :channels, :half], spec[source, :channels, half:]
        real = near_re * far_re + near_im * far_im
        imag = near_im * far_re - near_re * far_im
        cross = jnp.concatenate([real, imag], axis=1)
        beams.append(dot(steering[d], cross).astype(jnp.bfloat16))
    beams = dot(jnp.concatenate(beams, axis=0), inv[...])
    masked = []
    for u, (_, _, _, _, target, row) in enumerate(units):
        weight = jnp.concatenate(
            [mask[target, h, pl.ds(row, 1), :] for h in range(L // cols)], axis=1
        )
        masked.append((beams[u * angles : (u + 1) * angles, :] * weight).astype(jnp.bfloat16))
    for u in range(0, 2 * len(twins), 2):
        part = dot(jnp.concatenate(masked[u : u + 2], axis=0), lag_range[units[u][2]])
        window[units[u][3]] += part[:angles]
        window[units[u + 1][3]] += part[angles:]
    for u in range(2 * len(twins), len(units)):
        window[units[u][3]] += dot(masked[u], lag_range[units[u][2]])


def fill_mask(mask, entry, spec, slot, channels, nbands):
    rounds = mask.shape[2] // 2
    rows = spec[slot, channels:, :].astype(jnp.float32)
    cols = mask.shape[3]
    for j in range(nbands):
        h, lane = divmod(j * (mask.shape[1] * cols // nbands), cols)
        width = mask.shape[1] * cols // nbands
        mask[entry, h, :rounds, lane : lane + width] = jnp.broadcast_to(
            rows[:, j * (cols // nbands) : j * (cols // nbands) + 1], (rounds, width)
        )
    mask[entry, :, rounds:, :] = jnp.ones((mask.shape[1], rounds, cols), jnp.float32)


def neighbour_slots():
    parity = lax.rem(lax.axis_index(AXIS) // Q, 2)
    return Q * (2 - parity), Q * (1 + parity)


def early_kernel(
    nbands, near, mates, even, odd, inv_all, steering, lag_range,
    spec, window, inv, mask, sem,
):
    me = lax.rem(lax.axis_index(AXIS), Q)
    copy = pltpu.make_async_copy(inv_all.at[me], inv, sem)
    copy.start()
    even_slot, odd_slot = neighbour_slots()
    spec[0:2] = near[...]
    spec[2:4] = mates[...]
    spec[pl.ds(even_slot, 2)] = even[...]
    spec[pl.ds(odd_slot, 2)] = odd[...]
    window[...] = jnp.zeros_like(window)
    channels = steering.shape[2]
    for p in range(Q):
        fill_mask(mask, p, spec, p, channels, nbands)
    for p in range(Q // 2):
        fill_mask(mask, Q + p, spec, 2 * Q + p, channels, nbands)
    copy.wait()
    plan = early_units(me, steering.shape[0] - 1)
    run_units(plan, spec, mask, steering, inv, lag_range, window)


def late_kernel(
    nbands, spec_in, window_in, even, odd, inv, steering, lag_range,
    keep, send, spec, window, mask,
):
    me = lax.rem(lax.axis_index(AXIS), Q)
    even_slot, odd_slot = neighbour_slots()
    spec[pl.ds(even_slot + 2, 2)] = even[...]
    spec[pl.ds(odd_slot + 2, 2)] = odd[...]
    channels = steering.shape[2]
    for p in range(Q):
        fill_mask(mask, p, spec, p, channels, nbands)
        fill_mask(mask, Q + p, spec, 2 * Q + p, channels, nbands)
    plan = late_units(me, steering.shape[0] - 1)
    run_units(plan, spec, mask, steering, inv, lag_range, window)

    width = window.shape[2] // 3

    def segment(s):
        total = None
        for slot, part in ((s, 1), (s - 1, 2), (s + 1, 0)):
            if 0 <= slot < 2 * Q:
                value = window[slot, :, part * width : (part + 1) * width]
                total = value if total is None else total + value
        return total

    core = lax.rem(me, 2)
    here = [segment(s) for s in list(range(Q)) + [2 * Q, -1]]
    there = [segment(Q + p) for p in range(Q)]

    @pl.when(core == 0)
    def _():
        for n, value in enumerate(there):
            keep[n] = value
        for n in range(Q, Q + 2):
            keep[n] = jnp.zeros_like(there[0])
        for n, value in enumerate(here):
            send[n] = value.astype(jnp.bfloat16)

    @pl.when(core == 1)
    def _():
        for n, value in enumerate(here):
            keep[n] = value
        for n, value in enumerate(there):
            send[n] = value.astype(jnp.bfloat16)
        for n in range(Q, Q + 2):
            send[n] = jnp.zeros_like(there[0]).astype(jnp.bfloat16)


def join_kernel(swap, near_in, mates_in, near, mates):
    near[1] = swap[0]
    mates[1] = swap[1]


def core_sum_kernel(kept, received, mine, send):
    side = lax.rem(lax.axis_index(AXIS), Q) // 2

    def total(n):
        return kept[n] + received[n].astype(jnp.float32)

    for n in range(2):
        mine[n] = total(2 * side + n)
        send[n] = total(2 * (1 - side) + n).astype(jnp.bfloat16)
    mine[2] = total(Q + side)
    send[2] = total(Q + 1 - side).astype(jnp.bfloat16)


def plane_sum_kernel(kept, received, mine, send):
    core = lax.rem(lax.axis_index(AXIS), 2)
    totals = [kept[n] + received[n].astype(jnp.float32) for n in range(3)]
    mine[0] = totals[0]
    mine[1] = totals[1]

    @pl.when(core == 0)
    def _():
        send[0] = totals[0].astype(jnp.bfloat16)
        send[1] = totals[1].astype(jnp.bfloat16)

    @pl.when(core == 1)
    def _():
        send[0] = totals[2].astype(jnp.bfloat16)
        send[1] = jnp.zeros_like(totals[2]).astype(jnp.bfloat16)


def end_sum_kernel(kept, received, mine, send):
    me = lax.rem(lax.axis_index(AXIS), Q)
    first = received[0].astype(jnp.float32)
    second = received[1].astype(jnp.float32)
    core, side = lax.rem(me, 2), me // 2

    @pl.when(core == 0)
    def _():
        mine[...] = first
        send[...] = second

    @pl.when((core == 1) & (side == 0))
    def _():
        mine[...] = kept[1]
        send[...] = kept[0] + first

    @pl.when((core == 1) & (side == 1))
    def _():
        mine[...] = kept[1] + first
        send[...] = kept[0]


def image_kernel(kept, received, image):
    image[...] = kept[...] + received[...]


def near_vmem(*values):
    return [pltpu.with_memory_space_constraint(value, pltpu.VMEM) for value in values]


def local_call(kernel, name, outs, *values, aliases={}):
    return pl.pallas_call(
        kernel,
        in_specs=[VMEM_SPEC] * len(values),
        out_specs=[VMEM_SPEC] * len(outs),
        out_shape=outs,
        input_output_aliases=aliases,
        compiler_params=pltpu.CompilerParams(vmem_limit_bytes=LIMIT),
        name=name,
    )(*near_vmem(*values))


def early_call(nbands, near, mates, even, odd, inv, steering, lag_range):
    _, rows, cols = near.shape
    angles, group = steering.shape[1], lag_range.shape[2]
    rounds = steering.shape[0] - 1
    return pl.pallas_call(
        functools.partial(early_kernel, nbands),
        in_specs=[VMEM_SPEC] * 4 + [HBM_SPEC] + [VMEM_SPEC] * 2,
        out_specs=[VMEM_SPEC] * 3,
        out_shape=[
            pltpu.VMEM((3 * Q, rows, cols), jnp.bfloat16),
            pltpu.VMEM((2 * Q, angles, group), jnp.float32),
            pltpu.VMEM(inv.shape[1:], inv.dtype),
        ],
        scratch_shapes=[
            pltpu.VMEM((2 * Q, L // cols, 2 * rounds, cols), jnp.float32),
            pltpu.SemaphoreType.DMA(()),
        ],
        compiler_params=pltpu.CompilerParams(vmem_limit_bytes=LIMIT),
        name="early_pairs",
    )(*near_vmem(near, mates, even, odd), in_hbm(inv), *near_vmem(steering, lag_range))


def late_call(nbands, spec, window, even, odd, inv, steering, lag_range):
    cols = spec.shape[2]
    angles, group = steering.shape[1], lag_range.shape[2]
    rounds = steering.shape[0] - 1
    pieces = (Q + 2, angles, group // 3)
    return pl.pallas_call(
        functools.partial(late_kernel, nbands),
        in_specs=[VMEM_SPEC] * 7,
        out_specs=[VMEM_SPEC] * 4,
        out_shape=[
            pltpu.VMEM(pieces, jnp.float32),
            pltpu.VMEM(pieces, jnp.bfloat16),
            pltpu.VMEM(spec.shape, spec.dtype),
            pltpu.VMEM(window.shape, window.dtype),
        ],
        input_output_aliases={0: 2, 1: 3},
        scratch_shapes=[pltpu.VMEM((2 * Q, L // cols, 2 * rounds, cols), jnp.float32)],
        compiler_params=pltpu.CompilerParams(vmem_limit_bytes=LIMIT),
        name="late_pairs",
    )(*near_vmem(spec, window, even, odd, inv, steering, lag_range))[:2]


def exchange(value, devices, target):
    pairs = [(i, target(i)) for i in range(devices) if target(i) is not None]
    pairs = [(i, j) for i, j in pairs if 0 <= j < devices]
    return lax.ppermute(value, AXIS, pairs)


def per_device(devices, strain, steering, lag_range, pair_listed, band_used):
    def planes(value, parity):
        return exchange(value, devices, lambda i: i + (Q if i // Q % 2 == parity else -Q))

    def flip(value, by):
        return exchange(value, devices, lambda i: i ^ by)

    swap, folds, table = send_call(strain, pair_listed, jnp.transpose(band_used, (0, 2, 1)))
    joined = pltpu.VMEM(swap.shape, swap.dtype)
    near, mates = local_call(keep_kernel, "spectrum_kept", [joined, joined], swap, folds, table)
    near, mates = local_call(
        join_kernel, "join", [joined, joined], flip(swap, 1), near, mates, aliases={1: 0, 2: 1}
    )
    mates = flip(mates, 2)
    near_odd, near_even = planes(near, 1), planes(near, 0)
    far_odd, far_even = planes(mates, 1), planes(mates, 0)
    nbands = band_used.shape[2]
    inv = jnp.asarray(inverse_table(strain.shape[1]))
    spec, window, inv = early_call(
        nbands, near, mates, near_even, near_odd, inv, steering, lag_range
    )
    kept, send = late_call(
        nbands, spec, window, far_even, far_odd, inv, steering, lag_range
    )

    def pieces(count, dtype):
        return pltpu.VMEM(((count,) if count else ()) + kept.shape[1:], dtype)

    def ends(i):
        if i % 2 == 0:
            return i + Q
        return i + 2 * Q if i % Q < 2 else i - Q

    kept, send = local_call(
        core_sum_kernel,
        "core_sum",
        [pieces(3, jnp.float32), pieces(3, jnp.bfloat16)],
        kept,
        flip(send, 1),
    )
    kept, send = local_call(
        plane_sum_kernel,
        "plane_sum",
        [pieces(2, jnp.float32), pieces(2, jnp.bfloat16)],
        kept,
        flip(send, 2),
    )
    kept, send = local_call(
        end_sum_kernel,
        "end_sum",
        [pieces(0, jnp.float32), pieces(0, jnp.float32)],
        kept,
        exchange(send, devices, ends),
    )
    return local_call(
        image_kernel,
        "image",
        [jax.ShapeDtypeStruct(kept.shape, jnp.float32)],
        kept,
        flip(send, 1),
    )[0]


def solution(mesh):
    return jax.shard_map(
        functools.partial(per_device, mesh.shape[AXIS]),
        mesh=mesh,
        in_specs=(
            P(("win", AXIS), None),
            P(),
            P(),
            P(("win", AXIS), None),
            P(("win", AXIS), None, None),
        ),
        out_specs=P(None, ("win", AXIS)),
        check_vma=False,
    )
```

```python
import functools

import jax
import jax.numpy as jnp
import numpy as np
from jax import lax
from jax.experimental import pallas as pl
from jax.experimental.pallas import tpu as pltpu
from jax.sharding import PartitionSpec as P

AXIS = "fib"
F = 512
L = 512
Q = 4
LIMIT = 16 << 20
VMEM_SPEC = pl.BlockSpec(memory_space=pltpu.VMEM)
HBM_SPEC = pl.BlockSpec(memory_space=pl.ANY)


STEP = 32


def forward_factors(samples):
    m = np.arange(F // Q, dtype=np.int64)
    k = (Q * m[None, :] + np.arange(Q)[:, None] + 1)[:, None, :]
    scale = samples ** (-0.5)
    parts = []
    for step, factor in ((STEP, scale), (1, 1.0)):
        count = samples // Q // STEP if step == STEP else STEP
        t = step * np.arange(count, dtype=np.int64)[None, :, None]
        phase = (t * k % samples) * (2.0 * np.pi / samples)
        parts += [np.cos(phase) * factor, np.sin(phase) * factor]
    table = np.stack(parts)
    return np.stack([table[:, 0::2], table[:, 1::2]]).astype(np.float32)


def inverse_table(samples):
    freqs = F // Q
    k = Q * np.arange(freqs, dtype=np.int64)[None, :, None] + np.arange(Q)[:, None, None] + 1
    lag = np.arange(L, dtype=np.int64)[None, None, :] - L // 2
    theta = (k * lag % samples) * (2.0 * np.pi / samples)
    table = np.concatenate([np.cos(theta), -np.sin(theta)], axis=1) * (2 * F) ** (-0.5)
    return table.astype(jnp.bfloat16)


def in_hbm(value):
    return pltpu.with_memory_space_constraint(value, pltpu.HBM)


def dot(a, b):
    return jnp.dot(a, b, preferred_element_type=jnp.float32)


def combine(a, b):
    half = a.shape[1] // 2
    return jnp.concatenate([a[:, :half] + b[:, half:], a[:, half:] - b[:, :half]], axis=1)


def complex_classes(folds, table):
    channels = folds.shape[1]
    both = folds[...].reshape(2 * channels, folds.shape[2])
    values = []
    for n, sign in ((0, 1.0), (1, -1.0)):
        product = dot(both, table[n])
        values.append(combine(product[:channels], product[channels:] * sign))
    return values


def real_classes(folds, table):
    return [dot(folds[n], table[n]) for n in range(2)]


def fill_table(factors, table):
    half = table.shape[2] // 2
    for n in range(2):
        cos_v, sin_v = factors[2, n], factors[3, n]
        for u in range(factors.shape[2]):
            cos_u, sin_u = factors[0, n, u : u + 1, :], factors[1, n, u : u + 1, :]
            rows = slice(u * STEP, (u + 1) * STEP)
            table[n, rows, :half] = (cos_u * cos_v - sin_u * sin_v).astype(jnp.bfloat16)
            table[n, rows, half:] = (-sin_u * cos_v - cos_u * sin_v).astype(jnp.bfloat16)


def send_kernel(
    strain, factors, listed, bands,
    swap, folds, kept_table,
    time, sent_table, factors_in, listed_in, bands_in, sems,
):
    me = lax.rem(lax.axis_index(AXIS), Q)
    core, side = lax.rem(me, 2), me // 2
    channels, samples = strain.shape
    quarter = samples // Q
    depth = quarter // 2
    small = [
        pltpu.make_async_copy(factors, factors_in, sems.at[2 * Q]),
        pltpu.make_async_copy(listed, listed_in, sems.at[2 * Q + 1]),
        pltpu.make_async_copy(bands, bands_in, sems.at[2 * Q + 2]),
    ]
    copies = []
    for h in range(2):
        for q in range(Q):
            part = (slice(None), pl.ds(q * quarter + h * depth, depth))
            copies.append(
                pltpu.make_async_copy(strain.at[part], time.at[part], sems.at[h * Q + q])
            )
    for copy in small + copies:
        copy.start()
    for copy in small:
        copy.wait()

    fill_table(factors_in.at[1 - core], sent_table)
    nbands = bands.shape[1]
    width = swap.shape[2] // nbands
    rounds = bands.shape[2]
    used = (listed_in[...] * bands_in[0]).astype(jnp.float32)
    pick = lax.broadcasted_iota(jnp.int32, (rounds, rounds), 0) == lax.broadcasted_iota(
        jnp.int32, (rounds, rounds), 1
    )
    weight = jnp.concatenate(
        [
            jnp.broadcast_to(
                jnp.sum(
                    jnp.where(pick, jnp.broadcast_to(used[j : j + 1], (rounds, rounds)), 0.0),
                    axis=1,
                    keepdims=True,
                ),
                (rounds, width),
            )
            for j in range(nbands)
        ],
        axis=1,
    ).astype(jnp.bfloat16)
    for n in range(2):
        swap[n, channels:, :] = weight
    fill_table(factors_in.at[core], kept_table)

    for h in range(2):
        for copy in copies[h * Q : (h + 1) * Q]:
            copy.wait()
        here = pl.ds(h * depth, depth)
        q0, q1, q2, q3 = (time[:, pl.ds(q * quarter + h * depth, depth)] for q in range(Q))
        folds[0, 0, :, here] = q0 - q2
        folds[0, 1, :, here] = q1 - q3
        even = q0.astype(jnp.float32) + q2.astype(jnp.float32)
        odd = q1.astype(jnp.float32) + q3.astype(jnp.float32)
        folds[1, 0, :, here] = (even - odd).astype(jnp.bfloat16)
        folds[1, 1, :, here] = (even + odd).astype(jnp.bfloat16)

    def store(values):
        for n, value in enumerate(values):
            swap[lax.bitwise_xor(side, n), :channels, :] = value.astype(jnp.bfloat16)

    @pl.when(core == 0)
    def _():
        store(real_classes(folds.at[1], sent_table))

    @pl.when(core == 1)
    def _():
        store(complex_classes(folds.at[0], sent_table))


def keep_kernel(swap, folds, table, near, mates):
    me = lax.rem(lax.axis_index(AXIS), Q)
    core, side = lax.rem(me, 2), me // 2
    channels = folds.shape[2]
    near[0, channels:, :] = swap[0, channels:, :]
    mates[0, channels:, :] = swap[0, channels:, :]

    def store(values):
        for n, value in enumerate(values):
            value = value.astype(jnp.bfloat16)

            @pl.when(side == n)
            def _():
                near[0, :channels, :] = value

            @pl.when(side != n)
            def _():
                mates[0, :channels, :] = value

    @pl.when(core == 0)
    def _():
        store(complex_classes(folds.at[0], table))

    @pl.when(core == 1)
    def _():
        store(real_classes(folds.at[1], table))


def send_call(strain, listed, bands):
    channels, samples = strain.shape
    factors = forward_factors(samples)
    rows, cols = channels + bands.shape[2], 2 * factors.shape[4]
    quarter = samples // Q
    return pl.pallas_call(
        send_kernel,
        in_specs=[HBM_SPEC] * 4,
        out_specs=[VMEM_SPEC] * 3,
        out_shape=[
            pltpu.VMEM((2, rows, cols), jnp.bfloat16),
            pltpu.VMEM((2, 2, channels, quarter), jnp.bfloat16),
            pltpu.VMEM((2, quarter, cols), jnp.bfloat16),
        ],
        scratch_shapes=[
            pltpu.VMEM((channels, samples), jnp.bfloat16),
            pltpu.VMEM((2, quarter, cols), jnp.bfloat16),
            pltpu.VMEM(factors.shape, jnp.float32),
            pltpu.VMEM(listed.shape, listed.dtype),
            pltpu.VMEM(bands.shape, bands.dtype),
            pltpu.SemaphoreType.DMA((2 * Q + 3,)),
        ],
        compiler_params=pltpu.CompilerParams(vmem_limit_bytes=LIMIT),
        name="spectrum_sent",
    )(in_hbm(strain), in_hbm(jnp.asarray(factors)), in_hbm(listed), in_hbm(bands))


def make_unit(me, rounds, i, j):
    target_plane, i = i
    source_plane, j = j
    p, q = lax.bitwise_xor(me, i), lax.bitwise_xor(me, j)
    d = (target_plane + source_plane) * Q + i - j
    target = 2 * Q * target_plane + p
    source = Q * source_plane + q
    row = d - 1 if target_plane + source_plane or i != j else rounds
    return target, source, d, target_plane * Q + i, target_plane * Q + p, row


def early_units(me, rounds):
    base = 2 * (me // 2)

    def unit(i, j):
        return make_unit(me, rounds, i, j)

    def own(i, j):
        return unit((0, i), (0, j))

    def low(i, e):
        return unit((0, i), (1, base + e))

    def mid(e, f):
        return unit((1, base + e), (1, base + f))

    twins, rest = [], []
    for d in range(Q):
        group = [own(i, i - d) for i in range(d, Q)]
        twins += [group[n : n + 2] for n in range(0, len(group) // 2 * 2, 2)]
        rest += group[len(group) // 2 * 2 :]
    twins += [[low(i, 0), low(i + 1, 1)] for i in range(Q - 1)]
    twins.append([mid(0, 0), mid(1, 1)])
    rest += [low(Q - 1, 0), low(0, 1), mid(0, 1)]
    return twins, rest


def late_units(me, rounds):
    base = 2 * (1 - me // 2)

    def low(i, e):
        return make_unit(me, rounds, (0, i), (1, base + e))

    def mid(i, j):
        return make_unit(me, rounds, (1, i), (1, j))

    twins = [[low(i, 0), low(i + 1, 1)] for i in range(Q - 1)]
    twins.append([mid(base, base), mid(base + 1, base + 1)])
    twins.append([mid(0, 2), mid(1, 3)])
    twins.append([mid(1, 2), mid(base, base + 1)])
    return twins, [low(Q - 1, 0), low(0, 1), mid(0, 3)]


def run_units(plan, spec, mask, steering, inv, lag_range, window):
    channels, angles = steering.shape[2], steering.shape[1]
    cols = spec.shape[2]
    half = cols // 2
    twins, rest = plan
    units = [unit for pair in twins for unit in pair] + rest
    beams = []
    for target, source, d, _, _, _ in units:
        near_re, near_im = spec[target, :channels, :half], spec[target, :channels, half:]
        far_re, far_im = spec[source, :channels, :half], spec[source, :channels, half:]
        real = near_re * far_re + near_im * far_im
        imag = near_im * far_re - near_re * far_im
        cross = jnp.concatenate([real, imag], axis=1)
        beams.append(dot(steering[d], cross).astype(jnp.bfloat16))
    beams = dot(jnp.concatenate(beams, axis=0), inv[...])
    masked = []
    for u, (_, _, _, _, target, row) in enumerate(units):
        weight = jnp.concatenate(
            [mask[target, h, pl.ds(row, 1), :] for h in range(L // cols)], axis=1
        )
        masked.append((beams[u * angles : (u + 1) * angles, :] * weight).astype(jnp.bfloat16))
    for u in range(0, 2 * len(twins), 2):
        part = dot(jnp.concatenate(masked[u : u + 2], axis=0), lag_range[units[u][2]])
        window[units[u][3]] += part[:angles]
        window[units[u + 1][3]] += part[angles:]
    for u in range(2 * len(twins), len(units)):
        window[units[u][3]] += dot(masked[u], lag_range[units[u][2]])


def fill_mask(mask, entry, spec, slot, channels, nbands):
    rounds = mask.shape[2] // 2
    rows = spec[slot, channels:, :].astype(jnp.float32)
    cols = mask.shape[3]
    for j in range(nbands):
        h, lane = divmod(j * (mask.shape[1] * cols // nbands), cols)
        width = mask.shape[1] * cols // nbands
        mask[entry, h, :rounds, lane : lane + width] = jnp.broadcast_to(
            rows[:, j * (cols // nbands) : j * (cols // nbands) + 1], (rounds, width)
        )
    mask[entry, :, rounds:, :] = jnp.ones((mask.shape[1], rounds, cols), jnp.float32)


def neighbour_slots():
    parity = lax.rem(lax.axis_index(AXIS) // Q, 2)
    return Q * (2 - parity), Q * (1 + parity)


def early_kernel(
    nbands, near, mates, even, odd, inv_all, steering, lag_range,
    spec, window, inv, mask, sem,
):
    me = lax.rem(lax.axis_index(AXIS), Q)
    copy = pltpu.make_async_copy(inv_all.at[me], inv, sem)
    copy.start()
    even_slot, odd_slot = neighbour_slots()
    spec[0:2] = near[...]
    spec[2:4] = mates[...]
    spec[pl.ds(even_slot, 2)] = even[...]
    spec[pl.ds(odd_slot, 2)] = odd[...]
    window[...] = jnp.zeros_like(window)
    channels = steering.shape[2]
    for p in range(Q):
        fill_mask(mask, p, spec, p, channels, nbands)
    for p in range(Q // 2):
        fill_mask(mask, Q + p, spec, 2 * Q + p, channels, nbands)
    copy.wait()
    plan = early_units(me, steering.shape[0] - 1)
    run_units(plan, spec, mask, steering, inv, lag_range, window)


def late_kernel(
    nbands, spec_in, window_in, even, odd, inv, steering, lag_range,
    keep, send, spec, window, mask,
):
    me = lax.rem(lax.axis_index(AXIS), Q)
    even_slot, odd_slot = neighbour_slots()
    spec[pl.ds(even_slot + 2, 2)] = even[...]
    spec[pl.ds(odd_slot + 2, 2)] = odd[...]
    channels = steering.shape[2]
    for p in range(Q):
        fill_mask(mask, p, spec, p, channels, nbands)
        fill_mask(mask, Q + p, spec, 2 * Q + p, channels, nbands)
    plan = late_units(me, steering.shape[0] - 1)
    run_units(plan, spec, mask, steering, inv, lag_range, window)

    width = window.shape[2] // 3

    def segment(s):
        total = None
        for slot, part in ((s, 1), (s - 1, 2), (s + 1, 0)):
            if 0 <= slot < 2 * Q:
                value = window[slot, :, part * width : (part + 1) * width]
                total = value if total is None else total + value
        return total

    core = lax.rem(me, 2)
    here = [segment(s) for s in list(range(Q)) + [2 * Q, -1]]
    there = [segment(Q + p) for p in range(Q)]

    @pl.when(core == 0)
    def _():
        for n, value in enumerate(there):
            keep[n] = value
        for n in range(Q, Q + 2):
            keep[n] = jnp.zeros_like(there[0])
        for n, value in enumerate(here):
            send[n] = value.astype(jnp.bfloat16)

    @pl.when(core == 1)
    def _():
        for n, value in enumerate(here):
            keep[n] = value
        for n, value in enumerate(there):
            send[n] = value.astype(jnp.bfloat16)
        for n in range(Q, Q + 2):
            send[n] = jnp.zeros_like(there[0]).astype(jnp.bfloat16)


def join_kernel(swap, near_in, mates_in, near, mates):
    near[1] = swap[0]
    mates[1] = swap[1]


def core_sum_kernel(kept, received, mine, send):
    me = lax.rem(lax.axis_index(AXIS), Q)
    core, side = lax.rem(me, 2), me // 2

    def total(n):
        return kept[n] + received[n].astype(jnp.float32)

    @pl.when(core == 0)
    def _():
        for n in range(Q):
            send[n] = total(n).astype(jnp.bfloat16)
        mine[...] = jnp.zeros_like(mine)

    @pl.when(core == 1)
    def _():
        for n in range(2):
            mine[n] = total(2 * side + n)
            send[n] = total(2 * (1 - side) + n).astype(jnp.bfloat16)
        mine[2] = total(Q + side)
        send[2] = total(Q + 1 - side).astype(jnp.bfloat16)
        send[3] = jnp.zeros_like(send[2])


def plane_sum_kernel(kept, received, mine, send):
    me = lax.rem(lax.axis_index(AXIS), Q)
    core, side = lax.rem(me, 2), me // 2

    @pl.when(core == 0)
    def _():
        for n in range(2):
            mine[n] = received[2 * side + n].astype(jnp.float32)
            send[n] = received[2 * (1 - side) + n]

    @pl.when(core == 1)
    def _():
        for n in range(2):
            mine[n] = kept[n] + received[n].astype(jnp.float32)
        send[0] = (kept[2] + received[2].astype(jnp.float32)).astype(jnp.bfloat16)
        send[1] = jnp.zeros_like(send[0])


def end_sum_kernel(kept, received, mine, send):
    me = lax.rem(lax.axis_index(AXIS), Q)
    first = received[0].astype(jnp.float32)
    second = received[1].astype(jnp.float32)
    core, side = lax.rem(me, 2), me // 2

    @pl.when(core == 0)
    def _():
        mine[...] = kept[0] + first
        send[...] = kept[1] + second

    @pl.when((core == 1) & (side == 0))
    def _():
        mine[...] = kept[1]
        send[...] = kept[0] + first

    @pl.when((core == 1) & (side == 1))
    def _():
        mine[...] = kept[1] + first
        send[...] = kept[0]


def image_kernel(kept, received, image):
    image[...] = kept[...] + received[...]


def near_vmem(*values):
    return [pltpu.with_memory_space_constraint(value, pltpu.VMEM) for value in values]


def local_call(kernel, name, outs, *values, aliases={}):
    return pl.pallas_call(
        kernel,
        in_specs=[VMEM_SPEC] * len(values),
        out_specs=[VMEM_SPEC] * len(outs),
        out_shape=outs,
        input_output_aliases=aliases,
        compiler_params=pltpu.CompilerParams(vmem_limit_bytes=LIMIT),
        name=name,
    )(*near_vmem(*values))


def early_call(nbands, near, mates, even, odd, inv, steering, lag_range):
    _, rows, cols = near.shape
    angles, group = steering.shape[1], lag_range.shape[2]
    rounds = steering.shape[0] - 1
    return pl.pallas_call(
        functools.partial(early_kernel, nbands),
        in_specs=[VMEM_SPEC] * 4 + [HBM_SPEC] + [VMEM_SPEC] * 2,
        out_specs=[VMEM_SPEC] * 3,
        out_shape=[
            pltpu.VMEM((3 * Q, rows, cols), jnp.bfloat16),
            pltpu.VMEM((2 * Q, angles, group), jnp.float32),
            pltpu.VMEM(inv.shape[1:], inv.dtype),
        ],
        scratch_shapes=[
            pltpu.VMEM((2 * Q, L // cols, 2 * rounds, cols), jnp.float32),
            pltpu.SemaphoreType.DMA(()),
        ],
        compiler_params=pltpu.CompilerParams(vmem_limit_bytes=LIMIT),
        name="early_pairs",
    )(*near_vmem(near, mates, even, odd), in_hbm(inv), *near_vmem(steering, lag_range))


def late_call(nbands, spec, window, even, odd, inv, steering, lag_range):
    cols = spec.shape[2]
    angles, group = steering.shape[1], lag_range.shape[2]
    rounds = steering.shape[0] - 1
    pieces = (Q + 2, angles, group // 3)
    return pl.pallas_call(
        functools.partial(late_kernel, nbands),
        in_specs=[VMEM_SPEC] * 7,
        out_specs=[VMEM_SPEC] * 4,
        out_shape=[
            pltpu.VMEM(pieces, jnp.float32),
            pltpu.VMEM(pieces, jnp.bfloat16),
            pltpu.VMEM(spec.shape, spec.dtype),
            pltpu.VMEM(window.shape, window.dtype),
        ],
        input_output_aliases={0: 2, 1: 3},
        scratch_shapes=[pltpu.VMEM((2 * Q, L // cols, 2 * rounds, cols), jnp.float32)],
        compiler_params=pltpu.CompilerParams(vmem_limit_bytes=LIMIT),
        name="late_pairs",
    )(*near_vmem(spec, window, even, odd, inv, steering, lag_range))[:2]


def exchange(value, devices, target):
    pairs = [(i, target(i)) for i in range(devices) if target(i) is not None]
    pairs = [(i, j) for i, j in pairs if 0 <= j < devices]
    return lax.ppermute(value, AXIS, pairs)


def per_device(devices, strain, steering, lag_range, pair_listed, band_used):
    def planes(value, parity):
        return exchange(value, devices, lambda i: i + (Q if i // Q % 2 == parity else -Q))

    def flip(value, by):
        return exchange(value, devices, lambda i: i ^ by)

    swap, folds, table = send_call(strain, pair_listed, jnp.transpose(band_used, (0, 2, 1)))
    joined = pltpu.VMEM(swap.shape, swap.dtype)
    near, mates = local_call(keep_kernel, "spectrum_kept", [joined, joined], swap, folds, table)
    near, mates = local_call(
        join_kernel, "join", [joined, joined], flip(swap, 1), near, mates, aliases={1: 0, 2: 1}
    )
    mates = flip(mates, 2)
    near_odd, near_even = planes(near, 1), planes(near, 0)
    far_odd, far_even = planes(mates, 1), planes(mates, 0)
    nbands = band_used.shape[2]
    inv = jnp.asarray(inverse_table(strain.shape[1]))
    spec, window, inv = early_call(
        nbands, near, mates, near_even, near_odd, inv, steering, lag_range
    )
    kept, send = late_call(
        nbands, spec, window, far_even, far_odd, inv, steering, lag_range
    )

    def pieces(count, dtype):
        return pltpu.VMEM(((count,) if count else ()) + kept.shape[1:], dtype)

    def first(i):
        return i + Q if i % 2 == 0 else i ^ 2

    def second(i):
        if i % 2 == 0:
            return i ^ 2
        return i + 2 * Q if i % Q < 2 else i - Q

    kept, send = local_call(
        core_sum_kernel,
        "core_sum",
        [pieces(3, jnp.float32), pieces(Q, jnp.bfloat16)],
        kept,
        flip(send, 1),
    )
    kept, send = local_call(
        plane_sum_kernel,
        "plane_sum",
        [pieces(2, jnp.float32), pieces(2, jnp.bfloat16)],
        kept,
        exchange(send, devices, first),
    )
    kept, send = local_call(
        end_sum_kernel,
        "end_sum",
        [pieces(0, jnp.float32), pieces(0, jnp.float32)],
        kept,
        exchange(send, devices, second),
    )
    return local_call(
        image_kernel,
        "image",
        [jax.ShapeDtypeStruct(kept.shape, jnp.float32)],
        kept,
        flip(send, 1),
    )[0]


def solution(mesh):
    return jax.shard_map(
        functools.partial(per_device, mesh.shape[AXIS]),
        mesh=mesh,
        in_specs=(
            P(("win", AXIS), None),
            P(),
            P(),
            P(("win", AXIS), None),
            P(("win", AXIS), None, None),
        ),
        out_specs=P(None, ("win", AXIS)),
        check_vma=False,
    )
```

```python
import functools

import jax
import jax.numpy as jnp
import numpy as np
from jax import lax
from jax.experimental import pallas as pl
from jax.experimental.pallas import tpu as pltpu
from jax.sharding import PartitionSpec as P

AXIS = "fib"
F = 512
L = 512
Q = 4
LIMIT = 16 << 20
VMEM_SPEC = pl.BlockSpec(memory_space=pltpu.VMEM)
HBM_SPEC = pl.BlockSpec(memory_space=pl.ANY)


STEP = 32


def forward_factors(samples):
    m = np.arange(F // Q, dtype=np.int64)
    k = (Q * m[None, :] + np.arange(Q)[:, None] + 1)[:, None, :]
    scale = samples ** (-0.5)
    parts = []
    for step, factor in ((STEP, scale), (1, 1.0)):
        count = samples // Q // STEP if step == STEP else STEP
        t = step * np.arange(count, dtype=np.int64)[None, :, None]
        phase = (t * k % samples) * (2.0 * np.pi / samples)
        parts += [np.cos(phase) * factor, np.sin(phase) * factor]
    table = np.stack(parts)
    return np.stack([table[:, 0::2], table[:, 1::2]]).astype(np.float32)


def inverse_table(samples):
    freqs = F // Q
    k = Q * np.arange(freqs, dtype=np.int64)[None, :, None] + np.arange(Q)[:, None, None] + 1
    lag = np.arange(L, dtype=np.int64)[None, None, :] - L // 2
    theta = (k * lag % samples) * (2.0 * np.pi / samples)
    table = np.concatenate([np.cos(theta), -np.sin(theta)], axis=1) * (2 * F) ** (-0.5)
    return table.astype(jnp.bfloat16)


def in_hbm(value):
    return pltpu.with_memory_space_constraint(value, pltpu.HBM)


def dot(a, b):
    return jnp.dot(a, b, preferred_element_type=jnp.float32)


def combine(a, b):
    half = a.shape[1] // 2
    return jnp.concatenate([a[:, :half] + b[:, half:], a[:, half:] - b[:, :half]], axis=1)


def complex_classes(folds, table):
    channels = folds.shape[1]
    both = folds[...].reshape(2 * channels, folds.shape[2])
    values = []
    for n, sign in ((0, 1.0), (1, -1.0)):
        product = dot(both, table[n])
        values.append(combine(product[:channels], product[channels:] * sign))
    return values


def real_classes(folds, table):
    return [dot(folds[n], table[n]) for n in range(2)]


def fill_table(factors, table):
    half = table.shape[2] // 2
    for n in range(2):
        cos_v, sin_v = factors[2, n], factors[3, n]
        for u in range(factors.shape[2]):
            cos_u, sin_u = factors[0, n, u : u + 1, :], factors[1, n, u : u + 1, :]
            rows = slice(u * STEP, (u + 1) * STEP)
            table[n, rows, :half] = (cos_u * cos_v - sin_u * sin_v).astype(jnp.bfloat16)
            table[n, rows, half:] = (-sin_u * cos_v - cos_u * sin_v).astype(jnp.bfloat16)


def send_kernel(
    strain, factors, listed, bands,
    swap, folds, kept_table,
    time, sent_table, factors_in, listed_in, bands_in, sems,
):
    me = lax.rem(lax.axis_index(AXIS), Q)
    core, side = lax.rem(me, 2), me // 2
    channels, samples = strain.shape
    quarter = samples // Q
    depth = quarter // 2
    small = [
        pltpu.make_async_copy(factors, factors_in, sems.at[2 * Q]),
        pltpu.make_async_copy(listed, listed_in, sems.at[2 * Q + 1]),
        pltpu.make_async_copy(bands, bands_in, sems.at[2 * Q + 2]),
    ]
    copies = []
    for h in range(2):
        for q in range(Q):
            part = (slice(None), pl.ds(q * quarter + h * depth, depth))
            copies.append(
                pltpu.make_async_copy(strain.at[part], time.at[part], sems.at[h * Q + q])
            )
    for copy in small + copies:
        copy.start()
    for copy in small:
        copy.wait()

    fill_table(factors_in.at[1 - core], sent_table)
    nbands = bands.shape[1]
    width = swap.shape[2] // nbands
    rounds = bands.shape[2]
    used = (listed_in[...] * bands_in[0]).astype(jnp.float32)
    pick = lax.broadcasted_iota(jnp.int32, (rounds, rounds), 0) == lax.broadcasted_iota(
        jnp.int32, (rounds, rounds), 1
    )
    weight = jnp.concatenate(
        [
            jnp.broadcast_to(
                jnp.sum(
                    jnp.where(pick, jnp.broadcast_to(used[j : j + 1], (rounds, rounds)), 0.0),
                    axis=1,
                    keepdims=True,
                ),
                (rounds, width),
            )
            for j in range(nbands)
        ],
        axis=1,
    ).astype(jnp.bfloat16)
    for n in range(2):
        swap[n, channels:, :] = weight
    fill_table(factors_in.at[core], kept_table)

    for h in range(2):
        for copy in copies[h * Q : (h + 1) * Q]:
            copy.wait()
        here = pl.ds(h * depth, depth)
        q0, q1, q2, q3 = (time[:, pl.ds(q * quarter + h * depth, depth)] for q in range(Q))
        folds[0, 0, :, here] = q0 - q2
        folds[0, 1, :, here] = q1 - q3
        even = q0.astype(jnp.float32) + q2.astype(jnp.float32)
        odd = q1.astype(jnp.float32) + q3.astype(jnp.float32)
        folds[1, 0, :, here] = (even - odd).astype(jnp.bfloat16)
        folds[1, 1, :, here] = (even + odd).astype(jnp.bfloat16)

    def store(values):
        for n, value in enumerate(values):
            swap[lax.bitwise_xor(side, n), :channels, :] = value.astype(jnp.bfloat16)

    @pl.when(core == 0)
    def _():
        store(real_classes(folds.at[1], sent_table))

    @pl.when(core == 1)
    def _():
        store(complex_classes(folds.at[0], sent_table))


def keep_kernel(swap, folds, table, near, mates):
    me = lax.rem(lax.axis_index(AXIS), Q)
    core, side = lax.rem(me, 2), me // 2
    channels = folds.shape[2]
    near[0, channels:, :] = swap[0, channels:, :]
    mates[0, channels:, :] = swap[0, channels:, :]

    def store(values):
        for n, value in enumerate(values):
            value = value.astype(jnp.bfloat16)

            @pl.when(side == n)
            def _():
                near[0, :channels, :] = value

            @pl.when(side != n)
            def _():
                mates[0, :channels, :] = value

    @pl.when(core == 0)
    def _():
        store(complex_classes(folds.at[0], table))

    @pl.when(core == 1)
    def _():
        store(real_classes(folds.at[1], table))


def send_call(strain, listed, bands):
    channels, samples = strain.shape
    factors = forward_factors(samples)
    rows, cols = channels + bands.shape[2], 2 * factors.shape[4]
    quarter = samples // Q
    return pl.pallas_call(
        send_kernel,
        in_specs=[HBM_SPEC] * 4,
        out_specs=[VMEM_SPEC] * 3,
        out_shape=[
            pltpu.VMEM((2, rows, cols), jnp.bfloat16),
            pltpu.VMEM((2, 2, channels, quarter), jnp.bfloat16),
            pltpu.VMEM((2, quarter, cols), jnp.bfloat16),
        ],
        scratch_shapes=[
            pltpu.VMEM((channels, samples), jnp.bfloat16),
            pltpu.VMEM((2, quarter, cols), jnp.bfloat16),
            pltpu.VMEM(factors.shape, jnp.float32),
            pltpu.VMEM(listed.shape, listed.dtype),
            pltpu.VMEM(bands.shape, bands.dtype),
            pltpu.SemaphoreType.DMA((2 * Q + 3,)),
        ],
        compiler_params=pltpu.CompilerParams(vmem_limit_bytes=LIMIT),
        name="spectrum_sent",
    )(in_hbm(strain), in_hbm(jnp.asarray(factors)), in_hbm(listed), in_hbm(bands))


def make_unit(me, rounds, i, j):
    target_plane, i = i
    source_plane, j = j
    p, q = lax.bitwise_xor(me, i), lax.bitwise_xor(me, j)
    d = (target_plane + source_plane) * Q + i - j
    target = 2 * Q * target_plane + p
    source = Q * source_plane + q
    row = d - 1 if target_plane + source_plane or i != j else rounds
    return target, source, d, target_plane * Q + i, target_plane * Q + p, row


def early_units(me, rounds):
    base = 2 * (me // 2)

    def unit(i, j):
        return make_unit(me, rounds, i, j)

    def own(i, j):
        return unit((0, i), (0, j))

    def low(i, e):
        return unit((0, i), (1, base + e))

    def mid(e, f):
        return unit((1, base + e), (1, base + f))

    twins, rest = [], []
    for d in range(Q):
        group = [own(i, i - d) for i in range(d, Q)]
        twins += [group[n : n + 2] for n in range(0, len(group) // 2 * 2, 2)]
        rest += group[len(group) // 2 * 2 :]
    twins += [[low(i, 0), low(i + 1, 1)] for i in range(Q - 1)]
    twins.append([mid(0, 0), mid(1, 1)])
    rest += [low(Q - 1, 0), low(0, 1), mid(0, 1)]
    return twins, rest


def late_units(me, rounds):
    base = 2 * (1 - me // 2)

    def low(i, e):
        return make_unit(me, rounds, (0, i), (1, base + e))

    def mid(i, j):
        return make_unit(me, rounds, (1, i), (1, j))

    twins = [[low(i, 0), low(i + 1, 1)] for i in range(Q - 1)]
    twins.append([mid(base, base), mid(base + 1, base + 1)])
    twins.append([mid(0, 2), mid(1, 3)])
    twins.append([mid(1, 2), mid(base, base + 1)])
    return twins, [low(Q - 1, 0), low(0, 1), mid(0, 3)]


def run_units(plan, spec, mask, steering, inv, lag_range, window):
    channels, angles = steering.shape[2], steering.shape[1]
    cols = spec.shape[2]
    half = cols // 2
    twins, rest = plan
    units = [unit for pair in twins for unit in pair] + rest
    beams = []
    for target, source, d, _, _, _ in units:
        near_re, near_im = spec[target, :channels, :half], spec[target, :channels, half:]
        far_re, far_im = spec[source, :channels, :half], spec[source, :channels, half:]
        real = near_re * far_re + near_im * far_im
        imag = near_im * far_re - near_re * far_im
        cross = jnp.concatenate([real, imag], axis=1)
        beams.append(dot(steering[d], cross).astype(jnp.bfloat16))
    beams = dot(jnp.concatenate(beams, axis=0), inv[...])
    masked = []
    for u, (_, _, _, _, target, row) in enumerate(units):
        weight = jnp.concatenate(
            [mask[target, h, pl.ds(row, 1), :] for h in range(L // cols)], axis=1
        )
        masked.append((beams[u * angles : (u + 1) * angles, :] * weight).astype(jnp.bfloat16))
    for u in range(0, 2 * len(twins), 2):
        part = dot(jnp.concatenate(masked[u : u + 2], axis=0), lag_range[units[u][2]])
        window[units[u][3]] += part[:angles]
        window[units[u + 1][3]] += part[angles:]
    for u in range(2 * len(twins), len(units)):
        window[units[u][3]] += dot(masked[u], lag_range[units[u][2]])


def fill_mask(mask, entry, spec, slot, channels, nbands):
    rounds = mask.shape[2] // 2
    rows = spec[slot, channels:, :].astype(jnp.float32)
    cols = mask.shape[3]
    for j in range(nbands):
        h, lane = divmod(j * (mask.shape[1] * cols // nbands), cols)
        width = mask.shape[1] * cols // nbands
        mask[entry, h, :rounds, lane : lane + width] = jnp.broadcast_to(
            rows[:, j * (cols // nbands) : j * (cols // nbands) + 1], (rounds, width)
        )
    mask[entry, :, rounds:, :] = jnp.ones((mask.shape[1], rounds, cols), jnp.float32)


def neighbour_slots():
    me = lax.axis_index(AXIS)
    parity = lax.rem(me // Q + me, 2)
    return Q * (2 - parity), Q * (1 + parity)


def early_kernel(
    nbands, near, mates, even, odd, inv_all, steering, lag_range,
    spec, window, inv, mask, sem,
):
    me = lax.rem(lax.axis_index(AXIS), Q)
    copy = pltpu.make_async_copy(inv_all.at[me], inv, sem)
    copy.start()
    even_slot, odd_slot = neighbour_slots()
    spec[0:2] = near[...]
    spec[2:4] = mates[...]
    spec[pl.ds(even_slot, 2)] = even[...]
    spec[pl.ds(odd_slot, 2)] = odd[...]
    window[...] = jnp.zeros_like(window)
    channels = steering.shape[2]
    for p in range(Q):
        fill_mask(mask, p, spec, p, channels, nbands)
    for p in range(Q // 2):
        fill_mask(mask, Q + p, spec, 2 * Q + p, channels, nbands)
    copy.wait()
    plan = early_units(me, steering.shape[0] - 1)
    run_units(plan, spec, mask, steering, inv, lag_range, window)


def late_kernel(
    nbands, spec_in, window_in, even, odd, inv, steering, lag_range,
    keep, send, spec, window, mask,
):
    me = lax.rem(lax.axis_index(AXIS), Q)
    even_slot, odd_slot = neighbour_slots()
    spec[pl.ds(even_slot + 2, 2)] = even[...]
    spec[pl.ds(odd_slot + 2, 2)] = odd[...]
    channels = steering.shape[2]
    for p in range(Q):
        fill_mask(mask, p, spec, p, channels, nbands)
        fill_mask(mask, Q + p, spec, 2 * Q + p, channels, nbands)
    plan = late_units(me, steering.shape[0] - 1)
    run_units(plan, spec, mask, steering, inv, lag_range, window)

    width = window.shape[2] // 3

    def segment(s):
        total = None
        for slot, part in ((s, 1), (s - 1, 2), (s + 1, 0)):
            if 0 <= slot < 2 * Q:
                value = window[slot, :, part * width : (part + 1) * width]
                total = value if total is None else total + value
        return total

    core = lax.rem(me, 2)
    here = [segment(s) for s in list(range(Q)) + [2 * Q, -1]]
    there = [segment(Q + p) for p in range(Q)]

    @pl.when(core == 0)
    def _():
        for n, value in enumerate(there):
            keep[n] = value
        for n in range(Q, Q + 2):
            keep[n] = jnp.zeros_like(there[0])
        for n, value in enumerate(here):
            send[n] = value.astype(jnp.bfloat16)

    @pl.when(core == 1)
    def _():
        for n, value in enumerate(here):
            keep[n] = value
        for n, value in enumerate(there):
            send[n] = value.astype(jnp.bfloat16)
        for n in range(Q, Q + 2):
            send[n] = jnp.zeros_like(there[0]).astype(jnp.bfloat16)


def join_kernel(swap, near_in, mates_in, near, mates):
    near[1] = swap[0]
    mates[1] = swap[1]


def core_sum_kernel(kept, received, mine, send):
    side = lax.rem(lax.axis_index(AXIS), Q) // 2

    def total(n):
        return kept[n] + received[n].astype(jnp.float32)

    for n in range(2):
        mine[n] = total(2 * side + n)
        send[n] = total(2 * (1 - side) + n).astype(jnp.bfloat16)
    mine[2] = total(Q + side)
    send[2] = total(Q + 1 - side).astype(jnp.bfloat16)


def plane_sum_kernel(kept, received, mine, send):
    core = lax.rem(lax.axis_index(AXIS), 2)
    totals = [kept[n] + received[n].astype(jnp.float32) for n in range(3)]
    mine[0] = totals[0]
    mine[1] = totals[1]

    @pl.when(core == 0)
    def _():
        send[0] = totals[0].astype(jnp.bfloat16)
        send[1] = totals[1].astype(jnp.bfloat16)

    @pl.when(core == 1)
    def _():
        send[0] = totals[2].astype(jnp.bfloat16)
        send[1] = jnp.zeros_like(totals[2]).astype(jnp.bfloat16)


def end_sum_kernel(kept, received, mine, send):
    me = lax.rem(lax.axis_index(AXIS), Q)
    first = received[0].astype(jnp.float32)
    second = received[1].astype(jnp.float32)
    core, side = lax.rem(me, 2), me // 2

    @pl.when(core == 0)
    def _():
        mine[...] = first
        send[...] = second

    @pl.when((core == 1) & (side == 0))
    def _():
        mine[...] = kept[1]
        send[...] = kept[0] + first

    @pl.when((core == 1) & (side == 1))
    def _():
        mine[...] = kept[1] + first
        send[...] = kept[0]


def image_kernel(kept, received, image):
    image[...] = kept[...] + received[...]


def near_vmem(*values):
    return [pltpu.with_memory_space_constraint(value, pltpu.VMEM) for value in values]


def local_call(kernel, name, outs, *values, aliases={}):
    return pl.pallas_call(
        kernel,
        in_specs=[VMEM_SPEC] * len(values),
        out_specs=[VMEM_SPEC] * len(outs),
        out_shape=outs,
        input_output_aliases=aliases,
        compiler_params=pltpu.CompilerParams(vmem_limit_bytes=LIMIT),
        name=name,
    )(*near_vmem(*values))


def early_call(nbands, near, mates, even, odd, inv, steering, lag_range):
    _, rows, cols = near.shape
    angles, group = steering.shape[1], lag_range.shape[2]
    rounds = steering.shape[0] - 1
    return pl.pallas_call(
        functools.partial(early_kernel, nbands),
        in_specs=[VMEM_SPEC] * 4 + [HBM_SPEC] + [VMEM_SPEC] * 2,
        out_specs=[VMEM_SPEC] * 3,
        out_shape=[
            pltpu.VMEM((3 * Q, rows, cols), jnp.bfloat16),
            pltpu.VMEM((2 * Q, angles, group), jnp.float32),
            pltpu.VMEM(inv.shape[1:], inv.dtype),
        ],
        scratch_shapes=[
            pltpu.VMEM((2 * Q, L // cols, 2 * rounds, cols), jnp.float32),
            pltpu.SemaphoreType.DMA(()),
        ],
        compiler_params=pltpu.CompilerParams(vmem_limit_bytes=LIMIT),
        name="early_pairs",
    )(*near_vmem(near, mates, even, odd), in_hbm(inv), *near_vmem(steering, lag_range))


def late_call(nbands, spec, window, even, odd, inv, steering, lag_range):
    cols = spec.shape[2]
    angles, group = steering.shape[1], lag_range.shape[2]
    rounds = steering.shape[0] - 1
    pieces = (Q + 2, angles, group // 3)
    return pl.pallas_call(
        functools.partial(late_kernel, nbands),
        in_specs=[VMEM_SPEC] * 7,
        out_specs=[VMEM_SPEC] * 4,
        out_shape=[
            pltpu.VMEM(pieces, jnp.float32),
            pltpu.VMEM(pieces, jnp.bfloat16),
            pltpu.VMEM(spec.shape, spec.dtype),
            pltpu.VMEM(window.shape, window.dtype),
        ],
        input_output_aliases={0: 2, 1: 3},
        scratch_shapes=[pltpu.VMEM((2 * Q, L // cols, 2 * rounds, cols), jnp.float32)],
        compiler_params=pltpu.CompilerParams(vmem_limit_bytes=LIMIT),
        name="late_pairs",
    )(*near_vmem(spec, window, even, odd, inv, steering, lag_range))[:2]


def exchange(value, devices, target):
    pairs = [(i, target(i)) for i in range(devices) if target(i) is not None]
    pairs = [(i, j) for i, j in pairs if 0 <= j < devices]
    return lax.ppermute(value, AXIS, pairs)


def per_device(devices, strain, steering, lag_range, pair_listed, band_used):
    def planes(value, parity):
        return exchange(value, devices, lambda i: i + (Q if (i // Q + i) % 2 == parity else -Q))

    def flip(value, by):
        return exchange(value, devices, lambda i: i ^ by)

    swap, folds, table = send_call(strain, pair_listed, jnp.transpose(band_used, (0, 2, 1)))
    joined = pltpu.VMEM(swap.shape, swap.dtype)
    near, mates = local_call(keep_kernel, "spectrum_kept", [joined, joined], swap, folds, table)
    near, mates = local_call(
        join_kernel, "join", [joined, joined], flip(swap, 1), near, mates, aliases={1: 0, 2: 1}
    )
    mates = flip(mates, 2)
    near_odd, near_even = planes(near, 1), planes(near, 0)
    far_odd, far_even = planes(mates, 1), planes(mates, 0)
    nbands = band_used.shape[2]
    inv = jnp.asarray(inverse_table(strain.shape[1]))
    spec, window, inv = early_call(
        nbands, near, mates, near_even, near_odd, inv, steering, lag_range
    )
    kept, send = late_call(
        nbands, spec, window, far_even, far_odd, inv, steering, lag_range
    )

    def pieces(count, dtype):
        return pltpu.VMEM(((count,) if count else ()) + kept.shape[1:], dtype)

    def ends(i):
        if i % 2 == 0:
            return i + Q
        return i + 2 * Q if i % Q < 2 else i - Q

    kept, send = local_call(
        core_sum_kernel,
        "core_sum",
        [pieces(3, jnp.float32), pieces(3, jnp.bfloat16)],
        kept,
        flip(send, 1),
    )
    kept, send = local_call(
        plane_sum_kernel,
        "plane_sum",
        [pieces(2, jnp.float32), pieces(2, jnp.bfloat16)],
        kept,
        flip(send, 2),
    )
    kept, send = local_call(
        end_sum_kernel,
        "end_sum",
        [pieces(0, jnp.float32), pieces(0, jnp.float32)],
        kept,
        exchange(send, devices, ends),
    )
    return local_call(
        image_kernel,
        "image",
        [jax.ShapeDtypeStruct(kept.shape, jnp.float32)],
        kept,
        flip(send, 1),
    )[0]


def solution(mesh):
    return jax.shard_map(
        functools.partial(per_device, mesh.shape[AXIS]),
        mesh=mesh,
        in_specs=(
            P(("win", AXIS), None),
            P(),
            P(),
            P(("win", AXIS), None),
            P(("win", AXIS), None, None),
        ),
        out_specs=P(None, ("win", AXIS)),
        check_vma=False,
    )
```

```python
import functools

import jax
import jax.numpy as jnp
import numpy as np
from jax import lax
from jax.experimental import pallas as pl
from jax.experimental.pallas import tpu as pltpu
from jax.sharding import PartitionSpec as P

AXIS = "fib"
F = 512
L = 512
Q = 4
LIMIT = 16 << 20
VMEM_SPEC = pl.BlockSpec(memory_space=pltpu.VMEM)
HBM_SPEC = pl.BlockSpec(memory_space=pl.ANY)


STEP = 32


def forward_factors(samples):
    m = np.arange(F // Q, dtype=np.int64)
    k = (Q * m[None, :] + np.arange(Q)[:, None] + 1)[:, None, :]
    scale = samples ** (-0.5)
    parts = []
    for step, factor in ((STEP, scale), (1, 1.0)):
        count = samples // Q // STEP if step == STEP else STEP
        t = step * np.arange(count, dtype=np.int64)[None, :, None]
        phase = (t * k % samples) * (2.0 * np.pi / samples)
        parts += [np.cos(phase) * factor, np.sin(phase) * factor]
    table = np.stack(parts)
    return np.stack([table[:, 0::2], table[:, 1::2]]).astype(np.float32)


def inverse_table(samples):
    freqs = F // Q
    k = Q * np.arange(freqs, dtype=np.int64)[None, :, None] + np.arange(Q)[:, None, None] + 1
    lag = np.arange(L, dtype=np.int64)[None, None, :] - L // 2
    theta = (k * lag % samples) * (2.0 * np.pi / samples)
    table = np.concatenate([np.cos(theta), -np.sin(theta)], axis=1) * (2 * F) ** (-0.5)
    return table.astype(jnp.bfloat16)


def in_hbm(value):
    return pltpu.with_memory_space_constraint(value, pltpu.HBM)


def dot(a, b):
    return jnp.dot(a, b, preferred_element_type=jnp.float32)


def combine(a, b):
    half = a.shape[1] // 2
    return jnp.concatenate([a[:, :half] + b[:, half:], a[:, half:] - b[:, :half]], axis=1)


def complex_classes(folds, table):
    channels = folds.shape[1]
    both = folds[...].reshape(2 * channels, folds.shape[2])
    values = []
    for n, sign in ((0, 1.0), (1, -1.0)):
        product = dot(both, table[n])
        values.append(combine(product[:channels], product[channels:] * sign))
    return values


def real_classes(folds, table):
    return [dot(folds[n], table[n]) for n in range(2)]


def fill_table(factors, table):
    half = table.shape[2] // 2
    for n in range(2):
        cos_v, sin_v = factors[2, n], factors[3, n]
        for u in range(factors.shape[2]):
            cos_u, sin_u = factors[0, n, u : u + 1, :], factors[1, n, u : u + 1, :]
            rows = slice(u * STEP, (u + 1) * STEP)
            table[n, rows, :half] = (cos_u * cos_v - sin_u * sin_v).astype(jnp.bfloat16)
            table[n, rows, half:] = (-sin_u * cos_v - cos_u * sin_v).astype(jnp.bfloat16)


def send_kernel(
    strain, factors, listed, bands,
    swap, folds, kept_table,
    time, sent_table, factors_in, listed_in, bands_in, sems,
):
    me = lax.rem(lax.axis_index(AXIS), Q)
    core, side = lax.rem(me, 2), me // 2
    channels, samples = strain.shape
    quarter = samples // Q
    depth = quarter // 2
    small = [
        pltpu.make_async_copy(factors, factors_in, sems.at[2 * Q]),
        pltpu.make_async_copy(listed, listed_in, sems.at[2 * Q + 1]),
        pltpu.make_async_copy(bands, bands_in, sems.at[2 * Q + 2]),
    ]
    copies = []
    for h in range(2):
        for q in range(Q):
            part = (slice(None), pl.ds(q * quarter + h * depth, depth))
            copies.append(
                pltpu.make_async_copy(strain.at[part], time.at[part], sems.at[h * Q + q])
            )
    for copy in small + copies:
        copy.start()
    for copy in small:
        copy.wait()

    fill_table(factors_in.at[1 - core], sent_table)
    nbands = bands.shape[1]
    width = swap.shape[2] // nbands
    rounds = bands.shape[2]
    used = (listed_in[...] * bands_in[0]).astype(jnp.float32)
    pick = lax.broadcasted_iota(jnp.int32, (rounds, rounds), 0) == lax.broadcasted_iota(
        jnp.int32, (rounds, rounds), 1
    )
    weight = jnp.concatenate(
        [
            jnp.broadcast_to(
                jnp.sum(
                    jnp.where(pick, jnp.broadcast_to(used[j : j + 1], (rounds, rounds)), 0.0),
                    axis=1,
                    keepdims=True,
                ),
                (rounds, width),
            )
            for j in range(nbands)
        ],
        axis=1,
    ).astype(jnp.bfloat16)
    for n in range(2):
        swap[n, channels:, :] = weight
    fill_table(factors_in.at[core], kept_table)

    for h in range(2):
        for copy in copies[h * Q : (h + 1) * Q]:
            copy.wait()
        here = pl.ds(h * depth, depth)
        q0, q1, q2, q3 = (time[:, pl.ds(q * quarter + h * depth, depth)] for q in range(Q))
        folds[0, 0, :, here] = q0 - q2
        folds[0, 1, :, here] = q1 - q3
        even = q0.astype(jnp.float32) + q2.astype(jnp.float32)
        odd = q1.astype(jnp.float32) + q3.astype(jnp.float32)
        folds[1, 0, :, here] = (even - odd).astype(jnp.bfloat16)
        folds[1, 1, :, here] = (even + odd).astype(jnp.bfloat16)

    def store(values):
        for n, value in enumerate(values):
            swap[lax.bitwise_xor(side, n), :channels, :] = value.astype(jnp.bfloat16)

    @pl.when(core == 0)
    def _():
        store(real_classes(folds.at[1], sent_table))

    @pl.when(core == 1)
    def _():
        store(complex_classes(folds.at[0], sent_table))


def keep_kernel(swap, folds, table, near, mates):
    me = lax.rem(lax.axis_index(AXIS), Q)
    core, side = lax.rem(me, 2), me // 2
    channels = folds.shape[2]
    near[0, channels:, :] = swap[0, channels:, :]
    mates[0, channels:, :] = swap[0, channels:, :]

    def store(values):
        for n, value in enumerate(values):
            value = value.astype(jnp.bfloat16)

            @pl.when(side == n)
            def _():
                near[0, :channels, :] = value

            @pl.when(side != n)
            def _():
                mates[0, :channels, :] = value

    @pl.when(core == 0)
    def _():
        store(complex_classes(folds.at[0], table))

    @pl.when(core == 1)
    def _():
        store(real_classes(folds.at[1], table))


def send_call(strain, listed, bands):
    channels, samples = strain.shape
    factors = forward_factors(samples)
    rows, cols = channels + bands.shape[2], 2 * factors.shape[4]
    quarter = samples // Q
    return pl.pallas_call(
        send_kernel,
        in_specs=[HBM_SPEC] * 4,
        out_specs=[VMEM_SPEC] * 3,
        out_shape=[
            pltpu.VMEM((2, rows, cols), jnp.bfloat16),
            pltpu.VMEM((2, 2, channels, quarter), jnp.bfloat16),
            pltpu.VMEM((2, quarter, cols), jnp.bfloat16),
        ],
        scratch_shapes=[
            pltpu.VMEM((channels, samples), jnp.bfloat16),
            pltpu.VMEM((2, quarter, cols), jnp.bfloat16),
            pltpu.VMEM(factors.shape, jnp.float32),
            pltpu.VMEM(listed.shape, listed.dtype),
            pltpu.VMEM(bands.shape, bands.dtype),
            pltpu.SemaphoreType.DMA((2 * Q + 3,)),
        ],
        compiler_params=pltpu.CompilerParams(vmem_limit_bytes=LIMIT),
        name="spectrum_sent",
    )(in_hbm(strain), in_hbm(jnp.asarray(factors)), in_hbm(listed), in_hbm(bands))


def make_unit(me, rounds, i, j):
    target_plane, i = i
    source_plane, j = j
    p, q = lax.bitwise_xor(me, i), lax.bitwise_xor(me, j)
    d = (target_plane + source_plane) * Q + i - j
    target = 2 * Q * target_plane + p
    source = Q * source_plane + q
    row = d - 1 if target_plane + source_plane or i != j else rounds
    return target, source, d, target_plane * Q + i, target_plane * Q + p, row


def early_units(me, rounds):
    base = 2 * (me // 2)

    def unit(i, j):
        return make_unit(me, rounds, i, j)

    def own(i, j):
        return unit((0, i), (0, j))

    def low(i, e):
        return unit((0, i), (1, base + e))

    def mid(e, f):
        return unit((1, base + e), (1, base + f))

    twins, rest = [], []
    for d in range(Q):
        group = [own(i, i - d) for i in range(d, Q)]
        twins += [group[n : n + 2] for n in range(0, len(group) // 2 * 2, 2)]
        rest += group[len(group) // 2 * 2 :]
    twins += [[low(i, 0), low(i + 1, 1)] for i in range(Q - 1)]
    twins.append([mid(0, 0), mid(1, 1)])
    rest += [low(Q - 1, 0), low(0, 1), mid(0, 1)]
    return twins, rest


def late_units(me, rounds):
    base = 2 * (1 - me // 2)

    def mid(i, j):
        return make_unit(me, rounds, (1, i), (1, j))

    twins = [[mid(base, base), mid(base + 1, base + 1)]]
    twins.append([mid(0, 2), mid(1, 3)])
    twins.append([mid(1, 2), mid(base, base + 1)])
    return twins, [mid(0, 3)]


def mask_row(mask, target, row):
    return jnp.concatenate([mask[target, h, pl.ds(row, 1), :] for h in range(mask.shape[1])], axis=1)


def low_units(me, rounds):
    base = 2 * (1 - me // 2)
    return [
        make_unit(me, rounds, (0, i), (1, base + e)) for i in range(Q) for e in range(2)
    ]


def prepare_maps(units, mask, inv, lag_range, maps):
    for n, (_, _, d, _, target, row) in enumerate(units):
        weight = mask_row(mask, target, row).astype(jnp.bfloat16)
        maps[n] = dot(inv[...] * weight, lag_range[d]).astype(jnp.bfloat16)


def steered(units, spec, steering):
    channels = steering.shape[2]
    half = spec.shape[2] // 2
    beams = []
    for target, source, d, _, _, _ in units:
        near_re, near_im = spec[target, :channels, :half], spec[target, :channels, half:]
        far_re, far_im = spec[source, :channels, :half], spec[source, :channels, half:]
        real = near_re * far_re + near_im * far_im
        imag = near_im * far_re - near_re * far_im
        cross = jnp.concatenate([real, imag], axis=1)
        beams.append(dot(steering[d], cross).astype(jnp.bfloat16))
    return beams


def run_units(plan, spec, mask, steering, inv, lag_range, window, mapped=(), maps=None):
    angles = steering.shape[1]
    twins, rest = plan
    units = [unit for pair in twins for unit in pair] + rest
    beams = steered(units + list(mapped), spec, steering)
    mapped_beams = beams[len(units) :]
    beams = dot(jnp.concatenate(beams[: len(units)], axis=0), inv[...])
    masked = []
    for u, (_, _, _, _, target, row) in enumerate(units):
        weight = mask_row(mask, target, row)
        masked.append((beams[u * angles : (u + 1) * angles, :] * weight).astype(jnp.bfloat16))
    for u in range(0, 2 * len(twins), 2):
        part = dot(jnp.concatenate(masked[u : u + 2], axis=0), lag_range[units[u][2]])
        window[units[u][3]] += part[:angles]
        window[units[u + 1][3]] += part[angles:]
    for u in range(2 * len(twins), len(units)):
        window[units[u][3]] += dot(masked[u], lag_range[units[u][2]])
    for n in range(0, len(mapped), 2):
        both = jnp.concatenate(mapped_beams[n : n + 2], axis=1)
        window[mapped[n][3]] += dot(both, maps[n : n + 2].reshape(both.shape[1], -1))


def fill_mask(mask, entry, spec, slot, channels, nbands):
    rounds = mask.shape[2] // 2
    rows = spec[slot, channels:, :].astype(jnp.float32)
    cols = mask.shape[3]
    for j in range(nbands):
        h, lane = divmod(j * (mask.shape[1] * cols // nbands), cols)
        width = mask.shape[1] * cols // nbands
        mask[entry, h, :rounds, lane : lane + width] = jnp.broadcast_to(
            rows[:, j * (cols // nbands) : j * (cols // nbands) + 1], (rounds, width)
        )
    mask[entry, :, rounds:, :] = jnp.ones((mask.shape[1], rounds, cols), jnp.float32)


def neighbour_slots():
    parity = lax.rem(lax.axis_index(AXIS) // Q, 2)
    return Q * (2 - parity), Q * (1 + parity)


def early_kernel(
    nbands, near, mates, even, odd, inv_all, steering, lag_range,
    spec, window, inv, maps, mask, sem,
):
    me = lax.rem(lax.axis_index(AXIS), Q)
    copy = pltpu.make_async_copy(inv_all.at[me], inv, sem)
    copy.start()
    even_slot, odd_slot = neighbour_slots()
    spec[0:2] = near[...]
    spec[2:4] = mates[...]
    spec[pl.ds(even_slot, 2)] = even[...]
    spec[pl.ds(odd_slot, 2)] = odd[...]
    window[...] = jnp.zeros_like(window)
    channels = steering.shape[2]
    for p in range(Q):
        fill_mask(mask, p, spec, p, channels, nbands)
    for p in range(Q // 2):
        fill_mask(mask, Q + p, spec, 2 * Q + p, channels, nbands)
    copy.wait()
    plan = early_units(me, steering.shape[0] - 1)
    run_units(plan, spec, mask, steering, inv, lag_range, window)
    prepare_maps(low_units(me, steering.shape[0] - 1), mask, inv, lag_range, maps)


def late_kernel(
    nbands, spec_in, window_in, even, odd, inv, maps, steering, lag_range,
    keep, send, spec, window, mask,
):
    me = lax.rem(lax.axis_index(AXIS), Q)
    even_slot, odd_slot = neighbour_slots()
    spec[pl.ds(even_slot + 2, 2)] = even[...]
    spec[pl.ds(odd_slot + 2, 2)] = odd[...]
    channels = steering.shape[2]
    for p in range(Q):
        fill_mask(mask, p, spec, p, channels, nbands)
        fill_mask(mask, Q + p, spec, 2 * Q + p, channels, nbands)
    plan = late_units(me, steering.shape[0] - 1)
    mapped = low_units(me, steering.shape[0] - 1)
    run_units(plan, spec, mask, steering, inv, lag_range, window, mapped, maps)

    width = window.shape[2] // 3

    def segment(s):
        total = None
        for slot, part in ((s, 1), (s - 1, 2), (s + 1, 0)):
            if 0 <= slot < 2 * Q:
                value = window[slot, :, part * width : (part + 1) * width]
                total = value if total is None else total + value
        return total

    core = lax.rem(me, 2)
    here = [segment(s) for s in list(range(Q)) + [2 * Q, -1]]
    there = [segment(Q + p) for p in range(Q)]

    @pl.when(core == 0)
    def _():
        for n, value in enumerate(there):
            keep[n] = value
        for n in range(Q, Q + 2):
            keep[n] = jnp.zeros_like(there[0])
        for n, value in enumerate(here):
            send[n] = value.astype(jnp.bfloat16)

    @pl.when(core == 1)
    def _():
        for n, value in enumerate(here):
            keep[n] = value
        for n, value in enumerate(there):
            send[n] = value.astype(jnp.bfloat16)
        for n in range(Q, Q + 2):
            send[n] = jnp.zeros_like(there[0]).astype(jnp.bfloat16)


def join_kernel(swap, near_in, mates_in, near, mates):
    near[1] = swap[0]
    mates[1] = swap[1]


def core_sum_kernel(kept, received, mine, send):
    side = lax.rem(lax.axis_index(AXIS), Q) // 2

    def total(n):
        return kept[n] + received[n].astype(jnp.float32)

    for n in range(2):
        mine[n] = total(2 * side + n)
        send[n] = total(2 * (1 - side) + n).astype(jnp.bfloat16)
    mine[2] = total(Q + side)
    send[2] = total(Q + 1 - side).astype(jnp.bfloat16)


def plane_sum_kernel(kept, received, mine, send):
    core = lax.rem(lax.axis_index(AXIS), 2)
    totals = [kept[n] + received[n].astype(jnp.float32) for n in range(3)]
    mine[0] = totals[0]
    mine[1] = totals[1]

    @pl.when(core == 0)
    def _():
        send[0] = totals[0].astype(jnp.bfloat16)
        send[1] = totals[1].astype(jnp.bfloat16)

    @pl.when(core == 1)
    def _():
        send[0] = totals[2].astype(jnp.bfloat16)
        send[1] = jnp.zeros_like(totals[2]).astype(jnp.bfloat16)


def end_sum_kernel(kept, received, mine, send):
    me = lax.rem(lax.axis_index(AXIS), Q)
    first = received[0].astype(jnp.float32)
    second = received[1].astype(jnp.float32)
    core, side = lax.rem(me, 2), me // 2

    @pl.when(core == 0)
    def _():
        mine[...] = first
        send[...] = second

    @pl.when((core == 1) & (side == 0))
    def _():
        mine[...] = kept[1]
        send[...] = kept[0] + first

    @pl.when((core == 1) & (side == 1))
    def _():
        mine[...] = kept[1] + first
        send[...] = kept[0]


def image_kernel(kept, received, image):
    image[...] = kept[...] + received[...]


def near_vmem(*values):
    return [pltpu.with_memory_space_constraint(value, pltpu.VMEM) for value in values]


def local_call(kernel, name, outs, *values, aliases={}):
    return pl.pallas_call(
        kernel,
        in_specs=[VMEM_SPEC] * len(values),
        out_specs=[VMEM_SPEC] * len(outs),
        out_shape=outs,
        input_output_aliases=aliases,
        compiler_params=pltpu.CompilerParams(vmem_limit_bytes=LIMIT),
        name=name,
    )(*near_vmem(*values))


def early_call(nbands, near, mates, even, odd, inv, steering, lag_range):
    _, rows, cols = near.shape
    angles, group = steering.shape[1], lag_range.shape[2]
    rounds = steering.shape[0] - 1
    return pl.pallas_call(
        functools.partial(early_kernel, nbands),
        in_specs=[VMEM_SPEC] * 4 + [HBM_SPEC] + [VMEM_SPEC] * 2,
        out_specs=[VMEM_SPEC] * 4,
        out_shape=[
            pltpu.VMEM((3 * Q, rows, cols), jnp.bfloat16),
            pltpu.VMEM((2 * Q, angles, group), jnp.float32),
            pltpu.VMEM(inv.shape[1:], inv.dtype),
            pltpu.VMEM((2 * Q, cols, group), jnp.bfloat16),
        ],
        scratch_shapes=[
            pltpu.VMEM((2 * Q, L // cols, 2 * rounds, cols), jnp.float32),
            pltpu.SemaphoreType.DMA(()),
        ],
        compiler_params=pltpu.CompilerParams(vmem_limit_bytes=LIMIT),
        name="early_pairs",
    )(*near_vmem(near, mates, even, odd), in_hbm(inv), *near_vmem(steering, lag_range))


def late_call(nbands, spec, window, even, odd, inv, maps, steering, lag_range):
    cols = spec.shape[2]
    angles, group = steering.shape[1], lag_range.shape[2]
    rounds = steering.shape[0] - 1
    pieces = (Q + 2, angles, group // 3)
    return pl.pallas_call(
        functools.partial(late_kernel, nbands),
        in_specs=[VMEM_SPEC] * 8,
        out_specs=[VMEM_SPEC] * 4,
        out_shape=[
            pltpu.VMEM(pieces, jnp.float32),
            pltpu.VMEM(pieces, jnp.bfloat16),
            pltpu.VMEM(spec.shape, spec.dtype),
            pltpu.VMEM(window.shape, window.dtype),
        ],
        input_output_aliases={0: 2, 1: 3},
        scratch_shapes=[pltpu.VMEM((2 * Q, L // cols, 2 * rounds, cols), jnp.float32)],
        compiler_params=pltpu.CompilerParams(vmem_limit_bytes=LIMIT),
        name="late_pairs",
    )(*near_vmem(spec, window, even, odd, inv, maps, steering, lag_range))[:2]


def exchange(value, devices, target):
    pairs = [(i, target(i)) for i in range(devices) if target(i) is not None]
    pairs = [(i, j) for i, j in pairs if 0 <= j < devices]
    return lax.ppermute(value, AXIS, pairs)


def per_device(devices, strain, steering, lag_range, pair_listed, band_used):
    def planes(value, parity):
        return exchange(value, devices, lambda i: i + (Q if i // Q % 2 == parity else -Q))

    def flip(value, by):
        return exchange(value, devices, lambda i: i ^ by)

    swap, folds, table = send_call(strain, pair_listed, jnp.transpose(band_used, (0, 2, 1)))
    joined = pltpu.VMEM(swap.shape, swap.dtype)
    near, mates = local_call(keep_kernel, "spectrum_kept", [joined, joined], swap, folds, table)
    near, mates = local_call(
        join_kernel, "join", [joined, joined], flip(swap, 1), near, mates, aliases={1: 0, 2: 1}
    )
    mates = flip(mates, 2)
    near_odd, near_even = planes(near, 1), planes(near, 0)
    far_odd, far_even = planes(mates, 1), planes(mates, 0)
    nbands = band_used.shape[2]
    inv = jnp.asarray(inverse_table(strain.shape[1]))
    spec, window, inv, maps = early_call(
        nbands, near, mates, near_even, near_odd, inv, steering, lag_range
    )
    kept, send = late_call(
        nbands, spec, window, far_even, far_odd, inv, maps, steering, lag_range
    )

    def pieces(count, dtype):
        return pltpu.VMEM(((count,) if count else ()) + kept.shape[1:], dtype)

    def ends(i):
        if i % 2 == 0:
            return i + Q
        return i + 2 * Q if i % Q < 2 else i - Q

    kept, send = local_call(
        core_sum_kernel,
        "core_sum",
        [pieces(3, jnp.float32), pieces(3, jnp.bfloat16)],
        kept,
        flip(send, 1),
    )
    kept, send = local_call(
        plane_sum_kernel,
        "plane_sum",
        [pieces(2, jnp.float32), pieces(2, jnp.bfloat16)],
        kept,
        flip(send, 2),
    )
    kept, send = local_call(
        end_sum_kernel,
        "end_sum",
        [pieces(0, jnp.float32), pieces(0, jnp.float32)],
        kept,
        exchange(send, devices, ends),
    )
    return local_call(
        image_kernel,
        "image",
        [jax.ShapeDtypeStruct(kept.shape, jnp.float32)],
        kept,
        flip(send, 1),
    )[0]


def solution(mesh):
    return jax.shard_map(
        functools.partial(per_device, mesh.shape[AXIS]),
        mesh=mesh,
        in_specs=(
            P(("win", AXIS), None),
            P(),
            P(),
            P(("win", AXIS), None),
            P(("win", AXIS), None, None),
        ),
        out_specs=P(None, ("win", AXIS)),
        check_vma=False,
    )
```

```python
import functools

import jax
import jax.numpy as jnp
import numpy as np
from jax import lax
from jax.experimental import pallas as pl
from jax.experimental.pallas import tpu as pltpu
from jax.sharding import PartitionSpec as P

AXIS = "fib"
F = 512
L = 512
Q = 4
LIMIT = 16 << 20
VMEM_SPEC = pl.BlockSpec(memory_space=pltpu.VMEM)
HBM_SPEC = pl.BlockSpec(memory_space=pl.ANY)


STEP = 32


def forward_factors(samples):
    m = np.arange(F // Q, dtype=np.int64)
    k = (Q * m[None, :] + np.arange(Q)[:, None] + 1)[:, None, :]
    scale = samples ** (-0.5)
    parts = []
    for step, factor in ((STEP, scale), (1, 1.0)):
        count = samples // Q // STEP if step == STEP else STEP
        t = step * np.arange(count, dtype=np.int64)[None, :, None]
        phase = (t * k % samples) * (2.0 * np.pi / samples)
        parts += [np.cos(phase) * factor, np.sin(phase) * factor]
    table = np.stack(parts)
    return np.stack([table[:, 0::2], table[:, 1::2]]).astype(np.float32)


def inverse_table(samples):
    freqs = F // Q
    k = Q * np.arange(freqs, dtype=np.int64)[None, :, None] + np.arange(Q)[:, None, None] + 1
    lag = np.arange(L, dtype=np.int64)[None, None, :] - L // 2
    theta = (k * lag % samples) * (2.0 * np.pi / samples)
    table = np.concatenate([np.cos(theta), -np.sin(theta)], axis=1) * (2 * F) ** (-0.5)
    return table.astype(jnp.bfloat16)


def in_hbm(value):
    return pltpu.with_memory_space_constraint(value, pltpu.HBM)


def dot(a, b):
    return jnp.dot(a, b, preferred_element_type=jnp.float32)


def combine(a, b):
    half = a.shape[1] // 2
    return jnp.concatenate([a[:, :half] + b[:, half:], a[:, half:] - b[:, :half]], axis=1)


def complex_classes(folds, table):
    channels = folds.shape[1]
    both = folds[...].reshape(2 * channels, folds.shape[2])
    values = []
    for n, sign in ((0, 1.0), (1, -1.0)):
        product = dot(both, table[n])
        values.append(combine(product[:channels], product[channels:] * sign))
    return values


def real_classes(folds, table):
    return [dot(folds[n], table[n]) for n in range(2)]


def fill_table(factors, table):
    half = table.shape[2] // 2
    for n in range(2):
        cos_v, sin_v = factors[2, n], factors[3, n]
        for u in range(factors.shape[2]):
            cos_u, sin_u = factors[0, n, u : u + 1, :], factors[1, n, u : u + 1, :]
            rows = slice(u * STEP, (u + 1) * STEP)
            table[n, rows, :half] = (cos_u * cos_v - sin_u * sin_v).astype(jnp.bfloat16)
            table[n, rows, half:] = (-sin_u * cos_v - cos_u * sin_v).astype(jnp.bfloat16)


def send_kernel(
    strain, factors, listed, bands,
    swap, folds, kept_table,
    time, sent_table, factors_in, listed_in, bands_in, sems,
):
    me = lax.rem(lax.axis_index(AXIS), Q)
    core, side = lax.rem(me, 2), me // 2
    channels, samples = strain.shape
    quarter = samples // Q
    depth = quarter // 2
    small = [
        pltpu.make_async_copy(factors, factors_in, sems.at[2 * Q]),
        pltpu.make_async_copy(listed, listed_in, sems.at[2 * Q + 1]),
        pltpu.make_async_copy(bands, bands_in, sems.at[2 * Q + 2]),
    ]
    copies = []
    for h in range(2):
        for q in range(Q):
            part = (slice(None), pl.ds(q * quarter + h * depth, depth))
            copies.append(
                pltpu.make_async_copy(strain.at[part], time.at[part], sems.at[h * Q + q])
            )
    for copy in small + copies:
        copy.start()
    for copy in small:
        copy.wait()

    fill_table(factors_in.at[1 - core], sent_table)
    nbands = bands.shape[1]
    width = swap.shape[2] // nbands
    rounds = bands.shape[2]
    used = (listed_in[...] * bands_in[0]).astype(jnp.float32)
    pick = lax.broadcasted_iota(jnp.int32, (rounds, rounds), 0) == lax.broadcasted_iota(
        jnp.int32, (rounds, rounds), 1
    )
    weight = jnp.concatenate(
        [
            jnp.broadcast_to(
                jnp.sum(
                    jnp.where(pick, jnp.broadcast_to(used[j : j + 1], (rounds, rounds)), 0.0),
                    axis=1,
                    keepdims=True,
                ),
                (rounds, width),
            )
            for j in range(nbands)
        ],
        axis=1,
    ).astype(jnp.bfloat16)
    for n in range(2):
        swap[n, channels:, :] = weight
    fill_table(factors_in.at[core], kept_table)

    for h in range(2):
        for copy in copies[h * Q : (h + 1) * Q]:
            copy.wait()
        here = pl.ds(h * depth, depth)
        q0, q1, q2, q3 = (time[:, pl.ds(q * quarter + h * depth, depth)] for q in range(Q))
        folds[0, 0, :, here] = q0 - q2
        folds[0, 1, :, here] = q1 - q3
        even = q0.astype(jnp.float32) + q2.astype(jnp.float32)
        odd = q1.astype(jnp.float32) + q3.astype(jnp.float32)
        folds[1, 0, :, here] = (even - odd).astype(jnp.bfloat16)
        folds[1, 1, :, here] = (even + odd).astype(jnp.bfloat16)

    def store(values):
        for n, value in enumerate(values):
            swap[lax.bitwise_xor(side, n), :channels, :] = value.astype(jnp.bfloat16)

    @pl.when(core == 0)
    def _():
        store(real_classes(folds.at[1], sent_table))

    @pl.when(core == 1)
    def _():
        store(complex_classes(folds.at[0], sent_table))


def keep_kernel(swap, folds, table, near, mates):
    me = lax.rem(lax.axis_index(AXIS), Q)
    core, side = lax.rem(me, 2), me // 2
    channels = folds.shape[2]
    near[0, channels:, :] = swap[0, channels:, :]
    mates[channels:, :] = swap[0, channels:, :]

    def store(values):
        for n, value in enumerate(values):
            value = value.astype(jnp.bfloat16)

            @pl.when(side == n)
            def _():
                near[0, :channels, :] = value

            @pl.when(side != n)
            def _():
                mates[:channels, :] = value

    @pl.when(core == 0)
    def _():
        store(complex_classes(folds.at[0], table))

    @pl.when(core == 1)
    def _():
        store(real_classes(folds.at[1], table))


def send_call(strain, listed, bands):
    channels, samples = strain.shape
    factors = forward_factors(samples)
    rows, cols = channels + bands.shape[2], 2 * factors.shape[4]
    quarter = samples // Q
    return pl.pallas_call(
        send_kernel,
        in_specs=[HBM_SPEC] * 4,
        out_specs=[VMEM_SPEC] * 3,
        out_shape=[
            pltpu.VMEM((2, rows, cols), jnp.bfloat16),
            pltpu.VMEM((2, 2, channels, quarter), jnp.bfloat16),
            pltpu.VMEM((2, quarter, cols), jnp.bfloat16),
        ],
        scratch_shapes=[
            pltpu.VMEM((channels, samples), jnp.bfloat16),
            pltpu.VMEM((2, quarter, cols), jnp.bfloat16),
            pltpu.VMEM(factors.shape, jnp.float32),
            pltpu.VMEM(listed.shape, listed.dtype),
            pltpu.VMEM(bands.shape, bands.dtype),
            pltpu.SemaphoreType.DMA((2 * Q + 3,)),
        ],
        compiler_params=pltpu.CompilerParams(vmem_limit_bytes=LIMIT),
        name="spectrum_sent",
    )(in_hbm(strain), in_hbm(jnp.asarray(factors)), in_hbm(listed), in_hbm(bands))


def make_unit(me, rounds, i, j):
    target_plane, i = i
    source_plane, j = j
    p, q = lax.bitwise_xor(me, i), lax.bitwise_xor(me, j)
    d = (target_plane + source_plane) * Q + i - j
    target = 2 * Q * target_plane + p
    source = Q * source_plane + q
    row = d - 1 if target_plane + source_plane or i != j else rounds
    return target, source, d, target_plane * Q + i, target_plane * Q + p, row


def early_units(me, rounds):
    base = 2 * (me // 2)

    def unit(i, j):
        return make_unit(me, rounds, i, j)

    def own(i, j):
        return unit((0, i), (0, j))

    def low(i, e):
        return unit((0, i), (1, base + e))

    def mid(e, f):
        return unit((1, base + e), (1, base + f))

    twins, rest = [], []
    for d in range(Q):
        group = [own(i, i - d) for i in range(d, Q)]
        twins += [group[n : n + 2] for n in range(0, len(group) // 2 * 2, 2)]
        rest += group[len(group) // 2 * 2 :]
    twins += [[low(i, 0), low(i + 1, 1)] for i in range(Q - 1)]
    twins.append([mid(0, 0), mid(1, 1)])
    rest += [low(Q - 1, 0), low(0, 1), mid(0, 1)]
    return twins, rest


def late_units(me, rounds):
    base = 2 * (1 - me // 2)

    def mid(i, j):
        return make_unit(me, rounds, (1, i), (1, j))

    twins = [[mid(base, base), mid(base + 1, base + 1)]]
    twins.append([mid(0, 2), mid(1, 3)])
    twins.append([mid(1, 2), mid(base, base + 1)])
    return twins, [mid(0, 3)]


def mask_row(mask, target, row):
    return jnp.concatenate([mask[target, h, pl.ds(row, 1), :] for h in range(mask.shape[1])], axis=1)


def low_units(me, rounds):
    base = 2 * (1 - me // 2)
    return [
        make_unit(me, rounds, (0, i), (1, base + e)) for i in range(Q) for e in range(2)
    ]


def prepare_maps(units, mask, inv, lag_range, maps):
    for n, (_, _, d, _, target, row) in enumerate(units):
        weight = mask_row(mask, target, row).astype(jnp.bfloat16)
        maps[n] = dot(inv[...] * weight, lag_range[d]).astype(jnp.bfloat16)


def steered(units, spec, steering):
    channels = steering.shape[2]
    half = spec.shape[2] // 2
    beams = []
    for target, source, d, _, _, _ in units:
        near_re, near_im = spec[target, :channels, :half], spec[target, :channels, half:]
        far_re, far_im = spec[source, :channels, :half], spec[source, :channels, half:]
        real = near_re * far_re + near_im * far_im
        imag = near_im * far_re - near_re * far_im
        cross = jnp.concatenate([real, imag], axis=1)
        beams.append(dot(steering[d], cross).astype(jnp.bfloat16))
    return beams


def run_units(plan, spec, mask, steering, inv, lag_range, window, mapped=(), maps=None):
    angles = steering.shape[1]
    twins, rest = plan
    units = [unit for pair in twins for unit in pair] + rest
    beams = steered(units + list(mapped), spec, steering)
    mapped_beams = beams[len(units) :]
    beams = dot(jnp.concatenate(beams[: len(units)], axis=0), inv[...])
    masked = []
    for u, (_, _, _, _, target, row) in enumerate(units):
        weight = mask_row(mask, target, row)
        masked.append((beams[u * angles : (u + 1) * angles, :] * weight).astype(jnp.bfloat16))
    for u in range(0, 2 * len(twins), 2):
        part = dot(jnp.concatenate(masked[u : u + 2], axis=0), lag_range[units[u][2]])
        window[units[u][3]] += part[:angles]
        window[units[u + 1][3]] += part[angles:]
    for u in range(2 * len(twins), len(units)):
        window[units[u][3]] += dot(masked[u], lag_range[units[u][2]])
    for n in range(0, len(mapped), 2):
        both = jnp.concatenate(mapped_beams[n : n + 2], axis=1)
        window[mapped[n][3]] += dot(both, maps[n : n + 2].reshape(both.shape[1], -1))


def fill_mask(mask, entry, spec, slot, channels, nbands):
    rounds = mask.shape[2] // 2
    rows = spec[slot, channels:, :].astype(jnp.float32)
    cols = mask.shape[3]
    for j in range(nbands):
        h, lane = divmod(j * (mask.shape[1] * cols // nbands), cols)
        width = mask.shape[1] * cols // nbands
        mask[entry, h, :rounds, lane : lane + width] = jnp.broadcast_to(
            rows[:, j * (cols // nbands) : j * (cols // nbands) + 1], (rounds, width)
        )
    mask[entry, :, rounds:, :] = jnp.ones((mask.shape[1], rounds, cols), jnp.float32)


def neighbour_slots():
    parity = lax.rem(lax.axis_index(AXIS) // Q, 2)
    return Q * (2 - parity), Q * (1 + parity)


def early_kernel(
    nbands, near, mates, even, odd, inv_all, steering, lag_range,
    spec, window, inv, maps, mask, sem,
):
    me = lax.rem(lax.axis_index(AXIS), Q)
    copy = pltpu.make_async_copy(inv_all.at[me], inv, sem)
    copy.start()
    even_slot, odd_slot = neighbour_slots()
    spec[0:2] = near[...]
    spec[2:4] = mates[...]
    spec[pl.ds(even_slot, 2)] = even[...]
    spec[pl.ds(odd_slot, 2)] = odd[...]
    window[...] = jnp.zeros_like(window)
    channels = steering.shape[2]
    for p in range(Q):
        fill_mask(mask, p, spec, p, channels, nbands)
    for p in range(Q // 2):
        fill_mask(mask, Q + p, spec, 2 * Q + p, channels, nbands)
    copy.wait()
    plan = early_units(me, steering.shape[0] - 1)
    run_units(plan, spec, mask, steering, inv, lag_range, window)
    prepare_maps(low_units(me, steering.shape[0] - 1), mask, inv, lag_range, maps)


def late_kernel(
    nbands, spec_in, window_in, even, odd, inv, maps, steering, lag_range,
    keep, send, spec, window, mask,
):
    me = lax.rem(lax.axis_index(AXIS), Q)
    even_slot, odd_slot = neighbour_slots()
    spec[pl.ds(even_slot + 2, 2)] = even[...]
    spec[pl.ds(odd_slot + 2, 2)] = odd[...]
    channels = steering.shape[2]
    for p in range(Q):
        fill_mask(mask, p, spec, p, channels, nbands)
        fill_mask(mask, Q + p, spec, 2 * Q + p, channels, nbands)
    plan = late_units(me, steering.shape[0] - 1)
    mapped = low_units(me, steering.shape[0] - 1)
    run_units(plan, spec, mask, steering, inv, lag_range, window, mapped, maps)

    width = window.shape[2] // 3

    def segment(s):
        total = None
        for slot, part in ((s, 1), (s - 1, 2), (s + 1, 0)):
            if 0 <= slot < 2 * Q:
                value = window[slot, :, part * width : (part + 1) * width]
                total = value if total is None else total + value
        return total

    core = lax.rem(me, 2)
    here = [segment(s) for s in list(range(Q)) + [2 * Q, -1]]
    there = [segment(Q + p) for p in range(Q)]

    @pl.when(core == 0)
    def _():
        for n, value in enumerate(there):
            keep[n] = value
        for n in range(Q, Q + 2):
            keep[n] = jnp.zeros_like(there[0])
        for n, value in enumerate(here):
            send[n] = value.astype(jnp.bfloat16)

    @pl.when(core == 1)
    def _():
        for n, value in enumerate(here):
            keep[n] = value
        for n, value in enumerate(there):
            send[n] = value.astype(jnp.bfloat16)
        for n in range(Q, Q + 2):
            send[n] = jnp.zeros_like(there[0]).astype(jnp.bfloat16)


def join_kernel(swap, near_in, near, other):
    near[1] = swap[0]
    other[...] = swap[1]


def stack_kernel(first, second, both):
    both[0] = first[...]
    both[1] = second[...]


def core_sum_kernel(kept, received, mine, send):
    side = lax.rem(lax.axis_index(AXIS), Q) // 2

    def total(n):
        return kept[n] + received[n].astype(jnp.float32)

    for n in range(2):
        mine[n] = total(2 * side + n)
        send[n] = total(2 * (1 - side) + n).astype(jnp.bfloat16)
    mine[2] = total(Q + side)
    send[2] = total(Q + 1 - side).astype(jnp.bfloat16)


def plane_sum_kernel(kept, received, mine, send):
    core = lax.rem(lax.axis_index(AXIS), 2)
    totals = [kept[n] + received[n].astype(jnp.float32) for n in range(3)]
    mine[0] = totals[0]
    mine[1] = totals[1]

    @pl.when(core == 0)
    def _():
        send[0] = totals[0].astype(jnp.bfloat16)
        send[1] = totals[1].astype(jnp.bfloat16)

    @pl.when(core == 1)
    def _():
        send[0] = totals[2].astype(jnp.bfloat16)
        send[1] = jnp.zeros_like(totals[2]).astype(jnp.bfloat16)


def end_sum_kernel(kept, received, mine, send):
    me = lax.rem(lax.axis_index(AXIS), Q)
    first = received[0].astype(jnp.float32)
    second = received[1].astype(jnp.float32)
    core, side = lax.rem(me, 2), me // 2

    @pl.when(core == 0)
    def _():
        mine[...] = first
        send[...] = second

    @pl.when((core == 1) & (side == 0))
    def _():
        mine[...] = kept[1]
        send[...] = kept[0] + first

    @pl.when((core == 1) & (side == 1))
    def _():
        mine[...] = kept[1] + first
        send[...] = kept[0]


def image_kernel(kept, received, image):
    image[...] = kept[...] + received[...]


def near_vmem(*values):
    return [pltpu.with_memory_space_constraint(value, pltpu.VMEM) for value in values]


def local_call(kernel, name, outs, *values, aliases={}):
    return pl.pallas_call(
        kernel,
        in_specs=[VMEM_SPEC] * len(values),
        out_specs=[VMEM_SPEC] * len(outs),
        out_shape=outs,
        input_output_aliases=aliases,
        compiler_params=pltpu.CompilerParams(vmem_limit_bytes=LIMIT),
        name=name,
    )(*near_vmem(*values))


def early_call(nbands, near, mates, even, odd, inv, steering, lag_range):
    _, rows, cols = near.shape
    angles, group = steering.shape[1], lag_range.shape[2]
    rounds = steering.shape[0] - 1
    return pl.pallas_call(
        functools.partial(early_kernel, nbands),
        in_specs=[VMEM_SPEC] * 4 + [HBM_SPEC] + [VMEM_SPEC] * 2,
        out_specs=[VMEM_SPEC] * 4,
        out_shape=[
            pltpu.VMEM((3 * Q, rows, cols), jnp.bfloat16),
            pltpu.VMEM((2 * Q, angles, group), jnp.float32),
            pltpu.VMEM(inv.shape[1:], inv.dtype),
            pltpu.VMEM((2 * Q, cols, group), jnp.bfloat16),
        ],
        scratch_shapes=[
            pltpu.VMEM((2 * Q, L // cols, 2 * rounds, cols), jnp.float32),
            pltpu.SemaphoreType.DMA(()),
        ],
        compiler_params=pltpu.CompilerParams(vmem_limit_bytes=LIMIT),
        name="early_pairs",
    )(*near_vmem(near, mates, even, odd), in_hbm(inv), *near_vmem(steering, lag_range))


def late_call(nbands, spec, window, even, odd, inv, maps, steering, lag_range):
    cols = spec.shape[2]
    angles, group = steering.shape[1], lag_range.shape[2]
    rounds = steering.shape[0] - 1
    pieces = (Q + 2, angles, group // 3)
    return pl.pallas_call(
        functools.partial(late_kernel, nbands),
        in_specs=[VMEM_SPEC] * 8,
        out_specs=[VMEM_SPEC] * 4,
        out_shape=[
            pltpu.VMEM(pieces, jnp.float32),
            pltpu.VMEM(pieces, jnp.bfloat16),
            pltpu.VMEM(spec.shape, spec.dtype),
            pltpu.VMEM(window.shape, window.dtype),
        ],
        input_output_aliases={0: 2, 1: 3},
        scratch_shapes=[pltpu.VMEM((2 * Q, L // cols, 2 * rounds, cols), jnp.float32)],
        compiler_params=pltpu.CompilerParams(vmem_limit_bytes=LIMIT),
        name="late_pairs",
    )(*near_vmem(spec, window, even, odd, inv, maps, steering, lag_range))[:2]


def exchange(value, devices, target):
    pairs = [(i, target(i)) for i in range(devices) if target(i) is not None]
    pairs = [(i, j) for i, j in pairs if 0 <= j < devices]
    return lax.ppermute(value, AXIS, pairs)


def per_device(devices, strain, steering, lag_range, pair_listed, band_used):
    def planes(value, parity):
        return exchange(value, devices, lambda i: i + (Q if i // Q % 2 == parity else -Q))

    def flip(value, by):
        return exchange(value, devices, lambda i: i ^ by)

    swap, folds, table = send_call(strain, pair_listed, jnp.transpose(band_used, (0, 2, 1)))
    joined = pltpu.VMEM(swap.shape, swap.dtype)
    single = pltpu.VMEM(swap.shape[1:], swap.dtype)
    near, mate = local_call(keep_kernel, "spectrum_kept", [joined, single], swap, folds, table)
    mate = flip(mate, 2)
    near, other = local_call(
        join_kernel, "join", [joined, single], flip(swap, 1), near, aliases={1: 0}
    )
    other = flip(other, 2)
    mates = local_call(stack_kernel, "stack", [joined], mate, other)[0]
    near_odd, near_even = planes(near, 1), planes(near, 0)
    far_odd, far_even = planes(mates, 1), planes(mates, 0)
    nbands = band_used.shape[2]
    inv = jnp.asarray(inverse_table(strain.shape[1]))
    spec, window, inv, maps = early_call(
        nbands, near, mates, near_even, near_odd, inv, steering, lag_range
    )
    kept, send = late_call(
        nbands, spec, window, far_even, far_odd, inv, maps, steering, lag_range
    )

    def pieces(count, dtype):
        return pltpu.VMEM(((count,) if count else ()) + kept.shape[1:], dtype)

    def ends(i):
        if i % 2 == 0:
            return i + Q
        return i + 2 * Q if i % Q < 2 else i - Q

    kept, send = local_call(
        core_sum_kernel,
        "core_sum",
        [pieces(3, jnp.float32), pieces(3, jnp.bfloat16)],
        kept,
        flip(send, 1),
    )
    kept, send = local_call(
        plane_sum_kernel,
        "plane_sum",
        [pieces(2, jnp.float32), pieces(2, jnp.bfloat16)],
        kept,
        flip(send, 2),
    )
    kept, send = local_call(
        end_sum_kernel,
        "end_sum",
        [pieces(0, jnp.float32), pieces(0, jnp.float32)],
        kept,
        exchange(send, devices, ends),
    )
    return local_call(
        image_kernel,
        "image",
        [jax.ShapeDtypeStruct(kept.shape, jnp.float32)],
        kept,
        flip(send, 1),
    )[0]


def solution(mesh):
    return jax.shard_map(
        functools.partial(per_device, mesh.shape[AXIS]),
        mesh=mesh,
        in_specs=(
            P(("win", AXIS), None),
            P(),
            P(),
            P(("win", AXIS), None),
            P(("win", AXIS), None, None),
        ),
        out_specs=P(None, ("win", AXIS)),
        check_vma=False,
    )
```

```python
import functools

import jax
import jax.numpy as jnp
import numpy as np
from jax import lax
from jax.experimental import pallas as pl
from jax.experimental.pallas import tpu as pltpu
from jax.sharding import PartitionSpec as P

AXIS = "fib"
F = 512
L = 512
Q = 4
LIMIT = 16 << 20
VMEM_SPEC = pl.BlockSpec(memory_space=pltpu.VMEM)
HBM_SPEC = pl.BlockSpec(memory_space=pl.ANY)


STEP = 32


def forward_factors(samples):
    m = np.arange(F // Q, dtype=np.int64)
    k = (Q * m[None, :] + np.arange(Q)[:, None] + 1)[:, None, :]
    scale = samples ** (-0.5)
    parts = []
    for step, factor in ((STEP, scale), (1, 1.0)):
        count = samples // Q // STEP if step == STEP else STEP
        t = step * np.arange(count, dtype=np.int64)[None, :, None]
        phase = (t * k % samples) * (2.0 * np.pi / samples)
        parts += [np.cos(phase) * factor, np.sin(phase) * factor]
    table = np.stack(parts)
    return np.stack([table[:, 0::2], table[:, 1::2]]).astype(np.float32)


def inverse_table(samples):
    freqs = F // Q
    k = Q * np.arange(freqs, dtype=np.int64)[None, :, None] + np.arange(Q)[:, None, None] + 1
    lag = np.arange(L, dtype=np.int64)[None, None, :] - L // 2
    theta = (k * lag % samples) * (2.0 * np.pi / samples)
    table = np.concatenate([np.cos(theta), -np.sin(theta)], axis=1) * (2 * F) ** (-0.5)
    return table.astype(jnp.bfloat16)


def in_hbm(value):
    return pltpu.with_memory_space_constraint(value, pltpu.HBM)


def dot(a, b):
    return jnp.dot(a, b, preferred_element_type=jnp.float32)


def combine(a, b):
    half = a.shape[1] // 2
    return jnp.concatenate([a[:, :half] + b[:, half:], a[:, half:] - b[:, :half]], axis=1)


def complex_classes(folds, table):
    channels = folds.shape[1]
    both = folds[...].reshape(2 * channels, folds.shape[2])
    values = []
    for n, sign in ((0, 1.0), (1, -1.0)):
        product = dot(both, table[n])
        values.append(combine(product[:channels], product[channels:] * sign))
    return values


def real_classes(folds, table):
    return [dot(folds[n], table[n]) for n in range(2)]


def fill_table(factors, table):
    half = table.shape[2] // 2
    for n in range(2):
        cos_v, sin_v = factors[2, n], factors[3, n]
        for u in range(factors.shape[2]):
            cos_u, sin_u = factors[0, n, u : u + 1, :], factors[1, n, u : u + 1, :]
            rows = slice(u * STEP, (u + 1) * STEP)
            table[n, rows, :half] = (cos_u * cos_v - sin_u * sin_v).astype(jnp.bfloat16)
            table[n, rows, half:] = (-sin_u * cos_v - cos_u * sin_v).astype(jnp.bfloat16)


def send_kernel(
    strain, factors, listed, bands,
    swap, folds, kept_table,
    time, sent_table, factors_in, listed_in, bands_in, sems,
):
    me = lax.rem(lax.axis_index(AXIS), Q)
    core, side = lax.rem(me, 2), me // 2
    channels, samples = strain.shape
    quarter = samples // Q
    depth = quarter // 2
    small = [
        pltpu.make_async_copy(factors, factors_in, sems.at[2 * Q]),
        pltpu.make_async_copy(listed, listed_in, sems.at[2 * Q + 1]),
        pltpu.make_async_copy(bands, bands_in, sems.at[2 * Q + 2]),
    ]
    copies = []
    for h in range(2):
        for q in range(Q):
            part = (slice(None), pl.ds(q * quarter + h * depth, depth))
            copies.append(
                pltpu.make_async_copy(strain.at[part], time.at[part], sems.at[h * Q + q])
            )
    for copy in small + copies:
        copy.start()
    for copy in small:
        copy.wait()

    fill_table(factors_in.at[1 - core], sent_table)
    nbands = bands.shape[1]
    width = swap.shape[2] // nbands
    rounds = bands.shape[2]
    used = (listed_in[...] * bands_in[0]).astype(jnp.float32)
    pick = lax.broadcasted_iota(jnp.int32, (rounds, rounds), 0) == lax.broadcasted_iota(
        jnp.int32, (rounds, rounds), 1
    )
    weight = jnp.concatenate(
        [
            jnp.broadcast_to(
                jnp.sum(
                    jnp.where(pick, jnp.broadcast_to(used[j : j + 1], (rounds, rounds)), 0.0),
                    axis=1,
                    keepdims=True,
                ),
                (rounds, width),
            )
            for j in range(nbands)
        ],
        axis=1,
    ).astype(jnp.bfloat16)
    for n in range(2):
        swap[n, channels:, :] = weight
    fill_table(factors_in.at[core], kept_table)

    for h in range(2):
        for copy in copies[h * Q : (h + 1) * Q]:
            copy.wait()
        here = pl.ds(h * depth, depth)
        q0, q1, q2, q3 = (time[:, pl.ds(q * quarter + h * depth, depth)] for q in range(Q))
        folds[0, 0, :, here] = q0 - q2
        folds[0, 1, :, here] = q1 - q3
        even = q0.astype(jnp.float32) + q2.astype(jnp.float32)
        odd = q1.astype(jnp.float32) + q3.astype(jnp.float32)
        folds[1, 0, :, here] = (even - odd).astype(jnp.bfloat16)
        folds[1, 1, :, here] = (even + odd).astype(jnp.bfloat16)

    def store(values):
        for n, value in enumerate(values):
            swap[lax.bitwise_xor(side, n), :channels, :] = value.astype(jnp.bfloat16)

    @pl.when(core == 0)
    def _():
        store(real_classes(folds.at[1], sent_table))

    @pl.when(core == 1)
    def _():
        store(complex_classes(folds.at[0], sent_table))


def keep_kernel(swap, folds, table, near, mates):
    me = lax.rem(lax.axis_index(AXIS), Q)
    core, side = lax.rem(me, 2), me // 2
    channels = folds.shape[2]
    near[0, channels:, :] = swap[0, channels:, :]
    mates[channels:, :] = swap[0, channels:, :]

    def store(values):
        for n, value in enumerate(values):
            value = value.astype(jnp.bfloat16)

            @pl.when(side == n)
            def _():
                near[0, :channels, :] = value

            @pl.when(side != n)
            def _():
                mates[:channels, :] = value

    @pl.when(core == 0)
    def _():
        store(complex_classes(folds.at[0], table))

    @pl.when(core == 1)
    def _():
        store(real_classes(folds.at[1], table))


def send_call(strain, listed, bands):
    channels, samples = strain.shape
    factors = forward_factors(samples)
    rows, cols = channels + bands.shape[2], 2 * factors.shape[4]
    quarter = samples // Q
    return pl.pallas_call(
        send_kernel,
        in_specs=[HBM_SPEC] * 4,
        out_specs=[VMEM_SPEC] * 3,
        out_shape=[
            pltpu.VMEM((2, rows, cols), jnp.bfloat16),
            pltpu.VMEM((2, 2, channels, quarter), jnp.bfloat16),
            pltpu.VMEM((2, quarter, cols), jnp.bfloat16),
        ],
        scratch_shapes=[
            pltpu.VMEM((channels, samples), jnp.bfloat16),
            pltpu.VMEM((2, quarter, cols), jnp.bfloat16),
            pltpu.VMEM(factors.shape, jnp.float32),
            pltpu.VMEM(listed.shape, listed.dtype),
            pltpu.VMEM(bands.shape, bands.dtype),
            pltpu.SemaphoreType.DMA((2 * Q + 3,)),
        ],
        compiler_params=pltpu.CompilerParams(vmem_limit_bytes=LIMIT),
        name="spectrum_sent",
    )(in_hbm(strain), in_hbm(jnp.asarray(factors)), in_hbm(listed), in_hbm(bands))


def make_unit(me, rounds, i, j):
    target_plane, i = i
    source_plane, j = j
    p, q = lax.bitwise_xor(me, i), lax.bitwise_xor(me, j)
    d = (target_plane + source_plane) * Q + i - j
    target = 2 * Q * target_plane + p
    source = Q * source_plane + q
    row = d - 1 if target_plane + source_plane or i != j else rounds
    return target, source, d, target_plane * Q + i, target_plane * Q + p, row


def early_units(me, rounds):
    base = 2 * (me // 2)

    def unit(i, j):
        return make_unit(me, rounds, i, j)

    def own(i, j):
        return unit((0, i), (0, j))

    def low(i, e):
        return unit((0, i), (1, base + e))

    def mid(e, f):
        return unit((1, base + e), (1, base + f))

    twins, rest = [], []
    for d in range(Q):
        group = [own(i, i - d) for i in range(d, Q)]
        twins += [group[n : n + 2] for n in range(0, len(group) // 2 * 2, 2)]
        rest += group[len(group) // 2 * 2 :]
    twins += [[low(i, 0), low(i + 1, 1)] for i in range(Q - 1)]
    twins.append([mid(0, 0), mid(1, 1)])
    rest += [low(Q - 1, 0), low(0, 1), mid(0, 1)]
    return twins, rest


def late_units(me, rounds):
    base = 2 * (1 - me // 2)

    def mid(i, j):
        return make_unit(me, rounds, (1, i), (1, j))

    twins = [[mid(base, base), mid(base + 1, base + 1)]]
    twins.append([mid(0, 2), mid(1, 3)])
    twins.append([mid(1, 2), mid(base, base + 1)])
    return twins, [mid(0, 3)]


def mask_row(mask, target, row):
    return jnp.concatenate([mask[target, h, pl.ds(row, 1), :] for h in range(mask.shape[1])], axis=1)


def low_units(me, rounds):
    base = 2 * (1 - me // 2)
    return [
        make_unit(me, rounds, (0, i), (1, base + e)) for i in range(Q) for e in range(2)
    ]


def prepare_maps(units, mask, inv, lag_range, maps):
    for n, (_, _, d, _, target, row) in enumerate(units):
        weight = mask_row(mask, target, row).astype(jnp.bfloat16)
        maps[n] = dot(inv[...] * weight, lag_range[d]).astype(jnp.bfloat16)


def steered(units, spec, steering):
    channels = steering.shape[2]
    half = spec.shape[2] // 2
    beams = []
    for target, source, d, _, _, _ in units:
        near_re, near_im = spec[target, :channels, :half], spec[target, :channels, half:]
        far_re, far_im = spec[source, :channels, :half], spec[source, :channels, half:]
        real = near_re * far_re + near_im * far_im
        imag = near_im * far_re - near_re * far_im
        cross = jnp.concatenate([real, imag], axis=1)
        beams.append(dot(steering[d], cross).astype(jnp.bfloat16))
    return beams


def run_units(plan, spec, mask, steering, inv, lag_range, window, mapped=(), maps=None):
    angles = steering.shape[1]
    twins, rest = plan
    units = [unit for pair in twins for unit in pair] + rest
    beams = steered(units + list(mapped), spec, steering)
    mapped_beams = beams[len(units) :]
    beams = dot(jnp.concatenate(beams[: len(units)], axis=0), inv[...])
    masked = []
    for u, (_, _, _, _, target, row) in enumerate(units):
        weight = mask_row(mask, target, row)
        masked.append((beams[u * angles : (u + 1) * angles, :] * weight).astype(jnp.bfloat16))
    for u in range(0, 2 * len(twins), 2):
        part = dot(jnp.concatenate(masked[u : u + 2], axis=0), lag_range[units[u][2]])
        window[units[u][3]] += part[:angles]
        window[units[u + 1][3]] += part[angles:]
    for u in range(2 * len(twins), len(units)):
        window[units[u][3]] += dot(masked[u], lag_range[units[u][2]])
    for n in range(0, len(mapped), 2):
        both = jnp.concatenate(mapped_beams[n : n + 2], axis=1)
        window[mapped[n][3]] += dot(both, maps[n : n + 2].reshape(both.shape[1], -1))


def fill_mask(mask, entry, spec, slot, channels, nbands):
    rounds = mask.shape[2] // 2
    rows = spec[slot, channels:, :].astype(jnp.float32)
    cols = mask.shape[3]
    for j in range(nbands):
        h, lane = divmod(j * (mask.shape[1] * cols // nbands), cols)
        width = mask.shape[1] * cols // nbands
        mask[entry, h, :rounds, lane : lane + width] = jnp.broadcast_to(
            rows[:, j * (cols // nbands) : j * (cols // nbands) + 1], (rounds, width)
        )
    mask[entry, :, rounds:, :] = jnp.ones((mask.shape[1], rounds, cols), jnp.float32)


def neighbour_slots():
    parity = lax.rem(lax.axis_index(AXIS) // Q, 2)
    return Q * (2 - parity), Q * (1 + parity)


def early_kernel(
    nbands, near, mates, even, odd, inv_all, steering, lag_range,
    spec, window, inv, maps, mask, sem,
):
    me = lax.rem(lax.axis_index(AXIS), Q)
    copy = pltpu.make_async_copy(inv_all.at[me], inv, sem)
    copy.start()
    even_slot, odd_slot = neighbour_slots()
    spec[0:2] = near[...]
    spec[2:4] = mates[...]
    spec[pl.ds(even_slot, 2)] = even[...]
    spec[pl.ds(odd_slot, 2)] = odd[...]
    window[...] = jnp.zeros_like(window)
    channels = steering.shape[2]
    for p in range(Q):
        fill_mask(mask, p, spec, p, channels, nbands)
    for p in range(Q // 2):
        fill_mask(mask, Q + p, spec, 2 * Q + p, channels, nbands)
    copy.wait()
    plan = early_units(me, steering.shape[0] - 1)
    run_units(plan, spec, mask, steering, inv, lag_range, window)
    prepare_maps(low_units(me, steering.shape[0] - 1), mask, inv, lag_range, maps)


def late_kernel(
    nbands, spec_in, window_in, even, odd, inv, maps, steering, lag_range,
    keep, send, spec, window, mask,
):
    me = lax.rem(lax.axis_index(AXIS), Q)
    even_slot, odd_slot = neighbour_slots()
    spec[pl.ds(even_slot + 2, 2)] = even[...]
    spec[pl.ds(odd_slot + 2, 2)] = odd[...]
    channels = steering.shape[2]
    for p in range(Q):
        fill_mask(mask, p, spec, p, channels, nbands)
        fill_mask(mask, Q + p, spec, 2 * Q + p, channels, nbands)
    plan = late_units(me, steering.shape[0] - 1)
    mapped = low_units(me, steering.shape[0] - 1)
    run_units(plan, spec, mask, steering, inv, lag_range, window, mapped, maps)

    width = window.shape[2] // 3

    def segment(s):
        total = None
        for slot, part in ((s, 1), (s - 1, 2), (s + 1, 0)):
            if 0 <= slot < 2 * Q:
                value = window[slot, :, part * width : (part + 1) * width]
                total = value if total is None else total + value
        return total

    core = lax.rem(me, 2)
    here = [segment(s) for s in list(range(Q)) + [2 * Q, -1]]
    there = [segment(Q + p) for p in range(Q)]

    @pl.when(core == 0)
    def _():
        for n, value in enumerate(there):
            keep[n] = value
        for n in range(Q, Q + 2):
            keep[n] = jnp.zeros_like(there[0])
        for n, value in enumerate(here):
            send[n] = value.astype(jnp.bfloat16)

    @pl.when(core == 1)
    def _():
        for n, value in enumerate(here):
            keep[n] = value
        for n, value in enumerate(there):
            send[n] = value.astype(jnp.bfloat16)
        for n in range(Q, Q + 2):
            send[n] = jnp.zeros_like(there[0]).astype(jnp.bfloat16)


def join_kernel(swap, near_in, near, other):
    near[1] = swap[0]
    other[...] = swap[1]


def stack_kernel(first, second, both):
    both[0] = first[...]
    both[1] = second[...]


def core_sum_kernel(kept, received, mine, send, later):
    me = lax.rem(lax.axis_index(AXIS), Q)
    core, side = lax.rem(me, 2), me // 2

    def total(n):
        return kept[n] + received[n].astype(jnp.float32)

    for n in range(2):
        mine[n] = total(2 * side + n)
        later[n] = total(2 * (1 - side) + n).astype(jnp.bfloat16)
    mine[2] = total(Q + side)

    @pl.when(core == 0)
    def _():
        send[...] = later[...]

    @pl.when(core == 1)
    def _():
        send[0] = total(Q + 1 - side).astype(jnp.bfloat16)
        send[1] = jnp.zeros_like(send[0])


def plane_sum_kernel(kept, received, send):
    core = lax.rem(lax.axis_index(AXIS), 2)

    @pl.when(core == 0)
    def _():
        for n in range(2):
            send[n] = (kept[n] + received[n].astype(jnp.float32)).astype(jnp.bfloat16)

    @pl.when(core == 1)
    def _():
        send[0] = (kept[2] + received[0].astype(jnp.float32)).astype(jnp.bfloat16)
        send[1] = jnp.zeros_like(send[0])


def end_sum_kernel(kept, later, received, mine, send):
    me = lax.rem(lax.axis_index(AXIS), Q)
    first = received[0].astype(jnp.float32)
    second = received[1].astype(jnp.float32)
    core, side = lax.rem(me, 2), me // 2
    own = [kept[n] + later[n].astype(jnp.float32) for n in range(2)]

    @pl.when(core == 0)
    def _():
        mine[...] = first
        send[...] = second

    @pl.when((core == 1) & (side == 0))
    def _():
        mine[...] = own[1]
        send[...] = own[0] + first

    @pl.when((core == 1) & (side == 1))
    def _():
        mine[...] = own[1] + first
        send[...] = own[0]


def image_kernel(kept, received, image):
    image[...] = kept[...] + received[...]


def near_vmem(*values):
    return [pltpu.with_memory_space_constraint(value, pltpu.VMEM) for value in values]


def local_call(kernel, name, outs, *values, aliases={}):
    return pl.pallas_call(
        kernel,
        in_specs=[VMEM_SPEC] * len(values),
        out_specs=[VMEM_SPEC] * len(outs),
        out_shape=outs,
        input_output_aliases=aliases,
        compiler_params=pltpu.CompilerParams(vmem_limit_bytes=LIMIT),
        name=name,
    )(*near_vmem(*values))


def early_call(nbands, near, mates, even, odd, inv, steering, lag_range):
    _, rows, cols = near.shape
    angles, group = steering.shape[1], lag_range.shape[2]
    rounds = steering.shape[0] - 1
    return pl.pallas_call(
        functools.partial(early_kernel, nbands),
        in_specs=[VMEM_SPEC] * 4 + [HBM_SPEC] + [VMEM_SPEC] * 2,
        out_specs=[VMEM_SPEC] * 4,
        out_shape=[
            pltpu.VMEM((3 * Q, rows, cols), jnp.bfloat16),
            pltpu.VMEM((2 * Q, angles, group), jnp.float32),
            pltpu.VMEM(inv.shape[1:], inv.dtype),
            pltpu.VMEM((2 * Q, cols, group), jnp.bfloat16),
        ],
        scratch_shapes=[
            pltpu.VMEM((2 * Q, L // cols, 2 * rounds, cols), jnp.float32),
            pltpu.SemaphoreType.DMA(()),
        ],
        compiler_params=pltpu.CompilerParams(vmem_limit_bytes=LIMIT),
        name="early_pairs",
    )(*near_vmem(near, mates, even, odd), in_hbm(inv), *near_vmem(steering, lag_range))


def late_call(nbands, spec, window, even, odd, inv, maps, steering, lag_range):
    cols = spec.shape[2]
    angles, group = steering.shape[1], lag_range.shape[2]
    rounds = steering.shape[0] - 1
    pieces = (Q + 2, angles, group // 3)
    return pl.pallas_call(
        functools.partial(late_kernel, nbands),
        in_specs=[VMEM_SPEC] * 8,
        out_specs=[VMEM_SPEC] * 4,
        out_shape=[
            pltpu.VMEM(pieces, jnp.float32),
            pltpu.VMEM(pieces, jnp.bfloat16),
            pltpu.VMEM(spec.shape, spec.dtype),
            pltpu.VMEM(window.shape, window.dtype),
        ],
        input_output_aliases={0: 2, 1: 3},
        scratch_shapes=[pltpu.VMEM((2 * Q, L // cols, 2 * rounds, cols), jnp.float32)],
        compiler_params=pltpu.CompilerParams(vmem_limit_bytes=LIMIT),
        name="late_pairs",
    )(*near_vmem(spec, window, even, odd, inv, maps, steering, lag_range))[:2]


def exchange(value, devices, target):
    pairs = [(i, target(i)) for i in range(devices) if target(i) is not None]
    pairs = [(i, j) for i, j in pairs if 0 <= j < devices]
    return lax.ppermute(value, AXIS, pairs)


def per_device(devices, strain, steering, lag_range, pair_listed, band_used):
    def planes(value, parity):
        return exchange(value, devices, lambda i: i + (Q if i // Q % 2 == parity else -Q))

    def flip(value, by):
        return exchange(value, devices, lambda i: i ^ by)

    swap, folds, table = send_call(strain, pair_listed, jnp.transpose(band_used, (0, 2, 1)))
    joined = pltpu.VMEM(swap.shape, swap.dtype)
    single = pltpu.VMEM(swap.shape[1:], swap.dtype)
    near, mate = local_call(keep_kernel, "spectrum_kept", [joined, single], swap, folds, table)
    mate = flip(mate, 2)
    near, other = local_call(
        join_kernel, "join", [joined, single], flip(swap, 1), near, aliases={1: 0}
    )
    other = flip(other, 2)
    mates = local_call(stack_kernel, "stack", [joined], mate, other)[0]
    near_odd, near_even = planes(near, 1), planes(near, 0)
    far_odd, far_even = planes(mates, 1), planes(mates, 0)
    nbands = band_used.shape[2]
    inv = jnp.asarray(inverse_table(strain.shape[1]))
    spec, window, inv, maps = early_call(
        nbands, near, mates, near_even, near_odd, inv, steering, lag_range
    )
    kept, send = late_call(
        nbands, spec, window, far_even, far_odd, inv, maps, steering, lag_range
    )

    def pieces(count, dtype):
        return pltpu.VMEM(((count,) if count else ()) + kept.shape[1:], dtype)

    def ends(i):
        if i % 2 == 0:
            return i + Q
        return i + 2 * Q if i % Q < 2 else i - Q

    kept, send, later = local_call(
        core_sum_kernel,
        "core_sum",
        [pieces(3, jnp.float32), pieces(2, jnp.bfloat16), pieces(2, jnp.bfloat16)],
        kept,
        flip(send, 1),
    )
    received = flip(send, 2)
    later = exchange(later, devices, lambda i: i ^ 2 if i % 2 else None)
    send = local_call(
        plane_sum_kernel, "plane_sum", [pieces(2, jnp.bfloat16)], kept, received
    )[0]
    kept, send = local_call(
        end_sum_kernel,
        "end_sum",
        [pieces(0, jnp.float32), pieces(0, jnp.float32)],
        kept,
        later,
        exchange(send, devices, ends),
    )
    return local_call(
        image_kernel,
        "image",
        [jax.ShapeDtypeStruct(kept.shape, jnp.float32)],
        kept,
        flip(send, 1),
    )[0]


def solution(mesh):
    return jax.shard_map(
        functools.partial(per_device, mesh.shape[AXIS]),
        mesh=mesh,
        in_specs=(
            P(("win", AXIS), None),
            P(),
            P(),
            P(("win", AXIS), None),
            P(("win", AXIS), None, None),
        ),
        out_specs=P(None, ("win", AXIS)),
        check_vma=False,
    )
```
